32 devices in a mesh: grp: 2 (over x), chol: 16 (over z, y, core).
Axes of the slice: x: 2, y: 2, z: 4, core: 2. Of those that a mesh axis runs over, the one named last changes fastest.
Arguments:
- chol_full: bfloat16 [128, 1024, 1024], P(None, 'chol'), may hold values from -0.015625 to 0.015625
- chol_half: bfloat16 [128, 1024, 256], P(None, 'chol'), may hold values from -0.046875 to 0.046875
- green: bfloat16 [128, 1024, 256], P('grp', 'chol'), parts along dimension 0, may hold values from -6 to 6
- gauss: float32 [128, 128], P('grp'), parts along dimension 0, may hold values from -5 to 5
- orbitals: bfloat16 [128, 1024, 256], P(('grp', 'chol')), parts along dimension 0, may hold values from -6 to 6
Outputs:
- new_orbitals: bfloat16 [128, 1024, 256], P(('grp', 'chol')), parts along dimension 0
- log_factor: float32 [128], P(('grp', 'chol')), parts along dimension 0
The draws below stay inside these ranges and needn't reach their ends.
There are 2 independent parts, one for each index of `grp`. The reference program is written for one: setup_inputs(seed, part) draws one part's arguments, and reference() takes and returns one part's arrays. A program takes and returns all parts, laid end to end along the dimension named above; an argument that names none is the same for every part. Nothing has to cross between parts.
All inputs are finite; a program needn't handle non-finite values.
Results may differ from the reference program's by a relative error of at most 0.0032.
Values may be sent and summed in bfloat16 or wider, within the bound.
A program may use at most 128 MiB of HBM per device.

```python
import jax
import jax.numpy as jnp
from jax import lax

N = 1024
NOCC = 256
NCH = 128
WALKERS = 64


def raised(drawn, own_key, source, target, parts, factor):
    def block_of(dim):
        return (jnp.arange(drawn.shape[dim]) // (drawn.shape[dim] // parts)).reshape((-1,) + (1,) * (drawn.ndim - 1 - dim))

    one_side = jax.random.permutation(own_key, parts)[block_of(target)]
    other_side = (block_of(target) + parts // 2) % parts
    return jnp.where((block_of(source) == one_side) | (block_of(source) == other_side), factor * drawn, drawn)


def block_scale(rng, dims, shards, smallest, high):
    loudness = 1.0
    for position, blocks in shards:
        steps = jax.random.uniform(jax.random.fold_in(jax.random.fold_in(rng, 6), position), (blocks,), jnp.float32, smallest / len(shards), high / len(shards))
        loudness = loudness * jnp.repeat(jnp.exp(steps), dims[position] // blocks).reshape((-1,) + (1,) * (len(dims) - 1 - position))
    return loudness


def bell_draw(own_key, dims, spread, limit, cuts=(), dtype=jnp.bfloat16):
    entries = spread * jax.random.normal(own_key, dims, jnp.float32)
    if cuts:
        entries = entries * block_scale(own_key, dims, cuts, -0.22, 0.18)
    return jnp.clip(entries, -limit, limit).astype(dtype)


def noise_with(key, dims, deviation, most, shards, heavy, kind=jnp.bfloat16):
    array = deviation * jax.random.normal(key, dims, jnp.float32)
    if shards:
        array = array * block_scale(key, dims, shards, -0.22, 0.18)
    return jnp.clip(raised(array, jax.random.fold_in(key, 3), *heavy), -most, most).astype(kind)


def setup_inputs(seed: int = 0, part: int = 0) -> dict:
    splits = jax.random.split(jax.random.key(seed), 6)
    part_splits = jax.random.split(jax.random.fold_in(splits[5], part), 6)
    return {
        "chol_full": bell_draw(splits[0], (NCH, N, N), (N * NCH) ** -0.5, 0.015625, ((1, 16),)),
        "chol_half": bell_draw(splits[1], (NCH, N, NOCC), (N * NOCC // 16) ** -0.5, 0.046875, ((1, 16),)),
        "green": noise_with(part_splits[2], (WALKERS, N, NOCC), 1.0, 6.0, ((1, 16),), (1, 0, 16, 2.0)),
        "gauss": bell_draw(part_splits[3], (WALKERS, NCH), 1.0, 5.0, (), jnp.float32),
        "orbitals": bell_draw(part_splits[4], (WALKERS, N, NOCC), 1.0, 6.0, ((0, 16),)),
    }


def reference(chol_full, chol_half, green, gauss, orbitals):
    walkers = green.shape[0]
    vbias = jnp.dot(green.reshape(walkers, -1), chol_half.reshape(NCH, -1).T, preferred_element_type=jnp.float32)
    xbar = jnp.clip(-0.3 * vbias, -1.0, 1.0)
    log_factor = jnp.sum(gauss * xbar - 0.5 * xbar * xbar, axis=1)
    fields = (gauss - xbar).astype(jnp.bfloat16)
    flat_chol = chol_full.reshape(NCH, N * N)

    def advance(item):
        field_row, orbit = item
        potential = (jnp.dot(field_row[None, :], flat_chol, preferred_element_type=jnp.float32) * 0.3).astype(jnp.bfloat16)
        potential = potential.reshape(N, N)
        moved = jnp.dot(potential, orbit, preferred_element_type=jnp.float32)
        return (orbit.astype(jnp.float32) + moved).astype(jnp.bfloat16)

    new_orbitals = lax.map(advance, (fields, orbitals))
    return new_orbitals, log_factor
```

```python
import functools

import jax
import jax.numpy as jnp
from jax import lax
from jax.experimental import pallas as pl
from jax.experimental.pallas import tpu as pltpu
from jax.sharding import PartitionSpec as P

TILE = 16
LANES = 128
PLANE = 4
OWN_LIMIT = 2 << 20
CHUNKS = 2
FIRST = 2
SECOND = 3


def remote(src, dst, send, recv, peer):
    return pltpu.make_async_remote_copy(
        src_ref=src,
        dst_ref=dst,
        send_sem=send,
        recv_sem=recv,
        device_id={"chol": peer},
        device_id_type=pl.DeviceIdType.MESH,
    )


def direct_kernel(
    n, chol_hbm, half_hbm, green_hbm, gauss_ref, orb_ref,
    out_ref, log_ref,
    chol, half, green, part, part_in, fields_own, fields_in, send, recv,
    load_sem, aux_sem, part_send, part_recv, field_send, field_recv, pot_send, pot_recv,
):
    me = lax.axis_index("chol")
    owned = part.shape[1]
    tiles = chol.shape[0]
    width = chol.shape[3]

    half_copy = pltpu.make_async_copy(half_hbm, half, aux_sem.at[0])
    green_copy = pltpu.make_async_copy(green_hbm, green, aux_sem.at[1])
    half_copy.start()
    green_copy.start()
    loads = [
        pltpu.make_async_copy(chol_hbm.at[:, pl.ds(t * TILE, TILE), :], chol.at[t], load_sem.at[t])
        for t in range(tiles)
    ]
    for load in loads:
        load.start()

    barrier = pltpu.get_barrier_semaphore()

    def greet(k, _):
        pl.semaphore_signal(
            barrier, inc=1, device_id={"chol": lax.rem(me + k, n)}, device_id_type=pl.DeviceIdType.MESH
        )
        return 0

    lax.fori_loop(1, n, greet, 0)

    half_copy.wait()
    green_copy.wait()

    def bias(t, acc):
        rows = pl.ds(pl.multiple_of(t * TILE, TILE), TILE)
        left = jnp.swapaxes(green[:, rows, :], 0, 1)
        right = jnp.swapaxes(half[:, rows, :], 0, 1)
        for r in range(TILE):
            acc += lax.dot_general(
                left[r], right[r], (((1,), (1,)), ((), ())), preferred_element_type=jnp.float32
            )
        return acc

    total = lax.fori_loop(0, tiles, bias, jnp.zeros((n * owned, half.shape[0]), jnp.float32))
    for d in range(n):
        part[d] = total[d * owned:(d + 1) * owned]
    pl.semaphore_wait(barrier, n - 1)

    def peer_of(k):
        return lax.rem(me + k, n)

    def push_part(k, _):
        to = peer_of(k)
        remote(part.at[to], part_in.at[me], part_send.at[to], part_recv.at[me], to).start()
        return 0

    lax.fori_loop(1, n, push_part, 0)
    part_in[me] = part[me]

    def wait_part(k, _):
        peer = peer_of(k)
        copy = remote(part.at[peer], part_in.at[peer], part_send.at[peer], part_recv.at[peer], peer)
        copy.wait_recv()
        return 0

    lax.fori_loop(1, n, wait_part, 0)
    vbias = jnp.sum(part_in[...], axis=0)
    gauss = gauss_ref[me]
    xbar = jnp.clip(-0.3 * vbias, -1.0, 1.0)
    log_ref[...] = jnp.broadcast_to(
        jnp.sum(gauss * xbar - 0.5 * xbar * xbar, axis=1, keepdims=True), log_ref.shape
    )
    mine = gauss - xbar
    fields_own[...] = mine
    fields_in[me] = mine

    def push_field(k, _):
        to = peer_of(k)
        remote(fields_own, fields_in.at[me], field_send.at[to], field_recv.at[me], to).start()
        return 0

    lax.fori_loop(1, n, push_field, 0)

    def wait_field(k, _):
        peer = peer_of(k)
        remote(fields_own, fields_in.at[peer], field_send.at[peer], field_recv.at[peer], peer).wait_recv()
        return 0

    lax.fori_loop(1, n, wait_field, 0)
    fields = jnp.concatenate([fields_in[d] for d in range(n)], axis=0).astype(jnp.bfloat16)

    def walkers_of(d):
        return pl.ds(d * owned, owned)

    def rows_of(d):
        return pl.ds(pl.multiple_of(d * TILE, TILE), TILE)

    for t in range(tiles):
        loads[t].wait()

        def strip(c, _):
            cols = pl.ds(pl.multiple_of(c * LANES, LANES), LANES)
            block = jnp.swapaxes(chol[t, :, :, cols], 0, 1)
            pots = [
                (jnp.dot(fields, block[r], preferred_element_type=jnp.float32) * 0.3).astype(jnp.bfloat16)
                for r in range(TILE)
            ]
            send[t, :, :, cols] = jnp.swapaxes(jnp.stack(pots, axis=0), 0, 1)
            return 0

        lax.fori_loop(0, width // LANES, strip, 0)

        def push_pot(k, _):
            to = peer_of(k)
            remote(
                send.at[t, walkers_of(to)], recv.at[t, :, rows_of(me), :],
                pot_send.at[t, to], pot_recv.at[t, me], to,
            ).start()
            return 0

        lax.fori_loop(1, n, push_pot, 0)
        recv[t, :, rows_of(me), :] = send[t, walkers_of(me)]

    for t in range(tiles):

        def wait_pot(k, _):
            peer = peer_of(k)
            remote(
                send.at[t, walkers_of(peer)], recv.at[t, :, rows_of(peer), :],
                pot_send.at[t, peer], pot_recv.at[t, peer], peer,
            ).wait_recv()
            return 0

        lax.fori_loop(1, n, wait_pot, 0)

        def advance(w, _):
            orbit = orb_ref[w].reshape(width, orb_ref.shape[-1])
            for first in range(0, n, 16):
                span = min(16, n - first)
                moved = jnp.dot(
                    recv[t, w, first * TILE:(first + span) * TILE, :], orbit,
                    preferred_element_type=jnp.float32,
                ).reshape(span, TILE, orbit.shape[-1])
                old = orb_ref[w, first:first + span, t].astype(jnp.float32)
                out_ref[w, first:first + span, t] = (old + moved).astype(jnp.bfloat16)
            return 0

        lax.fori_loop(0, owned, advance, 0)

    def drain(k, _):
        peer = peer_of(k)
        remote(part.at[peer], part_in.at[peer], part_send.at[peer], part_recv.at[peer], peer).wait_send()
        remote(fields_own, fields_in.at[peer], field_send.at[peer], field_recv.at[peer], peer).wait_send()
        for t in range(tiles):
            remote(
                send.at[t, walkers_of(peer)], recv.at[t, :, rows_of(peer), :],
                pot_send.at[t, peer], pot_recv.at[t, peer], peer,
            ).wait_send()
        return 0

    lax.fori_loop(1, n, drain, 0)


def line_kernel(
    n, chol_hbm, half_hbm, green_hbm, gauss_ref, orb_ref,
    out_ref, log_ref,
    chol, half, green, part, part_in, fields_own, fields_in, send, recv, guest, done, lent,
    load_sem, aux_sem, part_send, part_recv, field_send, field_recv, pot_send, pot_recv,
    orb_recv, ahead_send, back_send, lend_send, lend_recv, done_send, done_recv,
):
    me = lax.axis_index("chol")
    owned = part.shape[1]
    tiles = chol.shape[0]
    width = chol.shape[3]
    nocc = orb_ref.shape[-1]
    planes = n // PLANE
    line = planes * owned
    chunks = CHUNKS * owned
    span = n // CHUNKS

    z = me // PLANE
    seat = lax.rem(me, PLANE)
    side = z // 2
    far = 1 - side
    near_in, near_out = 1 + side, 3 * side
    far_in, far_out = 1 + far, 3 * far
    ahead = z + 1 - 2 * side
    buddy = near_in + near_out - z
    inner = z == near_in
    outer = z == near_out

    half_copy = pltpu.make_async_copy(half_hbm, half, aux_sem.at[0])
    green_copy = pltpu.make_async_copy(green_hbm, green, aux_sem.at[1])
    half_copy.start()
    green_copy.start()
    loads = [
        pltpu.make_async_copy(chol_hbm.at[:, pl.ds(t * TILE, TILE), :], chol.at[t], load_sem.at[t])
        for t in range(tiles)
    ]
    for load in loads:
        load.start()

    barrier = pltpu.get_barrier_semaphore()

    def peer_of(k):
        return lax.rem(me + k, n)

    def greet(k, _):
        pl.semaphore_signal(
            barrier, inc=1, device_id={"chol": peer_of(k)}, device_id_type=pl.DeviceIdType.MESH
        )
        return 0

    lax.fori_loop(1, n, greet, 0)
    pl.semaphore_wait(barrier, n - 1)

    def at(plane):
        return plane * PLANE + seat

    def piece(ref, c):
        return ref.at[c // CHUNKS, pl.ds(lax.rem(c, CHUNKS) * span, span)]

    def own_orbit(c):
        return remote(piece(orb_ref, c), piece(guest.at[z], c), ahead_send.at[0, c], orb_recv.at[z, c], at(ahead))

    def orbit_on(c):
        there = piece(guest.at[near_out], c)
        return remote(there, there, ahead_send.at[1, c], orb_recv.at[near_out, c], at(ahead))

    def orbit_back(plane, k, c):
        there = piece(guest.at[plane], c)
        return remote(there, there, back_send.at[k, c], orb_recv.at[plane, c], at(buddy))

    def await_orbit(plane, c):
        there = piece(guest.at[plane], c)
        remote(there, there, back_send.at[0, c], orb_recv.at[plane, c], at(ahead)).wait_recv()

    def start_own(first, last):
        def step(c, _):
            own_orbit(c).start()
            return 0

        lax.fori_loop(first, last, step, 0)

    start_own(0, FIRST)

    half_copy.wait()
    green_copy.wait()

    def bias(t, acc):
        rows = pl.ds(pl.multiple_of(t * TILE, TILE), TILE)
        left = jnp.swapaxes(green[:, rows, :], 0, 1)
        right = jnp.swapaxes(half[:, rows, :], 0, 1)
        for r in range(TILE):
            acc += lax.dot_general(
                left[r], right[r], (((1,), (1,)), ((), ())), preferred_element_type=jnp.float32
            )
        return acc

    total = lax.fori_loop(0, tiles, bias, jnp.zeros((n * owned, half.shape[0]), jnp.float32))
    for d in range(n):
        part[d] = total[d * owned:(d + 1) * owned]

    def push_part(k, _):
        to = peer_of(k)
        remote(part.at[to], part_in.at[me], part_send.at[to], part_recv.at[me], to).start()
        return 0

    lax.fori_loop(1, n, push_part, 0)
    start_own(FIRST, SECOND)
    part_in[me] = part[me]

    def wait_part(k, _):
        peer = peer_of(k)
        copy = remote(part.at[peer], part_in.at[peer], part_send.at[peer], part_recv.at[peer], peer)
        copy.wait_recv()
        return 0

    lax.fori_loop(1, n, wait_part, 0)
    vbias = jnp.sum(part_in[...], axis=0)
    gauss = gauss_ref[me]
    xbar = jnp.clip(-0.3 * vbias, -1.0, 1.0)
    log_ref[...] = jnp.broadcast_to(
        jnp.sum(gauss * xbar - 0.5 * xbar * xbar, axis=1, keepdims=True), log_ref.shape
    )
    mine = gauss - xbar
    fields_own[...] = mine
    fields_in[me] = mine

    def push_field(k, _):
        to = peer_of(k)
        remote(fields_own, fields_in.at[me], field_send.at[to], field_recv.at[me], to).start()
        return 0

    lax.fori_loop(1, n, push_field, 0)
    start_own(SECOND, chunks)

    def wait_field(k, _):
        peer = peer_of(k)
        remote(fields_own, fields_in.at[peer], field_send.at[peer], field_recv.at[peer], peer).wait_recv()
        return 0

    lax.fori_loop(1, n, wait_field, 0)
    fields = jnp.concatenate(
        [fields_in[plane * PLANE + s] for s in range(PLANE) for plane in range(planes)], axis=0
    ).astype(jnp.bfloat16)

    groups = ((far * 2 * owned, 2 * owned), (buddy * owned, owned), (z * owned, owned))

    def pot_copy(t, g, there, source):
        first, count = groups[g]
        return remote(
            send.at[t, pl.ds(there * line + first, count)], recv.at[pl.ds(first, count), source, t],
            pot_send.at[t, g, there], pot_recv.at[t, g, source], z * PLANE + there,
        )

    partner = seat + 1 - 2 * lax.rem(seat, 2)
    beside = lax.rem(seat + 2, PLANE)
    diagonal = lax.rem(partner + 2, PLANE)
    others = (beside, diagonal, partner)

    def push(t, g):
        for s in others:
            pot_copy(t, g, s, seat).start()

    def await_pots(g, seats):
        def step(t, _):
            for s in seats:
                pot_copy(t, g, s, s).wait_recv()
            return 0

        lax.fori_loop(0, tiles, step, 0)

    def fill(t):
        loads[t].wait()

        def strip(c, _):
            cols = pl.ds(pl.multiple_of(c * LANES, LANES), LANES)
            block = jnp.swapaxes(chol[t, :, :, cols], 0, 1)
            pots = [
                (jnp.dot(fields, block[r], preferred_element_type=jnp.float32) * 0.3).astype(jnp.bfloat16)
                for r in range(TILE)
            ]
            send[t, :, :, cols] = jnp.swapaxes(jnp.stack(pots, axis=0), 0, 1)
            return 0

        lax.fori_loop(0, width // LANES, strip, 0)
        recv[:, seat, t] = send[t, pl.ds(seat * line, line)]

    def forward(first, last):
        @pl.when(inner)
        def _():
            def step(c, _):
                await_orbit(near_out, c)
                orbit_on(c).start()
                await_orbit(far_in, c)
                orbit_back(far_in, 0, c).start()
                return 0

            lax.fori_loop(first, last, step, 0)

    def forward_far(first, last):
        def step(c, _):
            await_orbit(far_out, c)

            @pl.when(inner)
            def _():
                orbit_back(far_out, 1, c).start()

            return 0

        lax.fori_loop(first, last, step, 0)

    passed = 0
    for t in range(tiles):
        fill(t)
        push(t, 0)
        last = chunks - (chunks >> (t + 1)) if t < tiles - 1 else chunks
        forward(passed, last)
        passed = last
    for g in (1, 2):
        for t in range(tiles):
            push(t, g)

    def lend(s):
        return remote(
            recv.at[pl.ds(buddy * owned, owned), s], lent.at[:, s], lend_send.at[s], lend_recv.at[s], at(buddy)
        )

    @pl.when(outer)
    def _():
        lend(seat).start()
        await_pots(1, (partner,))
        lend(partner).start()

        def arrived(c, _):
            await_orbit(far_in, c)
            return 0

        lax.fori_loop(0, chunks, arrived, 0)

    def hand_back(plane, w):
        return remote(
            done.at[plane * owned + w], out_ref.at[w, pl.ds(z * PLANE, PLANE)],
            done_send.at[plane, w], done_recv.at[z, w], at(plane),
        )

    def rows_done(left, orbit, old):
        moved = jnp.dot(
            left.reshape(-1, width), orbit.reshape(width, nocc), preferred_element_type=jnp.float32
        )
        return (old.astype(jnp.float32) + moved.reshape(old.shape)).astype(jnp.bfloat16)

    here = pl.ds(z * PLANE, PLANE)

    def serve(plane, first, last):
        def step(w, _):
            done[plane * owned + w] = rows_done(
                recv[plane * owned + w], guest[plane, w], guest[plane, w, here]
            )
            hand_back(plane, w).start()
            return 0

        lax.fori_loop(first, last, step, 0)

    ready = chunks * 5 // 8
    forward_far(0, ready)
    await_pots(0, others)
    serve(far_in, 0, owned)
    for w in range(owned):
        if ready < CHUNKS * (w + 1):
            forward_far(ready, CHUNKS * (w + 1))
            ready = CHUNKS * (w + 1)
        serve(far_out, w, w + 1)

    @pl.when(outer)
    def _():
        for s in (beside, diagonal):
            await_pots(1, (s,))
            lend(s).start()

    @pl.when(inner)
    def _():
        await_pots(1, others)
        serve(near_out, 0, owned)

    await_pots(2, others)

    def advance(w, _):
        out_ref[w, here] = rows_done(recv[z * owned + w], orb_ref[w], orb_ref[w, here])
        return 0

    lax.fori_loop(0, owned, advance, 0)

    @pl.when(inner)
    def _():
        for s in (seat, partner, beside, diagonal):
            lend(s).wait_recv()

            def borrow(w, _):
                row = near_out * PLANE + s
                out_ref[w, row] = rows_done(lent[w, s], orb_ref[w], orb_ref[w, row])
                return 0

            lax.fori_loop(0, owned, borrow, 0)

    def drain(k, _):
        peer = peer_of(k)
        remote(part.at[peer], part_in.at[peer], part_send.at[peer], part_recv.at[peer], peer).wait_send()
        remote(fields_own, fields_in.at[peer], field_send.at[peer], field_recv.at[peer], peer).wait_send()
        return 0

    lax.fori_loop(1, n, drain, 0)

    def drain_pot(t, _):
        for g in range(len(groups)):
            for s in others:
                pot_copy(t, g, s, seat).wait_send()
        return 0

    lax.fori_loop(0, tiles, drain_pot, 0)

    def drain_orbit(c, _):
        own_orbit(c).wait_send()

        @pl.when(inner)
        def _():
            orbit_on(c).wait_send()
            orbit_back(far_in, 0, c).wait_send()
            orbit_back(far_out, 1, c).wait_send()

        return 0

    lax.fori_loop(0, chunks, drain_orbit, 0)

    @pl.when(outer)
    def _():
        for s in range(PLANE):
            lend(s).wait_send()

    def settle(plane):
        def step(w, _):
            remote(
                done.at[plane * owned + w], out_ref.at[w, pl.ds(plane * PLANE, PLANE)],
                done_send.at[plane, w], done_recv.at[plane, w], at(plane),
            ).wait_recv()
            return 0

        lax.fori_loop(0, owned, step, 0)

    def flush(plane):
        def step(w, _):
            hand_back(plane, w).wait_send()
            return 0

        lax.fori_loop(0, owned, step, 0)

    for plane in (far_in, far_out):
        flush(plane)
        settle(plane)

    @pl.when(inner)
    def _():
        flush(near_out)

    @pl.when(outer)
    def _():
        settle(near_in)


def on_device(n, chol_full, chol_half, green, gauss, orbitals):
    walkers, local_rows, nocc = green.shape
    owned, width, _ = orbitals.shape
    vectors = chol_half.shape[0]
    tiles = local_rows // TILE
    vmem = pl.BlockSpec(memory_space=pltpu.VMEM)
    hbm = pl.BlockSpec(memory_space=pl.ANY)
    dma = pltpu.SemaphoreType.DMA
    split = (owned, n, tiles, TILE, nocc)
    lined = n == 4 * PLANE and orbitals.size * orbitals.dtype.itemsize <= OWN_LIMIT
    if lined:
        line = walkers // PLANE
        planes = n // PLANE
        chunks = CHUNKS * owned
        extra = [
            pltpu.VMEM((line, PLANE, tiles, TILE, width), jnp.bfloat16),
            pltpu.VMEM((planes,) + split, jnp.bfloat16),
            pltpu.VMEM((line, PLANE, tiles, TILE, nocc), jnp.bfloat16),
            pltpu.VMEM((owned, PLANE, tiles, TILE, width), jnp.bfloat16),
        ]
        extra_sems = [
            dma((tiles, 3, PLANE)), dma((tiles, 3, PLANE)),
            dma((planes, chunks)), dma((2, chunks)), dma((2, chunks)),
            dma((PLANE,)), dma((PLANE,)), dma((planes, owned)), dma((planes, owned)),
        ]
    else:
        extra = [pltpu.VMEM((tiles, owned, n * TILE, width), jnp.bfloat16)]
        extra_sems = [dma((tiles, n)), dma((tiles, n))]
    moved, logs = pl.pallas_call(
        functools.partial(line_kernel if lined else direct_kernel, n),
        out_shape=(
            jax.ShapeDtypeStruct(split, jnp.bfloat16),
            jax.ShapeDtypeStruct((owned, LANES), jnp.float32),
        ),
        in_specs=[hbm, hbm, hbm, vmem, vmem],
        out_specs=(vmem, vmem),
        scratch_shapes=[
            pltpu.VMEM((tiles, vectors, TILE, width), jnp.bfloat16),
            pltpu.VMEM((vectors, local_rows, nocc), jnp.bfloat16),
            pltpu.VMEM((walkers, local_rows, nocc), jnp.bfloat16),
            pltpu.VMEM((n, owned, vectors), jnp.float32),
            pltpu.VMEM((n, owned, vectors), jnp.float32),
            pltpu.VMEM((owned, vectors), jnp.float32),
            pltpu.VMEM((n, owned, vectors), jnp.float32),
            pltpu.VMEM((tiles, walkers, TILE, width), jnp.bfloat16),
            *extra,
            dma((tiles,)), dma((2,)), dma((n,)), dma((n,)), dma((n,)), dma((n,)),
            *extra_sems,
        ],
        compiler_params=pltpu.CompilerParams(
            collective_id=0, has_side_effects=True, vmem_limit_bytes=60 << 20
        ),
    )(chol_full, chol_half, green, gauss.reshape(n, owned, vectors), orbitals.reshape(split))
    return moved.reshape(orbitals.shape), logs[:, 0]


def solution(mesh):
    placed = (
        P(None, "chol", None),
        P(None, "chol", None),
        P("grp", "chol", None),
        P("grp", None),
        P(("grp", "chol"), None, None),
    )
    return jax.shard_map(
        functools.partial(on_device, mesh.shape["chol"]),
        mesh=mesh,
        in_specs=placed,
        out_specs=(P(("grp", "chol"), None, None), P(("grp", "chol"))),
        check_vma=False,
    )
```

```python
import functools

import jax
import jax.numpy as jnp
from jax import lax
from jax.experimental import pallas as pl
from jax.experimental.pallas import tpu as pltpu
from jax.sharding import PartitionSpec as P

TILE = 16
LANES = 128
PLANE = 4
OWN_LIMIT = 2 << 20
CHUNKS = 2
FIRST = 2
SECOND = 3


def remote(src, dst, send, recv, peer):
    return pltpu.make_async_remote_copy(
        src_ref=src,
        dst_ref=dst,
        send_sem=send,
        recv_sem=recv,
        device_id={"chol": peer},
        device_id_type=pl.DeviceIdType.MESH,
    )


def direct_kernel(
    n, chol_hbm, half_hbm, green_hbm, gauss_ref, orb_ref,
    out_ref, log_ref,
    chol, half, green, part, part_in, fields_own, fields_in, send, recv,
    load_sem, aux_sem, part_send, part_recv, field_send, field_recv, pot_send, pot_recv,
):
    me = lax.axis_index("chol")
    owned = part.shape[1]
    tiles = chol.shape[0]
    width = chol.shape[3]

    half_copy = pltpu.make_async_copy(half_hbm, half, aux_sem.at[0])
    green_copy = pltpu.make_async_copy(green_hbm, green, aux_sem.at[1])
    half_copy.start()
    green_copy.start()
    loads = [
        pltpu.make_async_copy(chol_hbm.at[:, pl.ds(t * TILE, TILE), :], chol.at[t], load_sem.at[t])
        for t in range(tiles)
    ]
    for load in loads:
        load.start()

    barrier = pltpu.get_barrier_semaphore()

    def greet(k, _):
        pl.semaphore_signal(
            barrier, inc=1, device_id={"chol": lax.rem(me + k, n)}, device_id_type=pl.DeviceIdType.MESH
        )
        return 0

    lax.fori_loop(1, n, greet, 0)

    half_copy.wait()
    green_copy.wait()

    def bias(t, acc):
        rows = pl.ds(pl.multiple_of(t * TILE, TILE), TILE)
        left = jnp.swapaxes(green[:, rows, :], 0, 1)
        right = jnp.swapaxes(half[:, rows, :], 0, 1)
        for r in range(TILE):
            acc += lax.dot_general(
                left[r], right[r], (((1,), (1,)), ((), ())), preferred_element_type=jnp.float32
            )
        return acc

    total = lax.fori_loop(0, tiles, bias, jnp.zeros((n * owned, half.shape[0]), jnp.float32))
    for d in range(n):
        part[d] = total[d * owned:(d + 1) * owned]
    pl.semaphore_wait(barrier, n - 1)

    def peer_of(k):
        return lax.rem(me + k, n)

    def push_part(k, _):
        to = peer_of(k)
        remote(part.at[to], part_in.at[me], part_send.at[to], part_recv.at[me], to).start()
        return 0

    lax.fori_loop(1, n, push_part, 0)
    part_in[me] = part[me]

    def wait_part(k, _):
        peer = peer_of(k)
        copy = remote(part.at[peer], part_in.at[peer], part_send.at[peer], part_recv.at[peer], peer)
        copy.wait_recv()
        return 0

    lax.fori_loop(1, n, wait_part, 0)
    vbias = jnp.sum(part_in[...], axis=0)
    gauss = gauss_ref[me]
    xbar = jnp.clip(-0.3 * vbias, -1.0, 1.0)
    log_ref[...] = jnp.broadcast_to(
        jnp.sum(gauss * xbar - 0.5 * xbar * xbar, axis=1, keepdims=True), log_ref.shape
    )
    mine = gauss - xbar
    fields_own[...] = mine
    fields_in[me] = mine

    def push_field(k, _):
        to = peer_of(k)
        remote(fields_own, fields_in.at[me], field_send.at[to], field_recv.at[me], to).start()
        return 0

    lax.fori_loop(1, n, push_field, 0)

    def wait_field(k, _):
        peer = peer_of(k)
        remote(fields_own, fields_in.at[peer], field_send.at[peer], field_recv.at[peer], peer).wait_recv()
        return 0

    lax.fori_loop(1, n, wait_field, 0)
    fields = jnp.concatenate([fields_in[d] for d in range(n)], axis=0).astype(jnp.bfloat16)

    def walkers_of(d):
        return pl.ds(d * owned, owned)

    def rows_of(d):
        return pl.ds(pl.multiple_of(d * TILE, TILE), TILE)

    for t in range(tiles):
        loads[t].wait()

        def strip(c, _):
            cols = pl.ds(pl.multiple_of(c * LANES, LANES), LANES)
            block = jnp.swapaxes(chol[t, :, :, cols], 0, 1)
            pots = [
                (jnp.dot(fields, block[r], preferred_element_type=jnp.float32) * 0.3).astype(jnp.bfloat16)
                for r in range(TILE)
            ]
            send[t, :, :, cols] = jnp.swapaxes(jnp.stack(pots, axis=0), 0, 1)
            return 0

        lax.fori_loop(0, width // LANES, strip, 0)

        def push_pot(k, _):
            to = peer_of(k)
            remote(
                send.at[t, walkers_of(to)], recv.at[t, :, rows_of(me), :],
                pot_send.at[t, to], pot_recv.at[t, me], to,
            ).start()
            return 0

        lax.fori_loop(1, n, push_pot, 0)
        recv[t, :, rows_of(me), :] = send[t, walkers_of(me)]

    for t in range(tiles):

        def wait_pot(k, _):
            peer = peer_of(k)
            remote(
                send.at[t, walkers_of(peer)], recv.at[t, :, rows_of(peer), :],
                pot_send.at[t, peer], pot_recv.at[t, peer], peer,
            ).wait_recv()
            return 0

        lax.fori_loop(1, n, wait_pot, 0)

        def advance(w, _):
            orbit = orb_ref[w].reshape(width, orb_ref.shape[-1])
            for first in range(0, n, 16):
                span = min(16, n - first)
                moved = jnp.dot(
                    recv[t, w, first * TILE:(first + span) * TILE, :], orbit,
                    preferred_element_type=jnp.float32,
                ).reshape(span, TILE, orbit.shape[-1])
                old = orb_ref[w, first:first + span, t].astype(jnp.float32)
                out_ref[w, first:first + span, t] = (old + moved).astype(jnp.bfloat16)
            return 0

        lax.fori_loop(0, owned, advance, 0)

    def drain(k, _):
        peer = peer_of(k)
        remote(part.at[peer], part_in.at[peer], part_send.at[peer], part_recv.at[peer], peer).wait_send()
        remote(fields_own, fields_in.at[peer], field_send.at[peer], field_recv.at[peer], peer).wait_send()
        for t in range(tiles):
            remote(
                send.at[t, walkers_of(peer)], recv.at[t, :, rows_of(peer), :],
                pot_send.at[t, peer], pot_recv.at[t, peer], peer,
            ).wait_send()
        return 0

    lax.fori_loop(1, n, drain, 0)


def line_kernel(
    n, chol_hbm, half_hbm, green_hbm, gauss_ref, orb_ref,
    out_ref, log_ref,
    chol, half, green, part, part_in, fields_own, fields_in, send, recv, guest, done, lent,
    load_sem, aux_sem, part_send, part_recv, field_send, field_recv, pot_send, pot_recv,
    orb_recv, ahead_send, back_send, lend_send, lend_recv, done_send, done_recv,
):
    me = lax.axis_index("chol")
    owned = part.shape[1]
    tiles = chol.shape[0]
    width = chol.shape[3]
    nocc = orb_ref.shape[-1]
    planes = n // PLANE
    line = planes * owned
    chunks = CHUNKS * owned
    span = n // CHUNKS

    z = me // PLANE
    seat = lax.rem(me, PLANE)
    side = z // 2
    far = 1 - side
    near_in, near_out = 1 + side, 3 * side
    far_in, far_out = 1 + far, 3 * far
    ahead = z + 1 - 2 * side
    buddy = near_in + near_out - z
    inner = z == near_in
    outer = z == near_out

    half_copy = pltpu.make_async_copy(half_hbm, half, aux_sem.at[0])
    green_copy = pltpu.make_async_copy(green_hbm, green, aux_sem.at[1])
    half_copy.start()
    green_copy.start()
    loads = [
        pltpu.make_async_copy(chol_hbm.at[:, pl.ds(t * TILE, TILE), :], chol.at[t], load_sem.at[t])
        for t in range(tiles)
    ]
    for load in loads:
        load.start()

    barrier = pltpu.get_barrier_semaphore()

    def peer_of(k):
        return lax.rem(me + k, n)

    def greet(k, _):
        pl.semaphore_signal(
            barrier, inc=1, device_id={"chol": peer_of(k)}, device_id_type=pl.DeviceIdType.MESH
        )
        return 0

    lax.fori_loop(1, n, greet, 0)
    pl.semaphore_wait(barrier, n - 1)

    def at(plane):
        return plane * PLANE + seat

    def piece(ref, c):
        return ref.at[c // CHUNKS, pl.ds(lax.rem(c, CHUNKS) * span, span)]

    def own_orbit(c):
        return remote(piece(orb_ref, c), piece(guest.at[z], c), ahead_send.at[0, c], orb_recv.at[z, c], at(ahead))

    def orbit_on(c):
        there = piece(guest.at[near_out], c)
        return remote(there, there, ahead_send.at[1, c], orb_recv.at[near_out, c], at(ahead))

    def orbit_back(plane, k, c):
        there = piece(guest.at[plane], c)
        return remote(there, there, back_send.at[k, c], orb_recv.at[plane, c], at(buddy))

    def await_orbit(plane, c):
        there = piece(guest.at[plane], c)
        remote(there, there, back_send.at[0, c], orb_recv.at[plane, c], at(ahead)).wait_recv()

    def start_own(first, last):
        def step(c, _):
            own_orbit(c).start()
            return 0

        lax.fori_loop(first, last, step, 0)

    def pass_on(first, last):
        @pl.when(inner)
        def _():
            def step(c, _):
                await_orbit(near_out, c)
                orbit_on(c).start()
                return 0

            lax.fori_loop(first, last, step, 0)

    def pass_back(first, last):
        @pl.when(inner)
        def _():
            def step(c, _):
                await_orbit(far_in, c)
                orbit_back(far_in, 0, c).start()
                return 0

            lax.fori_loop(first, last, step, 0)

    start_own(0, FIRST)

    half_copy.wait()
    green_copy.wait()

    def bias(t, acc):
        rows = pl.ds(pl.multiple_of(t * TILE, TILE), TILE)
        left = jnp.swapaxes(green[:, rows, :], 0, 1)
        right = jnp.swapaxes(half[:, rows, :], 0, 1)
        for r in range(TILE):
            acc += lax.dot_general(
                left[r], right[r], (((1,), (1,)), ((), ())), preferred_element_type=jnp.float32
            )
        return acc

    total = lax.fori_loop(0, tiles, bias, jnp.zeros((n * owned, half.shape[0]), jnp.float32))
    for d in range(n):
        part[d] = total[d * owned:(d + 1) * owned]

    def push_part(k, _):
        to = peer_of(k)
        remote(part.at[to], part_in.at[me], part_send.at[to], part_recv.at[me], to).start()
        return 0

    lax.fori_loop(1, n, push_part, 0)
    start_own(FIRST, SECOND)
    pass_back(0, FIRST)
    part_in[me] = part[me]

    def wait_part(k, _):
        peer = peer_of(k)
        copy = remote(part.at[peer], part_in.at[peer], part_send.at[peer], part_recv.at[peer], peer)
        copy.wait_recv()
        return 0

    lax.fori_loop(1, n, wait_part, 0)
    vbias = jnp.sum(part_in[...], axis=0)
    gauss = gauss_ref[me]
    xbar = jnp.clip(-0.3 * vbias, -1.0, 1.0)
    log_ref[...] = jnp.broadcast_to(
        jnp.sum(gauss * xbar - 0.5 * xbar * xbar, axis=1, keepdims=True), log_ref.shape
    )
    mine = gauss - xbar
    fields_own[...] = mine
    fields_in[me] = mine

    def push_field(k, _):
        to = peer_of(k)
        remote(fields_own, fields_in.at[me], field_send.at[to], field_recv.at[me], to).start()
        return 0

    lax.fori_loop(1, n, push_field, 0)
    start_own(SECOND, chunks)
    pass_back(FIRST, SECOND)

    def wait_field(k, _):
        peer = peer_of(k)
        remote(fields_own, fields_in.at[peer], field_send.at[peer], field_recv.at[peer], peer).wait_recv()
        return 0

    lax.fori_loop(1, n, wait_field, 0)
    fields = jnp.concatenate(
        [fields_in[plane * PLANE + s] for s in range(PLANE) for plane in range(planes)], axis=0
    ).astype(jnp.bfloat16)

    groups = ((far * 2 * owned, 2 * owned), (buddy * owned, owned), (z * owned, owned))

    def pot_copy(t, g, there, source):
        first, count = groups[g]
        return remote(
            send.at[t, pl.ds(there * line + first, count)], recv.at[pl.ds(first, count), source, t],
            pot_send.at[t, g, there], pot_recv.at[t, g, source], z * PLANE + there,
        )

    partner = seat + 1 - 2 * lax.rem(seat, 2)
    beside = lax.rem(seat + 2, PLANE)
    diagonal = lax.rem(partner + 2, PLANE)
    others = (beside, diagonal, partner)

    def push(t, g):
        for s in others:
            pot_copy(t, g, s, seat).start()

    def await_pots(g, seats):
        def step(t, _):
            for s in seats:
                pot_copy(t, g, s, s).wait_recv()
            return 0

        lax.fori_loop(0, tiles, step, 0)

    def fill(t):
        loads[t].wait()

        def strip(c, _):
            cols = pl.ds(pl.multiple_of(c * LANES, LANES), LANES)
            block = jnp.swapaxes(chol[t, :, :, cols], 0, 1)
            pots = [
                (jnp.dot(fields, block[r], preferred_element_type=jnp.float32) * 0.3).astype(jnp.bfloat16)
                for r in range(TILE)
            ]
            send[t, :, :, cols] = jnp.swapaxes(jnp.stack(pots, axis=0), 0, 1)
            return 0

        lax.fori_loop(0, width // LANES, strip, 0)
        recv[:, seat, t] = send[t, pl.ds(seat * line, line)]

    def forward_far(first, last):
        def step(c, _):
            await_orbit(far_out, c)

            @pl.when(inner)
            def _():
                orbit_back(far_out, 1, c).start()

            return 0

        lax.fori_loop(first, last, step, 0)

    for t in range(tiles):
        fill(t)
        push(t, 0)
        if t < tiles - 2:
            pass_back(SECOND + t, SECOND + t + 1)
    held = SECOND + tiles - 2
    for g in (1, 2):
        for t in range(tiles):
            push(t, g)

    def lend(s):
        return remote(
            recv.at[pl.ds(buddy * owned, owned), s], lent.at[:, s], lend_send.at[s], lend_recv.at[s], at(buddy)
        )

    pass_on(0, held + 1)
    pass_back(held, held + 2)
    pass_on(held + 1, held + 2)
    pass_back(held + 2, chunks)
    pass_on(held + 2, chunks)
    @pl.when(outer)
    def _():
        lend(seat).start()
        await_pots(1, (partner,))
        lend(partner).start()

        def arrived(c, _):
            await_orbit(far_in, c)
            return 0

        lax.fori_loop(0, chunks, arrived, 0)

    def hand_back(plane, w):
        return remote(
            done.at[plane * owned + w], out_ref.at[w, pl.ds(z * PLANE, PLANE)],
            done_send.at[plane, w], done_recv.at[z, w], at(plane),
        )

    def rows_done(left, orbit, old):
        moved = jnp.dot(
            left.reshape(-1, width), orbit.reshape(width, nocc), preferred_element_type=jnp.float32
        )
        return (old.astype(jnp.float32) + moved.reshape(old.shape)).astype(jnp.bfloat16)

    here = pl.ds(z * PLANE, PLANE)

    def serve(plane, first, last):
        def step(w, _):
            done[plane * owned + w] = rows_done(
                recv[plane * owned + w], guest[plane, w], guest[plane, w, here]
            )
            hand_back(plane, w).start()
            return 0

        lax.fori_loop(first, last, step, 0)

    ready = chunks * 5 // 8
    forward_far(0, ready)
    await_pots(0, others)
    serve(far_in, 0, owned)
    for w in range(owned):
        if ready < CHUNKS * (w + 1):
            forward_far(ready, CHUNKS * (w + 1))
            ready = CHUNKS * (w + 1)
        serve(far_out, w, w + 1)
        if w == owned - 2:
            @pl.when(outer)
            def _():
                for s in (beside, diagonal):
                    await_pots(1, (s,))
                    lend(s).start()

    @pl.when(inner)
    def _():
        await_pots(1, others)
        serve(near_out, 0, owned)

    await_pots(2, others)

    def advance(w, _):
        out_ref[w, here] = rows_done(recv[z * owned + w], orb_ref[w], orb_ref[w, here])
        return 0

    lax.fori_loop(0, owned, advance, 0)

    @pl.when(inner)
    def _():
        for s in (seat, partner, beside, diagonal):
            lend(s).wait_recv()

            def borrow(w, _):
                row = near_out * PLANE + s
                out_ref[w, row] = rows_done(lent[w, s], orb_ref[w], orb_ref[w, row])
                return 0

            lax.fori_loop(0, owned, borrow, 0)

    def drain(k, _):
        peer = peer_of(k)
        remote(part.at[peer], part_in.at[peer], part_send.at[peer], part_recv.at[peer], peer).wait_send()
        remote(fields_own, fields_in.at[peer], field_send.at[peer], field_recv.at[peer], peer).wait_send()
        return 0

    lax.fori_loop(1, n, drain, 0)

    def drain_pot(t, _):
        for g in range(len(groups)):
            for s in others:
                pot_copy(t, g, s, seat).wait_send()
        return 0

    lax.fori_loop(0, tiles, drain_pot, 0)

    def drain_orbit(c, _):
        own_orbit(c).wait_send()

        @pl.when(inner)
        def _():
            orbit_on(c).wait_send()
            orbit_back(far_in, 0, c).wait_send()
            orbit_back(far_out, 1, c).wait_send()

        return 0

    lax.fori_loop(0, chunks, drain_orbit, 0)

    @pl.when(outer)
    def _():
        for s in range(PLANE):
            lend(s).wait_send()

    def settle(plane):
        def step(w, _):
            remote(
                done.at[plane * owned + w], out_ref.at[w, pl.ds(plane * PLANE, PLANE)],
                done_send.at[plane, w], done_recv.at[plane, w], at(plane),
            ).wait_recv()
            return 0

        lax.fori_loop(0, owned, step, 0)

    def flush(plane):
        def step(w, _):
            hand_back(plane, w).wait_send()
            return 0

        lax.fori_loop(0, owned, step, 0)

    for plane in (far_in, far_out):
        flush(plane)
        settle(plane)

    @pl.when(inner)
    def _():
        flush(near_out)

    @pl.when(outer)
    def _():
        settle(near_in)


def on_device(n, chol_full, chol_half, green, gauss, orbitals):
    walkers, local_rows, nocc = green.shape
    owned, width, _ = orbitals.shape
    vectors = chol_half.shape[0]
    tiles = local_rows // TILE
    vmem = pl.BlockSpec(memory_space=pltpu.VMEM)
    hbm = pl.BlockSpec(memory_space=pl.ANY)
    dma = pltpu.SemaphoreType.DMA
    split = (owned, n, tiles, TILE, nocc)
    lined = n == 4 * PLANE and orbitals.size * orbitals.dtype.itemsize <= OWN_LIMIT
    if lined:
        line = walkers // PLANE
        planes = n // PLANE
        chunks = CHUNKS * owned
        extra = [
            pltpu.VMEM((line, PLANE, tiles, TILE, width), jnp.bfloat16),
            pltpu.VMEM((planes,) + split, jnp.bfloat16),
            pltpu.VMEM((line, PLANE, tiles, TILE, nocc), jnp.bfloat16),
            pltpu.VMEM((owned, PLANE, tiles, TILE, width), jnp.bfloat16),
        ]
        extra_sems = [
            dma((tiles, 3, PLANE)), dma((tiles, 3, PLANE)),
            dma((planes, chunks)), dma((2, chunks)), dma((2, chunks)),
            dma((PLANE,)), dma((PLANE,)), dma((planes, owned)), dma((planes, owned)),
        ]
    else:
        extra = [pltpu.VMEM((tiles, owned, n * TILE, width), jnp.bfloat16)]
        extra_sems = [dma((tiles, n)), dma((tiles, n))]
    moved, logs = pl.pallas_call(
        functools.partial(line_kernel if lined else direct_kernel, n),
        out_shape=(
            jax.ShapeDtypeStruct(split, jnp.bfloat16),
            jax.ShapeDtypeStruct((owned, LANES), jnp.float32),
        ),
        in_specs=[hbm, hbm, hbm, vmem, vmem],
        out_specs=(vmem, vmem),
        scratch_shapes=[
            pltpu.VMEM((tiles, vectors, TILE, width), jnp.bfloat16),
            pltpu.VMEM((vectors, local_rows, nocc), jnp.bfloat16),
            pltpu.VMEM((walkers, local_rows, nocc), jnp.bfloat16),
            pltpu.VMEM((n, owned, vectors), jnp.float32),
            pltpu.VMEM((n, owned, vectors), jnp.float32),
            pltpu.VMEM((owned, vectors), jnp.float32),
            pltpu.VMEM((n, owned, vectors), jnp.float32),
            pltpu.VMEM((tiles, walkers, TILE, width), jnp.bfloat16),
            *extra,
            dma((tiles,)), dma((2,)), dma((n,)), dma((n,)), dma((n,)), dma((n,)),
            *extra_sems,
        ],
        compiler_params=pltpu.CompilerParams(
            collective_id=0, has_side_effects=True, vmem_limit_bytes=60 << 20
        ),
    )(chol_full, chol_half, green, gauss.reshape(n, owned, vectors), orbitals.reshape(split))
    return moved.reshape(orbitals.shape), logs[:, 0]


def solution(mesh):
    placed = (
        P(None, "chol", None),
        P(None, "chol", None),
        P("grp", "chol", None),
        P("grp", None),
        P(("grp", "chol"), None, None),
    )
    return jax.shard_map(
        functools.partial(on_device, mesh.shape["chol"]),
        mesh=mesh,
        in_specs=placed,
        out_specs=(P(("grp", "chol"), None, None), P(("grp", "chol"))),
        check_vma=False,
    )
```

```python
import functools

import jax
import jax.numpy as jnp
from jax import lax
from jax.experimental import pallas as pl
from jax.experimental.pallas import tpu as pltpu
from jax.sharding import PartitionSpec as P

TILE = 16
LANES = 128
PLANE = 4
OWN_LIMIT = 2 << 20
CHUNKS = 2
FIRST = 2
SECOND = 3


def remote(src, dst, send, recv, peer):
    return pltpu.make_async_remote_copy(
        src_ref=src,
        dst_ref=dst,
        send_sem=send,
        recv_sem=recv,
        device_id={"chol": peer},
        device_id_type=pl.DeviceIdType.MESH,
    )


def direct_kernel(
    n, chol_hbm, half_hbm, green_hbm, gauss_ref, orb_ref,
    out_ref, log_ref,
    chol, half, green, part, part_in, fields_own, fields_in, send, recv,
    load_sem, aux_sem, part_send, part_recv, field_send, field_recv, pot_send, pot_recv,
):
    me = lax.axis_index("chol")
    owned = part.shape[1]
    tiles = chol.shape[0]
    width = chol.shape[3]

    half_copy = pltpu.make_async_copy(half_hbm, half, aux_sem.at[0])
    green_copy = pltpu.make_async_copy(green_hbm, green, aux_sem.at[1])
    half_copy.start()
    green_copy.start()
    loads = [
        pltpu.make_async_copy(chol_hbm.at[:, pl.ds(t * TILE, TILE), :], chol.at[t], load_sem.at[t])
        for t in range(tiles)
    ]
    for load in loads:
        load.start()

    barrier = pltpu.get_barrier_semaphore()

    def greet(k, _):
        pl.semaphore_signal(
            barrier, inc=1, device_id={"chol": lax.rem(me + k, n)}, device_id_type=pl.DeviceIdType.MESH
        )
        return 0

    lax.fori_loop(1, n, greet, 0)

    half_copy.wait()
    green_copy.wait()

    def bias(t, acc):
        rows = pl.ds(pl.multiple_of(t * TILE, TILE), TILE)
        left = jnp.swapaxes(green[:, rows, :], 0, 1)
        right = jnp.swapaxes(half[:, rows, :], 0, 1)
        for r in range(TILE):
            acc += lax.dot_general(
                left[r], right[r], (((1,), (1,)), ((), ())), preferred_element_type=jnp.float32
            )
        return acc

    total = lax.fori_loop(0, tiles, bias, jnp.zeros((n * owned, half.shape[0]), jnp.float32))
    for d in range(n):
        part[d] = total[d * owned:(d + 1) * owned]
    pl.semaphore_wait(barrier, n - 1)

    def peer_of(k):
        return lax.rem(me + k, n)

    def push_part(k, _):
        to = peer_of(k)
        remote(part.at[to], part_in.at[me], part_send.at[to], part_recv.at[me], to).start()
        return 0

    lax.fori_loop(1, n, push_part, 0)
    part_in[me] = part[me]

    def wait_part(k, _):
        peer = peer_of(k)
        copy = remote(part.at[peer], part_in.at[peer], part_send.at[peer], part_recv.at[peer], peer)
        copy.wait_recv()
        return 0

    lax.fori_loop(1, n, wait_part, 0)
    vbias = jnp.sum(part_in[...], axis=0)
    gauss = gauss_ref[me]
    xbar = jnp.clip(-0.3 * vbias, -1.0, 1.0)
    log_ref[...] = jnp.broadcast_to(
        jnp.sum(gauss * xbar - 0.5 * xbar * xbar, axis=1, keepdims=True), log_ref.shape
    )
    mine = gauss - xbar
    fields_own[...] = mine
    fields_in[me] = mine

    def push_field(k, _):
        to = peer_of(k)
        remote(fields_own, fields_in.at[me], field_send.at[to], field_recv.at[me], to).start()
        return 0

    lax.fori_loop(1, n, push_field, 0)

    def wait_field(k, _):
        peer = peer_of(k)
        remote(fields_own, fields_in.at[peer], field_send.at[peer], field_recv.at[peer], peer).wait_recv()
        return 0

    lax.fori_loop(1, n, wait_field, 0)
    fields = jnp.concatenate([fields_in[d] for d in range(n)], axis=0).astype(jnp.bfloat16)

    def walkers_of(d):
        return pl.ds(d * owned, owned)

    def rows_of(d):
        return pl.ds(pl.multiple_of(d * TILE, TILE), TILE)

    for t in range(tiles):
        loads[t].wait()

        def strip(c, _):
            cols = pl.ds(pl.multiple_of(c * LANES, LANES), LANES)
            block = jnp.swapaxes(chol[t, :, :, cols], 0, 1)
            pots = [
                (jnp.dot(fields, block[r], preferred_element_type=jnp.float32) * 0.3).astype(jnp.bfloat16)
                for r in range(TILE)
            ]
            send[t, :, :, cols] = jnp.swapaxes(jnp.stack(pots, axis=0), 0, 1)
            return 0

        lax.fori_loop(0, width // LANES, strip, 0)

        def push_pot(k, _):
            to = peer_of(k)
            remote(
                send.at[t, walkers_of(to)], recv.at[t, :, rows_of(me), :],
                pot_send.at[t, to], pot_recv.at[t, me], to,
            ).start()
            return 0

        lax.fori_loop(1, n, push_pot, 0)
        recv[t, :, rows_of(me), :] = send[t, walkers_of(me)]

    for t in range(tiles):

        def wait_pot(k, _):
            peer = peer_of(k)
            remote(
                send.at[t, walkers_of(peer)], recv.at[t, :, rows_of(peer), :],
                pot_send.at[t, peer], pot_recv.at[t, peer], peer,
            ).wait_recv()
            return 0

        lax.fori_loop(1, n, wait_pot, 0)

        def advance(w, _):
            orbit = orb_ref[w].reshape(width, orb_ref.shape[-1])
            for first in range(0, n, 16):
                span = min(16, n - first)
                moved = jnp.dot(
                    recv[t, w, first * TILE:(first + span) * TILE, :], orbit,
                    preferred_element_type=jnp.float32,
                ).reshape(span, TILE, orbit.shape[-1])
                old = orb_ref[w, first:first + span, t].astype(jnp.float32)
                out_ref[w, first:first + span, t] = (old + moved).astype(jnp.bfloat16)
            return 0

        lax.fori_loop(0, owned, advance, 0)

    def drain(k, _):
        peer = peer_of(k)
        remote(part.at[peer], part_in.at[peer], part_send.at[peer], part_recv.at[peer], peer).wait_send()
        remote(fields_own, fields_in.at[peer], field_send.at[peer], field_recv.at[peer], peer).wait_send()
        for t in range(tiles):
            remote(
                send.at[t, walkers_of(peer)], recv.at[t, :, rows_of(peer), :],
                pot_send.at[t, peer], pot_recv.at[t, peer], peer,
            ).wait_send()
        return 0

    lax.fori_loop(1, n, drain, 0)


def line_kernel(
    n, chol_hbm, half_hbm, green_hbm, gauss_ref, orb_ref,
    out_ref, log_ref,
    chol, half, green, part, part_in, fields_own, fields_in, send, recv, guest, done, lent,
    load_sem, aux_sem, part_send, part_recv, field_send, field_recv, pot_send, pot_recv,
    orb_recv, ahead_send, back_send, lend_send, lend_recv, done_send, done_recv,
):
    me = lax.axis_index("chol")
    owned = part.shape[1]
    tiles = chol.shape[0]
    width = chol.shape[3]
    nocc = orb_ref.shape[-1]
    planes = n // PLANE
    line = planes * owned
    chunks = CHUNKS * owned
    span = n // CHUNKS

    z = me // PLANE
    seat = lax.rem(me, PLANE)
    side = z // 2
    far = 1 - side
    near_in, near_out = 1 + side, 3 * side
    far_in, far_out = 1 + far, 3 * far
    ahead = z + 1 - 2 * side
    buddy = near_in + near_out - z
    inner = z == near_in
    outer = z == near_out

    half_copy = pltpu.make_async_copy(half_hbm, half, aux_sem.at[0])
    green_copy = pltpu.make_async_copy(green_hbm, green, aux_sem.at[1])
    half_copy.start()
    green_copy.start()
    loads = [
        pltpu.make_async_copy(chol_hbm.at[:, pl.ds(t * TILE, TILE), :], chol.at[t], load_sem.at[t])
        for t in range(tiles)
    ]
    for load in loads:
        load.start()

    barrier = pltpu.get_barrier_semaphore()

    def peer_of(k):
        return lax.rem(me + k, n)

    def greet(k, _):
        pl.semaphore_signal(
            barrier, inc=1, device_id={"chol": peer_of(k)}, device_id_type=pl.DeviceIdType.MESH
        )
        return 0

    lax.fori_loop(1, n, greet, 0)
    pl.semaphore_wait(barrier, n - 1)

    def at(plane):
        return plane * PLANE + seat

    def piece(ref, c):
        return ref.at[c // CHUNKS, pl.ds(lax.rem(c, CHUNKS) * span, span)]

    def own_orbit(c):
        return remote(piece(orb_ref, c), piece(guest.at[z], c), ahead_send.at[0, c], orb_recv.at[z, c], at(ahead))

    def orbit_on(c):
        there = piece(guest.at[near_out], c)
        return remote(there, there, ahead_send.at[1, c], orb_recv.at[near_out, c], at(ahead))

    def orbit_back(plane, k, c):
        there = piece(guest.at[plane], c)
        return remote(there, there, back_send.at[k, c], orb_recv.at[plane, c], at(buddy))

    def await_orbit(plane, c):
        there = piece(guest.at[plane], c)
        remote(there, there, back_send.at[0, c], orb_recv.at[plane, c], at(ahead)).wait_recv()

    def start_own(first, last):
        def step(c, _):
            own_orbit(c).start()
            return 0

        lax.fori_loop(first, last, step, 0)

    def pass_on(first, last):
        @pl.when(inner)
        def _():
            def step(c, _):
                await_orbit(near_out, c)
                orbit_on(c).start()
                return 0

            lax.fori_loop(first, last, step, 0)

    def pass_back(first, last):
        @pl.when(inner)
        def _():
            def step(c, _):
                await_orbit(far_in, c)
                orbit_back(far_in, 0, c).start()
                return 0

            lax.fori_loop(first, last, step, 0)

    start_own(0, FIRST)

    half_copy.wait()
    green_copy.wait()

    def bias(t, acc):
        rows = pl.ds(pl.multiple_of(t * TILE, TILE), TILE)
        left = jnp.swapaxes(green[:, rows, :], 0, 1)
        right = jnp.swapaxes(half[:, rows, :], 0, 1)
        for r in range(TILE):
            acc += lax.dot_general(
                left[r], right[r], (((1,), (1,)), ((), ())), preferred_element_type=jnp.float32
            )
        return acc

    total = lax.fori_loop(0, tiles, bias, jnp.zeros((n * owned, half.shape[0]), jnp.float32))
    for d in range(n):
        part[d] = total[d * owned:(d + 1) * owned]

    def push_part(k, _):
        to = peer_of(k)
        remote(part.at[to], part_in.at[me], part_send.at[to], part_recv.at[me], to).start()
        return 0

    lax.fori_loop(1, n, push_part, 0)
    start_own(FIRST, SECOND)
    pass_back(0, FIRST)
    part_in[me] = part[me]

    def wait_part(k, _):
        peer = peer_of(k)
        copy = remote(part.at[peer], part_in.at[peer], part_send.at[peer], part_recv.at[peer], peer)
        copy.wait_recv()
        return 0

    lax.fori_loop(1, n, wait_part, 0)
    vbias = jnp.sum(part_in[...], axis=0)
    gauss = gauss_ref[me]
    xbar = jnp.clip(-0.3 * vbias, -1.0, 1.0)
    log_ref[...] = jnp.broadcast_to(
        jnp.sum(gauss * xbar - 0.5 * xbar * xbar, axis=1, keepdims=True), log_ref.shape
    )
    mine = gauss - xbar
    fields_own[...] = mine
    fields_in[me] = mine

    def push_field(k, _):
        to = peer_of(k)
        remote(fields_own, fields_in.at[me], field_send.at[to], field_recv.at[me], to).start()
        return 0

    lax.fori_loop(1, n, push_field, 0)
    start_own(SECOND, chunks)
    pass_back(FIRST, SECOND)

    def wait_field(k, _):
        peer = peer_of(k)
        remote(fields_own, fields_in.at[peer], field_send.at[peer], field_recv.at[peer], peer).wait_recv()
        return 0

    lax.fori_loop(1, n, wait_field, 0)
    fields = jnp.concatenate(
        [fields_in[plane * PLANE + s] for s in range(PLANE) for plane in range(planes)], axis=0
    ).astype(jnp.bfloat16)

    order = (
        jnp.where(inner, far_in, near_in), jnp.where(inner, far_out, far_in),
        jnp.where(inner, near_out, far_out), z,
    )

    def pot_copy(t, plane, there, source):
        return remote(
            send.at[t, pl.ds(there * line + plane * owned, owned)],
            recv.at[pl.ds(plane * owned, owned), source, t],
            pot_send.at[t, plane, there], pot_recv.at[t, plane, source], z * PLANE + there,
        )

    partner = seat + 1 - 2 * lax.rem(seat, 2)
    beside = lax.rem(seat + 2, PLANE)
    diagonal = lax.rem(partner + 2, PLANE)
    others = (beside, diagonal, partner)

    def push(t, plane):
        for s in others:
            pot_copy(t, plane, s, seat).start()

    def await_pots(plane, seats):
        def step(t, _):
            for s in seats:
                pot_copy(t, plane, s, s).wait_recv()
            return 0

        lax.fori_loop(0, tiles, step, 0)

    def fill(t):
        loads[t].wait()

        def strip(c, _):
            cols = pl.ds(pl.multiple_of(c * LANES, LANES), LANES)
            block = jnp.swapaxes(chol[t, :, :, cols], 0, 1)
            pots = [
                (jnp.dot(fields, block[r], preferred_element_type=jnp.float32) * 0.3).astype(jnp.bfloat16)
                for r in range(TILE)
            ]
            send[t, :, :, cols] = jnp.swapaxes(jnp.stack(pots, axis=0), 0, 1)
            return 0

        lax.fori_loop(0, width // LANES, strip, 0)
        recv[:, seat, t] = send[t, pl.ds(seat * line, line)]

    def forward_far(first, last):
        def step(c, _):
            await_orbit(far_out, c)

            @pl.when(inner)
            def _():
                orbit_back(far_out, 1, c).start()

            return 0

        lax.fori_loop(first, last, step, 0)

    for t in range(tiles):
        fill(t)
        push(t, order[0])
        if t < tiles - 2:
            pass_back(SECOND + t, SECOND + t + 1)
    held = SECOND + tiles - 2
    for plane in order[1:]:
        for t in range(tiles):
            push(t, plane)

    def lend(s):
        return remote(
            recv.at[pl.ds(buddy * owned, owned), s], lent.at[:, s], lend_send.at[s], lend_recv.at[s], at(buddy)
        )

    pass_on(0, held + 1)
    pass_back(held, held + 2)
    pass_on(held + 1, held + 2)
    pass_back(held + 2, chunks)
    pass_on(held + 2, chunks)
    @pl.when(outer)
    def _():
        lend(seat).start()
        for s in (partner, beside, diagonal):
            await_pots(near_in, (s,))
            lend(s).start()

        def arrived(c, _):
            await_orbit(far_in, c)
            return 0

        lax.fori_loop(0, chunks, arrived, 0)

    def hand_back(plane, w):
        return remote(
            done.at[plane * owned + w], out_ref.at[w, pl.ds(z * PLANE, PLANE)],
            done_send.at[plane, w], done_recv.at[z, w], at(plane),
        )

    def rows_done(left, orbit, old):
        moved = jnp.dot(
            left.reshape(-1, width), orbit.reshape(width, nocc), preferred_element_type=jnp.float32
        )
        return (old.astype(jnp.float32) + moved.reshape(old.shape)).astype(jnp.bfloat16)

    here = pl.ds(z * PLANE, PLANE)

    def serve(plane, first, last):
        def step(w, _):
            done[plane * owned + w] = rows_done(
                recv[plane * owned + w], guest[plane, w], guest[plane, w, here]
            )
            hand_back(plane, w).start()
            return 0

        lax.fori_loop(first, last, step, 0)

    forward_far(0, CHUNKS)
    await_pots(far_in, others)
    serve(far_in, 0, owned)
    forward_far(CHUNKS, 2 * CHUNKS)
    await_pots(far_out, others)
    serve(far_out, 0, 2)
    for w in range(2, owned):
        forward_far(CHUNKS * w, CHUNKS * (w + 1))
        serve(far_out, w, w + 1)

    @pl.when(inner)
    def _():
        await_pots(near_out, others)
        serve(near_out, 0, owned)

    await_pots(z, others)

    def advance(w, _):
        out_ref[w, here] = rows_done(recv[z * owned + w], orb_ref[w], orb_ref[w, here])
        return 0

    lax.fori_loop(0, owned, advance, 0)

    @pl.when(inner)
    def _():
        for s in (seat, partner, beside, diagonal):
            lend(s).wait_recv()

            def borrow(w, _):
                row = near_out * PLANE + s
                out_ref[w, row] = rows_done(lent[w, s], orb_ref[w], orb_ref[w, row])
                return 0

            lax.fori_loop(0, owned, borrow, 0)

    def drain(k, _):
        peer = peer_of(k)
        remote(part.at[peer], part_in.at[peer], part_send.at[peer], part_recv.at[peer], peer).wait_send()
        remote(fields_own, fields_in.at[peer], field_send.at[peer], field_recv.at[peer], peer).wait_send()
        return 0

    lax.fori_loop(1, n, drain, 0)

    def drain_pot(t, _):
        for plane in range(planes):
            for s in others:
                pot_copy(t, plane, s, seat).wait_send()
        return 0

    lax.fori_loop(0, tiles, drain_pot, 0)

    def drain_orbit(c, _):
        own_orbit(c).wait_send()

        @pl.when(inner)
        def _():
            orbit_on(c).wait_send()
            orbit_back(far_in, 0, c).wait_send()
            orbit_back(far_out, 1, c).wait_send()

        return 0

    lax.fori_loop(0, chunks, drain_orbit, 0)

    @pl.when(outer)
    def _():
        for s in range(PLANE):
            lend(s).wait_send()

    def settle(plane):
        def step(w, _):
            remote(
                done.at[plane * owned + w], out_ref.at[w, pl.ds(plane * PLANE, PLANE)],
                done_send.at[plane, w], done_recv.at[plane, w], at(plane),
            ).wait_recv()
            return 0

        lax.fori_loop(0, owned, step, 0)

    def flush(plane):
        def step(w, _):
            hand_back(plane, w).wait_send()
            return 0

        lax.fori_loop(0, owned, step, 0)

    for plane in (far_in, far_out):
        flush(plane)
        settle(plane)

    @pl.when(inner)
    def _():
        flush(near_out)

    @pl.when(outer)
    def _():
        settle(near_in)


def on_device(n, chol_full, chol_half, green, gauss, orbitals):
    walkers, local_rows, nocc = green.shape
    owned, width, _ = orbitals.shape
    vectors = chol_half.shape[0]
    tiles = local_rows // TILE
    vmem = pl.BlockSpec(memory_space=pltpu.VMEM)
    hbm = pl.BlockSpec(memory_space=pl.ANY)
    dma = pltpu.SemaphoreType.DMA
    split = (owned, n, tiles, TILE, nocc)
    lined = n == 4 * PLANE and orbitals.size * orbitals.dtype.itemsize <= OWN_LIMIT
    if lined:
        line = walkers // PLANE
        planes = n // PLANE
        chunks = CHUNKS * owned
        extra = [
            pltpu.VMEM((line, PLANE, tiles, TILE, width), jnp.bfloat16),
            pltpu.VMEM((planes,) + split, jnp.bfloat16),
            pltpu.VMEM((line, PLANE, tiles, TILE, nocc), jnp.bfloat16),
            pltpu.VMEM((owned, PLANE, tiles, TILE, width), jnp.bfloat16),
        ]
        extra_sems = [
            dma((tiles, planes, PLANE)), dma((tiles, planes, PLANE)),
            dma((planes, chunks)), dma((2, chunks)), dma((2, chunks)),
            dma((PLANE,)), dma((PLANE,)), dma((planes, owned)), dma((planes, owned)),
        ]
    else:
        extra = [pltpu.VMEM((tiles, owned, n * TILE, width), jnp.bfloat16)]
        extra_sems = [dma((tiles, n)), dma((tiles, n))]
    moved, logs = pl.pallas_call(
        functools.partial(line_kernel if lined else direct_kernel, n),
        out_shape=(
            jax.ShapeDtypeStruct(split, jnp.bfloat16),
            jax.ShapeDtypeStruct((owned, LANES), jnp.float32),
        ),
        in_specs=[hbm, hbm, hbm, vmem, vmem],
        out_specs=(vmem, vmem),
        scratch_shapes=[
            pltpu.VMEM((tiles, vectors, TILE, width), jnp.bfloat16),
            pltpu.VMEM((vectors, local_rows, nocc), jnp.bfloat16),
            pltpu.VMEM((walkers, local_rows, nocc), jnp.bfloat16),
            pltpu.VMEM((n, owned, vectors), jnp.float32),
            pltpu.VMEM((n, owned, vectors), jnp.float32),
            pltpu.VMEM((owned, vectors), jnp.float32),
            pltpu.VMEM((n, owned, vectors), jnp.float32),
            pltpu.VMEM((tiles, walkers, TILE, width), jnp.bfloat16),
            *extra,
            dma((tiles,)), dma((2,)), dma((n,)), dma((n,)), dma((n,)), dma((n,)),
            *extra_sems,
        ],
        compiler_params=pltpu.CompilerParams(
            collective_id=0, has_side_effects=True, vmem_limit_bytes=60 << 20
        ),
    )(chol_full, chol_half, green, gauss.reshape(n, owned, vectors), orbitals.reshape(split))
    return moved.reshape(orbitals.shape), logs[:, 0]


def solution(mesh):
    placed = (
        P(None, "chol", None),
        P(None, "chol", None),
        P("grp", "chol", None),
        P("grp", None),
        P(("grp", "chol"), None, None),
    )
    return jax.shard_map(
        functools.partial(on_device, mesh.shape["chol"]),
        mesh=mesh,
        in_specs=placed,
        out_specs=(P(("grp", "chol"), None, None), P(("grp", "chol"))),
        check_vma=False,
    )
```

```python
import functools

import jax
import jax.numpy as jnp
from jax import lax
from jax.experimental import pallas as pl
from jax.experimental.pallas import tpu as pltpu
from jax.sharding import PartitionSpec as P

TILE = 16
LANES = 128
PLANE = 4
OWN_LIMIT = 2 << 20
CHUNKS = 2
FIRST = 1
SECOND = 2


def remote(src, dst, send, recv, peer):
    return pltpu.make_async_remote_copy(
        src_ref=src,
        dst_ref=dst,
        send_sem=send,
        recv_sem=recv,
        device_id={"chol": peer},
        device_id_type=pl.DeviceIdType.MESH,
    )


def direct_kernel(
    n, chol_hbm, half_hbm, green_hbm, gauss_ref, orb_ref,
    out_ref, log_ref,
    chol, half, green, part, part_in, fields_own, fields_in, send, recv,
    load_sem, aux_sem, part_send, part_recv, field_send, field_recv, pot_send, pot_recv,
):
    me = lax.axis_index("chol")
    owned = part.shape[1]
    tiles = chol.shape[0]
    width = chol.shape[3]

    half_copy = pltpu.make_async_copy(half_hbm, half, aux_sem.at[0])
    green_copy = pltpu.make_async_copy(green_hbm, green, aux_sem.at[1])
    half_copy.start()
    green_copy.start()
    loads = [
        pltpu.make_async_copy(chol_hbm.at[:, pl.ds(t * TILE, TILE), :], chol.at[t], load_sem.at[t])
        for t in range(tiles)
    ]
    for load in loads:
        load.start()

    barrier = pltpu.get_barrier_semaphore()

    def greet(k, _):
        pl.semaphore_signal(
            barrier, inc=1, device_id={"chol": lax.rem(me + k, n)}, device_id_type=pl.DeviceIdType.MESH
        )
        return 0

    lax.fori_loop(1, n, greet, 0)

    half_copy.wait()
    green_copy.wait()

    def bias(t, acc):
        rows = pl.ds(pl.multiple_of(t * TILE, TILE), TILE)
        left = jnp.swapaxes(green[:, rows, :], 0, 1)
        right = jnp.swapaxes(half[:, rows, :], 0, 1)
        for r in range(TILE):
            acc += lax.dot_general(
                left[r], right[r], (((1,), (1,)), ((), ())), preferred_element_type=jnp.float32
            )
        return acc

    total = lax.fori_loop(0, tiles, bias, jnp.zeros((n * owned, half.shape[0]), jnp.float32))
    for d in range(n):
        part[d] = total[d * owned:(d + 1) * owned]
    pl.semaphore_wait(barrier, n - 1)

    def peer_of(k):
        return lax.rem(me + k, n)

    def push_part(k, _):
        to = peer_of(k)
        remote(part.at[to], part_in.at[me], part_send.at[to], part_recv.at[me], to).start()
        return 0

    lax.fori_loop(1, n, push_part, 0)
    part_in[me] = part[me]

    def wait_part(k, _):
        peer = peer_of(k)
        copy = remote(part.at[peer], part_in.at[peer], part_send.at[peer], part_recv.at[peer], peer)
        copy.wait_recv()
        return 0

    lax.fori_loop(1, n, wait_part, 0)
    vbias = jnp.sum(part_in[...], axis=0)
    gauss = gauss_ref[me]
    xbar = jnp.clip(-0.3 * vbias, -1.0, 1.0)
    log_ref[...] = jnp.broadcast_to(
        jnp.sum(gauss * xbar - 0.5 * xbar * xbar, axis=1, keepdims=True), log_ref.shape
    )
    mine = gauss - xbar
    fields_own[...] = mine
    fields_in[me] = mine

    def push_field(k, _):
        to = peer_of(k)
        remote(fields_own, fields_in.at[me], field_send.at[to], field_recv.at[me], to).start()
        return 0

    lax.fori_loop(1, n, push_field, 0)

    def wait_field(k, _):
        peer = peer_of(k)
        remote(fields_own, fields_in.at[peer], field_send.at[peer], field_recv.at[peer], peer).wait_recv()
        return 0

    lax.fori_loop(1, n, wait_field, 0)
    fields = jnp.concatenate([fields_in[d] for d in range(n)], axis=0).astype(jnp.bfloat16)

    def walkers_of(d):
        return pl.ds(d * owned, owned)

    def rows_of(d):
        return pl.ds(pl.multiple_of(d * TILE, TILE), TILE)

    for t in range(tiles):
        loads[t].wait()

        def strip(c, _):
            cols = pl.ds(pl.multiple_of(c * LANES, LANES), LANES)
            block = jnp.swapaxes(chol[t, :, :, cols], 0, 1)
            pots = [
                (jnp.dot(fields, block[r], preferred_element_type=jnp.float32) * 0.3).astype(jnp.bfloat16)
                for r in range(TILE)
            ]
            send[t, :, :, cols] = jnp.swapaxes(jnp.stack(pots, axis=0), 0, 1)
            return 0

        lax.fori_loop(0, width // LANES, strip, 0)

        def push_pot(k, _):
            to = peer_of(k)
            remote(
                send.at[t, walkers_of(to)], recv.at[t, :, rows_of(me), :],
                pot_send.at[t, to], pot_recv.at[t, me], to,
            ).start()
            return 0

        lax.fori_loop(1, n, push_pot, 0)
        recv[t, :, rows_of(me), :] = send[t, walkers_of(me)]

    for t in range(tiles):

        def wait_pot(k, _):
            peer = peer_of(k)
            remote(
                send.at[t, walkers_of(peer)], recv.at[t, :, rows_of(peer), :],
                pot_send.at[t, peer], pot_recv.at[t, peer], peer,
            ).wait_recv()
            return 0

        lax.fori_loop(1, n, wait_pot, 0)

        def advance(w, _):
            orbit = orb_ref[w].reshape(width, orb_ref.shape[-1])
            for first in range(0, n, 16):
                span = min(16, n - first)
                moved = jnp.dot(
                    recv[t, w, first * TILE:(first + span) * TILE, :], orbit,
                    preferred_element_type=jnp.float32,
                ).reshape(span, TILE, orbit.shape[-1])
                old = orb_ref[w, first:first + span, t].astype(jnp.float32)
                out_ref[w, first:first + span, t] = (old + moved).astype(jnp.bfloat16)
            return 0

        lax.fori_loop(0, owned, advance, 0)

    def drain(k, _):
        peer = peer_of(k)
        remote(part.at[peer], part_in.at[peer], part_send.at[peer], part_recv.at[peer], peer).wait_send()
        remote(fields_own, fields_in.at[peer], field_send.at[peer], field_recv.at[peer], peer).wait_send()
        for t in range(tiles):
            remote(
                send.at[t, walkers_of(peer)], recv.at[t, :, rows_of(peer), :],
                pot_send.at[t, peer], pot_recv.at[t, peer], peer,
            ).wait_send()
        return 0

    lax.fori_loop(1, n, drain, 0)


def line_kernel(
    n, chol_hbm, half_hbm, green_hbm, gauss_hbm, orb_hbm,
    out_ref, log_ref,
    chol, half, green, gauss_ref, orb_ref, part, part_in, fields_own, fields_in, send, recv, guest, done, lent,
    load_sem, aux_sem, part_sem, field_sem, pot_send, pot_recv, orb_send, orb_recv,
    lend_send, lend_recv, done_send, done_recv,
):
    me = lax.axis_index("chol")
    owned = part.shape[1]
    tiles = chol.shape[0]
    width = chol.shape[3]
    nocc = orb_ref.shape[-1]
    planes = n // PLANE
    line = planes * owned
    chunks = CHUNKS * owned
    span = n // CHUNKS

    z = me // PLANE
    seat = lax.rem(me, PLANE)
    side = z // 2
    far = 1 - side
    near_in, near_out = 1 + side, 3 * side
    far_in, far_out = 1 + far, 3 * far
    ahead = z + 1 - 2 * side
    buddy = near_in + near_out - z
    inner = z == near_in
    outer = z == near_out

    half_copy = pltpu.make_async_copy(half_hbm, half, aux_sem.at[0])
    green_copy = pltpu.make_async_copy(green_hbm, green, aux_sem.at[1])
    gauss_copy = pltpu.make_async_copy(gauss_hbm, gauss_ref, aux_sem.at[2])
    orb_copy = pltpu.make_async_copy(orb_hbm, orb_ref, aux_sem.at[3])
    for copy in (orb_copy, green_copy, half_copy, gauss_copy):
        copy.start()
    loads = [
        pltpu.make_async_copy(chol_hbm.at[:, pl.ds(t * TILE, TILE), :], chol.at[t], load_sem.at[t])
        for t in range(tiles)
    ]
    barrier = pltpu.get_barrier_semaphore()

    def peer_of(k):
        return lax.rem(me + k, n)

    def greet(k, _):
        pl.semaphore_signal(
            barrier, inc=1, device_id={"chol": peer_of(k)}, device_id_type=pl.DeviceIdType.MESH
        )
        return 0

    lax.fori_loop(1, n, greet, 0)
    pl.semaphore_wait(barrier, n - 1)

    def at(plane):
        return plane * PLANE + seat

    def piece(ref, c):
        return ref.at[c // CHUNKS, pl.ds(lax.rem(c, CHUNKS) * span, span)]

    def own_orbit(c):
        return remote(piece(orb_ref, c), piece(guest.at[z], c), orb_send.at[0], orb_recv.at[z, c], at(ahead))

    def orbit_on(c):
        there = piece(guest.at[near_out], c)
        return remote(there, there, orb_send.at[1], orb_recv.at[near_out, c], at(ahead))

    def orbit_back(plane, k, c):
        there = piece(guest.at[plane], c)
        return remote(there, there, orb_send.at[k], orb_recv.at[plane, c], at(buddy))

    def await_orbit(plane, c):
        there = piece(guest.at[plane], c)
        remote(there, there, orb_send.at[0], orb_recv.at[plane, c], at(ahead)).wait_recv()

    def start_own(first, last):
        def step(c, _):
            own_orbit(c).start()
            return 0

        lax.fori_loop(first, last, step, 0)

    def pass_on(first, last):
        @pl.when(inner)
        def _():
            def step(c, _):
                await_orbit(near_out, c)
                orbit_on(c).start()
                return 0

            lax.fori_loop(first, last, step, 0)

    def pass_back(first, last):
        @pl.when(inner)
        def _():
            def step(c, _):
                await_orbit(far_in, c)
                orbit_back(far_in, 2, c).start()
                return 0

            lax.fori_loop(first, last, step, 0)

    orb_copy.wait()
    start_own(0, FIRST)

    half_copy.wait()
    green_copy.wait()
    for load in loads:
        load.start()
    gauss_copy.wait()

    def bias(t, acc):
        rows = pl.ds(pl.multiple_of(t * TILE, TILE), TILE)
        left = jnp.swapaxes(green[:, rows, :], 0, 1)
        right = jnp.swapaxes(half[:, rows, :], 0, 1)
        for r in range(TILE):
            acc += lax.dot_general(
                left[r], right[r], (((1,), (1,)), ((), ())), preferred_element_type=jnp.float32
            )
        return acc

    total = lax.fori_loop(0, tiles, bias, jnp.zeros((n * owned, half.shape[0]), jnp.float32))
    for d in range(n):
        part[d] = total[d * owned:(d + 1) * owned]

    def push_part(k, _):
        to = peer_of(k)
        remote(part.at[to], part_in.at[me], part_sem.at[0], part_sem.at[1], to).start()
        return 0

    lax.fori_loop(1, n, push_part, 0)
    start_own(FIRST, SECOND)
    pass_back(0, FIRST)
    part_in[me] = part[me]

    def gathered(ref, sem):
        every = ref.at[pl.ds(0, n - 1)]
        return remote(every, every, sem.at[0], sem.at[1], peer_of(1))

    gathered(part_in, part_sem).wait_recv()
    vbias = jnp.sum(part_in[...], axis=0)
    gauss = gauss_ref[me]
    xbar = jnp.clip(-0.3 * vbias, -1.0, 1.0)
    log_ref[...] = jnp.broadcast_to(
        jnp.sum(gauss * xbar - 0.5 * xbar * xbar, axis=1, keepdims=True), log_ref.shape
    )
    mine = gauss - xbar
    fields_own[...] = mine
    fields_in[me] = mine

    def push_field(k, _):
        to = peer_of(k)
        remote(fields_own, fields_in.at[me], field_sem.at[0], field_sem.at[1], to).start()
        return 0

    lax.fori_loop(1, n, push_field, 0)
    start_own(SECOND, chunks)
    pass_back(FIRST, SECOND)

    gathered(fields_in, field_sem).wait_recv()
    fields = jnp.concatenate(
        [fields_in[plane * PLANE + s] for s in range(PLANE) for plane in range(planes)], axis=0
    ).astype(jnp.bfloat16)

    order = (
        jnp.where(inner, far_in, near_in), jnp.where(inner, far_out, far_in),
        jnp.where(inner, near_out, far_out), z,
    )

    def pot_copy(t, plane, there, source):
        return remote(
            send.at[t, pl.ds(there * line + plane * owned, owned)],
            recv.at[pl.ds(plane * owned, owned), source, t],
            pot_send.at[0], pot_recv.at[plane, source], z * PLANE + there,
        )

    partner = seat + 1 - 2 * lax.rem(seat, 2)
    beside = lax.rem(seat + 2, PLANE)
    diagonal = lax.rem(partner + 2, PLANE)
    others = (beside, diagonal, partner)

    def push(t, plane):
        for s in others:
            pot_copy(t, plane, s, seat).start()

    def await_pots(plane, seats):
        for s in seats:
            every = recv.at[pl.ds(plane * owned, owned), s]
            remote(every, every, pot_send.at[0], pot_recv.at[plane, s], z * PLANE + partner).wait_recv()

    def fill(t):
        loads[t].wait()

        def strip(c, _):
            cols = pl.ds(pl.multiple_of(c * LANES, LANES), LANES)
            block = jnp.swapaxes(chol[t, :, :, cols], 0, 1)
            pots = [
                (jnp.dot(fields, block[r], preferred_element_type=jnp.float32) * 0.3).astype(jnp.bfloat16)
                for r in range(TILE)
            ]
            send[t, :, :, cols] = jnp.swapaxes(jnp.stack(pots, axis=0), 0, 1)
            return 0

        lax.fori_loop(0, width // LANES, strip, 0)
        recv[:, seat, t] = send[t, pl.ds(seat * line, line)]

    def forward_far(first, last):
        def step(c, _):
            await_orbit(far_out, c)

            @pl.when(inner)
            def _():
                orbit_back(far_out, 3, c).start()

            return 0

        lax.fori_loop(first, last, step, 0)

    for t in range(tiles):
        fill(t)
        push(t, order[0])
        if t < tiles - 2:
            pass_back(SECOND + t, SECOND + t + 1)
    held = SECOND + tiles - 2
    for plane in order[1:]:
        for t in range(tiles):
            push(t, plane)

    def lend(s):
        return remote(
            recv.at[pl.ds(buddy * owned, owned), s], lent.at[:, s], lend_send.at[0], lend_recv.at[s], at(buddy)
        )

    pass_on(0, held + 1)
    pass_back(held, held + 2)
    pass_on(held + 1, held + 2)
    pass_back(held + 2, chunks)
    pass_on(held + 2, chunks)
    @pl.when(outer)
    def _():
        lend(seat).start()
        for s in (partner, beside, diagonal):
            await_pots(near_in, (s,))
            lend(s).start()

        def arrived(c, _):
            await_orbit(far_in, c)
            return 0

        lax.fori_loop(0, chunks, arrived, 0)

    def hand_back(plane, w):
        return remote(
            done.at[plane * owned + w], out_ref.at[w, pl.ds(z * PLANE, PLANE)],
            done_send.at[plane], done_recv.at[z], at(plane),
        )

    def rows_done(left, orbit, old):
        moved = jnp.dot(
            left.reshape(-1, width), orbit.reshape(width, nocc), preferred_element_type=jnp.float32
        )
        return (old.astype(jnp.float32) + moved.reshape(old.shape)).astype(jnp.bfloat16)

    here = pl.ds(z * PLANE, PLANE)

    def serve(plane, first, last):
        def step(w, _):
            done[plane * owned + w] = rows_done(
                recv[plane * owned + w], guest[plane, w], guest[plane, w, here]
            )
            hand_back(plane, w).start()
            return 0

        lax.fori_loop(first, last, step, 0)

    forward_far(0, CHUNKS)
    await_pots(far_in, others)
    serve(far_in, 0, owned)
    forward_far(CHUNKS, 2 * CHUNKS)
    await_pots(far_out, others)
    serve(far_out, 0, 2)
    for w in range(2, owned):
        forward_far(CHUNKS * w, CHUNKS * (w + 1))
        serve(far_out, w, w + 1)

    @pl.when(inner)
    def _():
        await_pots(near_out, others)
        serve(near_out, 0, owned)

    await_pots(z, others)

    def advance(w, _):
        out_ref[w, here] = rows_done(recv[z * owned + w], orb_ref[w], orb_ref[w, here])
        return 0

    lax.fori_loop(0, owned, advance, 0)

    @pl.when(inner)
    def _():
        for s in (seat, partner, beside, diagonal):
            lend(s).wait_recv()

            def borrow(w, _):
                row = near_out * PLANE + s
                out_ref[w, row] = rows_done(lent[w, s], orb_ref[w], orb_ref[w, row])
                return 0

            lax.fori_loop(0, owned, borrow, 0)

    gathered(part_in, part_sem).wait_send()
    gathered(fields_in, field_sem).wait_send()
    every = send.at[:, pl.ds(0, (PLANE - 1) * line)]
    remote(every, every, pot_send.at[0], pot_recv.at[z, seat], at(ahead)).wait_send()

    def sent(ref, sem):
        remote(ref, ref, sem, lend_recv.at[0], at(ahead)).wait_send()

    sent(orb_ref, orb_send.at[0])

    @pl.when(inner)
    def _():
        for k in range(1, 4):
            sent(guest.at[0], orb_send.at[k])
        sent(done.at[pl.ds(0, owned)], done_send.at[near_out])

    @pl.when(outer)
    def _():
        sent(lent, lend_send.at[0])

    def settle(plane):
        block = out_ref.at[:, pl.ds(plane * PLANE, PLANE)]
        remote(block, block, done_send.at[plane], done_recv.at[plane], at(plane)).wait_recv()

    for plane in (far_in, far_out):
        sent(done.at[pl.ds(0, owned)], done_send.at[plane])
        settle(plane)

    @pl.when(outer)
    def _():
        settle(near_in)


def on_device(n, chol_full, chol_half, green, gauss, orbitals):
    walkers, local_rows, nocc = green.shape
    owned, width, _ = orbitals.shape
    vectors = chol_half.shape[0]
    tiles = local_rows // TILE
    vmem = pl.BlockSpec(memory_space=pltpu.VMEM)
    hbm = pl.BlockSpec(memory_space=pl.ANY)
    dma = pltpu.SemaphoreType.DMA
    split = (owned, n, tiles, TILE, nocc)
    params = pltpu.CompilerParams(collective_id=0, has_side_effects=True, vmem_limit_bytes=60 << 20)
    shared = [
        pltpu.VMEM((tiles, vectors, TILE, width), jnp.bfloat16),
        pltpu.VMEM((vectors, local_rows, nocc), jnp.bfloat16),
        pltpu.VMEM((walkers, local_rows, nocc), jnp.bfloat16),
    ]
    sums = [
        pltpu.VMEM((n, owned, vectors), jnp.float32),
        pltpu.VMEM((n, owned, vectors), jnp.float32),
        pltpu.VMEM((owned, vectors), jnp.float32),
        pltpu.VMEM((n, owned, vectors), jnp.float32),
        pltpu.VMEM((tiles, walkers, TILE, width), jnp.bfloat16),
    ]
    arrays = (chol_full, chol_half, green, gauss.reshape(n, owned, vectors), orbitals.reshape(split))
    if n == 4 * PLANE and orbitals.size * orbitals.dtype.itemsize <= OWN_LIMIT:
        line = walkers // PLANE
        planes = n // PLANE
        moved, logs = pl.pallas_call(
            functools.partial(line_kernel, n),
            out_shape=(pltpu.VMEM(split, jnp.bfloat16), pltpu.VMEM((owned, LANES), jnp.float32)),
            in_specs=[hbm] * 5,
            out_specs=(vmem, vmem),
            scratch_shapes=[
                *shared,
                pltpu.VMEM((n, owned, vectors), jnp.float32),
                pltpu.VMEM(split, jnp.bfloat16),
                *sums,
                pltpu.VMEM((line, PLANE, tiles, TILE, width), jnp.bfloat16),
                pltpu.VMEM((planes,) + split, jnp.bfloat16),
                pltpu.VMEM((line, PLANE, tiles, TILE, nocc), jnp.bfloat16),
                pltpu.VMEM((owned, PLANE, tiles, TILE, width), jnp.bfloat16),
                dma((tiles,)), dma((4,)), dma((2,)), dma((2,)), dma((1,)), dma((planes, PLANE)),
                dma((4,)), dma((planes, CHUNKS * owned)), dma((1,)), dma((PLANE,)), dma((planes,)), dma((planes,)),
            ],
            compiler_params=params,
        )(*arrays)
    else:
        moved, logs = pl.pallas_call(
            functools.partial(direct_kernel, n),
            out_shape=(
                jax.ShapeDtypeStruct(split, jnp.bfloat16),
                jax.ShapeDtypeStruct((owned, LANES), jnp.float32),
            ),
            in_specs=[hbm, hbm, hbm, vmem, vmem],
            out_specs=(vmem, vmem),
            scratch_shapes=[
                *shared,
                *sums,
                pltpu.VMEM((tiles, owned, n * TILE, width), jnp.bfloat16),
                dma((tiles,)), dma((2,)), dma((n,)), dma((n,)), dma((n,)), dma((n,)),
                dma((tiles, n)), dma((tiles, n)),
            ],
            compiler_params=params,
        )(*arrays)
    return moved.reshape(orbitals.shape), logs[:, 0]


def solution(mesh):
    placed = (
        P(None, "chol", None),
        P(None, "chol", None),
        P("grp", "chol", None),
        P("grp", None),
        P(("grp", "chol"), None, None),
    )
    return jax.shard_map(
        functools.partial(on_device, mesh.shape["chol"]),
        mesh=mesh,
        in_specs=placed,
        out_specs=(P(("grp", "chol"), None, None), P(("grp", "chol"))),
        check_vma=False,
    )
```

```python
import functools

import jax
import jax.numpy as jnp
from jax import lax
from jax.experimental import pallas as pl
from jax.experimental.pallas import tpu as pltpu
from jax.sharding import PartitionSpec as P

TILE = 16
LANES = 128
PLANE = 4
OWN_LIMIT = 2 << 20
CHUNKS = 2
FIRST = 1
SECOND = 2
THIRD = 3


def remote(src, dst, send, recv, peer):
    return pltpu.make_async_remote_copy(
        src_ref=src,
        dst_ref=dst,
        send_sem=send,
        recv_sem=recv,
        device_id={"chol": peer},
        device_id_type=pl.DeviceIdType.MESH,
    )


def direct_kernel(
    n, chol_hbm, half_hbm, green_hbm, gauss_ref, orb_ref,
    out_ref, log_ref,
    chol, half, green, part, part_in, fields_own, fields_in, send, recv,
    load_sem, aux_sem, part_send, part_recv, field_send, field_recv, pot_send, pot_recv,
):
    me = lax.axis_index("chol")
    owned = part.shape[1]
    tiles = chol.shape[0]
    width = chol.shape[3]

    half_copy = pltpu.make_async_copy(half_hbm, half, aux_sem.at[0])
    green_copy = pltpu.make_async_copy(green_hbm, green, aux_sem.at[1])
    half_copy.start()
    green_copy.start()
    loads = [
        pltpu.make_async_copy(chol_hbm.at[:, pl.ds(t * TILE, TILE), :], chol.at[t], load_sem.at[t])
        for t in range(tiles)
    ]
    for load in loads:
        load.start()

    barrier = pltpu.get_barrier_semaphore()

    def greet(k, _):
        pl.semaphore_signal(
            barrier, inc=1, device_id={"chol": lax.rem(me + k, n)}, device_id_type=pl.DeviceIdType.MESH
        )
        return 0

    lax.fori_loop(1, n, greet, 0)

    half_copy.wait()
    green_copy.wait()

    def bias(t, acc):
        rows = pl.ds(pl.multiple_of(t * TILE, TILE), TILE)
        left = jnp.swapaxes(green[:, rows, :], 0, 1)
        right = jnp.swapaxes(half[:, rows, :], 0, 1)
        for r in range(TILE):
            acc += lax.dot_general(
                left[r], right[r], (((1,), (1,)), ((), ())), preferred_element_type=jnp.float32
            )
        return acc

    total = lax.fori_loop(0, tiles, bias, jnp.zeros((n * owned, half.shape[0]), jnp.float32))
    for d in range(n):
        part[d] = total[d * owned:(d + 1) * owned]
    pl.semaphore_wait(barrier, n - 1)

    def peer_of(k):
        return lax.rem(me + k, n)

    def push_part(k, _):
        to = peer_of(k)
        remote(part.at[to], part_in.at[me], part_send.at[to], part_recv.at[me], to).start()
        return 0

    lax.fori_loop(1, n, push_part, 0)
    part_in[me] = part[me]

    def wait_part(k, _):
        peer = peer_of(k)
        copy = remote(part.at[peer], part_in.at[peer], part_send.at[peer], part_recv.at[peer], peer)
        copy.wait_recv()
        return 0

    lax.fori_loop(1, n, wait_part, 0)
    vbias = jnp.sum(part_in[...], axis=0)
    gauss = gauss_ref[me]
    xbar = jnp.clip(-0.3 * vbias, -1.0, 1.0)
    log_ref[...] = jnp.broadcast_to(
        jnp.sum(gauss * xbar - 0.5 * xbar * xbar, axis=1, keepdims=True), log_ref.shape
    )
    mine = gauss - xbar
    fields_own[...] = mine
    fields_in[me] = mine

    def push_field(k, _):
        to = peer_of(k)
        remote(fields_own, fields_in.at[me], field_send.at[to], field_recv.at[me], to).start()
        return 0

    lax.fori_loop(1, n, push_field, 0)

    def wait_field(k, _):
        peer = peer_of(k)
        remote(fields_own, fields_in.at[peer], field_send.at[peer], field_recv.at[peer], peer).wait_recv()
        return 0

    lax.fori_loop(1, n, wait_field, 0)
    fields = jnp.concatenate([fields_in[d] for d in range(n)], axis=0).astype(jnp.bfloat16)

    def walkers_of(d):
        return pl.ds(d * owned, owned)

    def rows_of(d):
        return pl.ds(pl.multiple_of(d * TILE, TILE), TILE)

    for t in range(tiles):
        loads[t].wait()

        def strip(c, _):
            cols = pl.ds(pl.multiple_of(c * LANES, LANES), LANES)
            block = jnp.swapaxes(chol[t, :, :, cols], 0, 1)
            pots = [
                (jnp.dot(fields, block[r], preferred_element_type=jnp.float32) * 0.3).astype(jnp.bfloat16)
                for r in range(TILE)
            ]
            send[t, :, :, cols] = jnp.swapaxes(jnp.stack(pots, axis=0), 0, 1)
            return 0

        lax.fori_loop(0, width // LANES, strip, 0)

        def push_pot(k, _):
            to = peer_of(k)
            remote(
                send.at[t, walkers_of(to)], recv.at[t, :, rows_of(me), :],
                pot_send.at[t, to], pot_recv.at[t, me], to,
            ).start()
            return 0

        lax.fori_loop(1, n, push_pot, 0)
        recv[t, :, rows_of(me), :] = send[t, walkers_of(me)]

    for t in range(tiles):

        def wait_pot(k, _):
            peer = peer_of(k)
            remote(
                send.at[t, walkers_of(peer)], recv.at[t, :, rows_of(peer), :],
                pot_send.at[t, peer], pot_recv.at[t, peer], peer,
            ).wait_recv()
            return 0

        lax.fori_loop(1, n, wait_pot, 0)

        def advance(w, _):
            orbit = orb_ref[w].reshape(width, orb_ref.shape[-1])
            for first in range(0, n, 16):
                span = min(16, n - first)
                moved = jnp.dot(
                    recv[t, w, first * TILE:(first + span) * TILE, :], orbit,
                    preferred_element_type=jnp.float32,
                ).reshape(span, TILE, orbit.shape[-1])
                old = orb_ref[w, first:first + span, t].astype(jnp.float32)
                out_ref[w, first:first + span, t] = (old + moved).astype(jnp.bfloat16)
            return 0

        lax.fori_loop(0, owned, advance, 0)

    def drain(k, _):
        peer = peer_of(k)
        remote(part.at[peer], part_in.at[peer], part_send.at[peer], part_recv.at[peer], peer).wait_send()
        remote(fields_own, fields_in.at[peer], field_send.at[peer], field_recv.at[peer], peer).wait_send()
        for t in range(tiles):
            remote(
                send.at[t, walkers_of(peer)], recv.at[t, :, rows_of(peer), :],
                pot_send.at[t, peer], pot_recv.at[t, peer], peer,
            ).wait_send()
        return 0

    lax.fori_loop(1, n, drain, 0)


def line_kernel(
    n, chol_hbm, half_hbm, green_hbm, gauss_hbm, orb_hbm,
    out_ref, log_ref,
    chol, half, green, gauss_ref, orb_ref, part, part_in, partial, partial_in, bias_ref, log_all, fields_ref,
    send, recv, guest, done, lent,
    load_sem, aux_sem, part_sem, sum_sem, field_sem, pot_send, pot_recv, orb_send, orb_recv,
    lend_send, lend_recv, done_send, done_recv,
):
    me = lax.axis_index("chol")
    owned = orb_ref.shape[0]
    tiles = chol.shape[0]
    width = chol.shape[3]
    nocc = orb_ref.shape[-1]
    planes = n // PLANE
    line = planes * owned
    chunks = CHUNKS * owned
    span = n // CHUNKS

    z = me // PLANE
    seat = lax.rem(me, PLANE)
    side = z // 2
    far = 1 - side
    near_in, near_out = 1 + side, 3 * side
    far_in, far_out = 1 + far, 3 * far
    ahead = z + 1 - 2 * side
    buddy = near_in + near_out - z
    inner = z == near_in
    outer = z == near_out

    half_copy = pltpu.make_async_copy(half_hbm, half, aux_sem.at[0])
    green_copy = pltpu.make_async_copy(green_hbm, green, aux_sem.at[1])
    gauss_copy = pltpu.make_async_copy(gauss_hbm, gauss_ref, aux_sem.at[2])
    orb_copy = pltpu.make_async_copy(orb_hbm, orb_ref, aux_sem.at[3])
    for copy in (orb_copy, green_copy, half_copy, gauss_copy):
        copy.start()
    loads = [
        pltpu.make_async_copy(chol_hbm.at[:, pl.ds(t * TILE, TILE), :], chol.at[t], load_sem.at[t])
        for t in range(tiles)
    ]
    barrier = pltpu.get_barrier_semaphore()

    partner = seat + 1 - 2 * lax.rem(seat, 2)
    beside = lax.rem(seat + 2, PLANE)
    diagonal = lax.rem(partner + 2, PLANE)
    others = (beside, diagonal, partner)

    def greet(peer):
        pl.semaphore_signal(barrier, inc=1, device_id={"chol": peer}, device_id_type=pl.DeviceIdType.MESH)

    greet(ahead * PLANE + seat)
    for s in others:
        greet(z * PLANE + s)

    @pl.when(inner)
    def _():
        greet(buddy * PLANE + seat)
        pl.semaphore_wait(barrier, PLANE + 1)

    @pl.when(outer)
    def _():
        pl.semaphore_wait(barrier, PLANE)

    def at(plane):
        return plane * PLANE + seat

    def piece(ref, c):
        return ref.at[c // CHUNKS, pl.ds(lax.rem(c, CHUNKS) * span, span)]

    def own_orbit(c):
        return remote(piece(orb_ref, c), piece(guest.at[z], c), orb_send.at[0], orb_recv.at[z, c], at(ahead))

    def orbit_on(c):
        there = piece(guest.at[near_out], c)
        return remote(there, there, orb_send.at[1], orb_recv.at[near_out, c], at(ahead))

    def orbit_back(plane, k, c):
        there = piece(guest.at[plane], c)
        return remote(there, there, orb_send.at[k], orb_recv.at[plane, c], at(buddy))

    def await_orbit(plane, c):
        there = piece(guest.at[plane], c)
        remote(there, there, orb_send.at[0], orb_recv.at[plane, c], at(ahead)).wait_recv()

    def start_own(first, last):
        def step(c, _):
            own_orbit(c).start()
            return 0

        lax.fori_loop(first, last, step, 0)

    def pass_on(first, last):
        @pl.when(inner)
        def _():
            def step(c, _):
                await_orbit(near_out, c)
                orbit_on(c).start()
                return 0

            lax.fori_loop(first, last, step, 0)

    def pass_back(first, last):
        @pl.when(inner)
        def _():
            def step(c, _):
                await_orbit(far_in, c)
                orbit_back(far_in, 2, c).start()
                return 0

            lax.fori_loop(first, last, step, 0)

    orb_copy.wait()
    start_own(0, FIRST)

    half_copy.wait()
    green_copy.wait()
    for load in loads:
        load.start()
    gauss_copy.wait()

    def bias(t, acc):
        rows = pl.ds(pl.multiple_of(t * TILE, TILE), TILE)
        left = jnp.swapaxes(green[:, rows, :], 0, 1)
        right = jnp.swapaxes(half[:, rows, :], 0, 1)
        for r in range(TILE):
            acc += lax.dot_general(
                left[r], right[r], (((1,), (1,)), ((), ())), preferred_element_type=jnp.float32
            )
        return acc

    total = lax.fori_loop(0, tiles, bias, jnp.zeros((n * owned, half.shape[0]), jnp.float32))
    for d in range(n):
        plane, s = divmod(d, PLANE)
        part[s, plane * owned:(plane + 1) * owned] = total[d * owned:(d + 1) * owned]

    def part_copy(there, source):
        return remote(part.at[there], part_in.at[source], part_sem.at[0], part_sem.at[1], z * PLANE + there)

    def field_copy(there):
        mine = fields_ref.at[seat]
        return remote(mine, mine, field_sem.at[0], field_sem.at[1], z * PLANE + there)

    def gathered(ref, sem):
        every = ref.at[pl.ds(0, PLANE - 1)]
        return remote(every, every, sem.at[0], sem.at[1], at(ahead))

    def sum_copy(k, to):
        return remote(partial.at[k], partial_in.at[k], sum_sem.at[0, k], sum_sem.at[1, k], to)

    def total_copy():
        return remote(bias_ref, bias_ref, sum_sem.at[0, 2], sum_sem.at[1, 2], at(buddy))

    for s in others:
        part_copy(s, seat).start()
    part_in[seat] = part[seat]

    @pl.when(inner)
    def _():
        start_own(FIRST, SECOND)

    pass_back(0, FIRST)
    gathered(part_in, part_sem).wait_recv()
    partial[0] = jnp.sum(part_in[...], axis=0)

    @pl.when(outer)
    def _():
        sum_copy(0, at(ahead)).start()
        start_own(FIRST, chunks)
        total_copy().wait_recv()

    @pl.when(inner)
    def _():
        sum_copy(0, at(ahead)).wait_recv()
        partial[1] = partial[0] + partial_in[0]
        sum_copy(1, at(ahead)).start()
        start_own(SECOND, THIRD)
        sum_copy(1, at(ahead)).wait_recv()
        bias_ref[...] = partial[1] + partial_in[1]
        total_copy().start()
        start_own(THIRD, chunks)

    pass_back(FIRST, SECOND)
    vbias = bias_ref[...]
    gauss = jnp.concatenate([gauss_ref[plane * PLANE + seat] for plane in range(planes)], axis=0)
    xbar = jnp.clip(-0.3 * vbias, -1.0, 1.0)
    logs = jnp.sum(gauss * xbar - 0.5 * xbar * xbar, axis=1, keepdims=True)
    log_all[...] = jnp.broadcast_to(logs, (line, LANES)).reshape(log_all.shape)
    log_ref[...] = log_all[z]
    fields_ref[seat] = (gauss - xbar).astype(jnp.bfloat16)

    for s in others:
        field_copy(s).start()
    gathered(fields_ref, field_sem).wait_recv()
    fields = fields_ref[...].reshape(n * owned, fields_ref.shape[-1])

    order = (
        jnp.where(inner, far_in, near_in), jnp.where(inner, far_out, far_in),
        jnp.where(inner, near_out, far_out), z,
    )

    def pot_copy(t, plane, there, source):
        return remote(
            send.at[t, pl.ds(there * line + plane * owned, owned)],
            recv.at[pl.ds(plane * owned, owned), source, t],
            pot_send.at[0], pot_recv.at[plane, source], z * PLANE + there,
        )

    def push(t, plane):
        for s in others:
            pot_copy(t, plane, s, seat).start()

    def await_pots(plane, seats):
        for s in seats:
            every = recv.at[pl.ds(plane * owned, owned), s]
            remote(every, every, pot_send.at[0], pot_recv.at[plane, s], z * PLANE + partner).wait_recv()

    def fill(t):
        loads[t].wait()

        def strip(c, _):
            cols = pl.ds(pl.multiple_of(c * LANES, LANES), LANES)
            block = jnp.swapaxes(chol[t, :, :, cols], 0, 1)
            pots = [
                (jnp.dot(fields, block[r], preferred_element_type=jnp.float32) * 0.3).astype(jnp.bfloat16)
                for r in range(TILE)
            ]
            send[t, :, :, cols] = jnp.swapaxes(jnp.stack(pots, axis=0), 0, 1)
            return 0

        lax.fori_loop(0, width // LANES, strip, 0)
        recv[:, seat, t] = send[t, pl.ds(seat * line, line)]

    def forward_far(first, last):
        def step(c, _):
            await_orbit(far_out, c)

            @pl.when(inner)
            def _():
                orbit_back(far_out, 3, c).start()

            return 0

        lax.fori_loop(first, last, step, 0)

    for t in range(tiles):
        fill(t)
        push(t, order[0])
        if t < tiles - 2:
            pass_back(SECOND + t, SECOND + t + 1)
    held = SECOND + tiles - 2
    for plane in order[1:]:
        for t in range(tiles):
            push(t, plane)

    def lend(s):
        return remote(
            recv.at[pl.ds(buddy * owned, owned), s], lent.at[:, s], lend_send.at[0], lend_recv.at[s], at(buddy)
        )

    pass_on(0, held + 1)
    pass_back(held, held + 2)
    pass_on(held + 1, held + 2)
    pass_back(held + 2, chunks)
    pass_on(held + 2, chunks)
    @pl.when(outer)
    def _():
        lend(seat).start()
        for s in (partner, beside, diagonal):
            await_pots(near_in, (s,))
            lend(s).start()

        def arrived(c, _):
            await_orbit(far_in, c)
            return 0

        lax.fori_loop(0, chunks, arrived, 0)

    def hand_back(plane, w):
        return remote(
            done.at[plane * owned + w], out_ref.at[w, pl.ds(z * PLANE, PLANE)],
            done_send.at[plane], done_recv.at[z], at(plane),
        )

    def rows_done(left, orbit, old):
        moved = jnp.dot(
            left.reshape(-1, width), orbit.reshape(width, nocc), preferred_element_type=jnp.float32
        )
        return (old.astype(jnp.float32) + moved.reshape(old.shape)).astype(jnp.bfloat16)

    here = pl.ds(z * PLANE, PLANE)

    def serve(plane, first, last):
        def step(w, _):
            done[plane * owned + w] = rows_done(
                recv[plane * owned + w], guest[plane, w], guest[plane, w, here]
            )
            hand_back(plane, w).start()
            return 0

        lax.fori_loop(first, last, step, 0)

    forward_far(0, CHUNKS)
    await_pots(far_in, others)
    serve(far_in, 0, owned)
    forward_far(CHUNKS, 2 * CHUNKS)
    await_pots(far_out, others)
    serve(far_out, 0, 2)
    for w in range(2, owned):
        forward_far(CHUNKS * w, CHUNKS * (w + 1))
        serve(far_out, w, w + 1)

    @pl.when(inner)
    def _():
        await_pots(near_out, others)
        serve(near_out, 0, owned)

    await_pots(z, others)

    def advance(w, _):
        out_ref[w, here] = rows_done(recv[z * owned + w], orb_ref[w], orb_ref[w, here])
        return 0

    lax.fori_loop(0, owned, advance, 0)

    @pl.when(inner)
    def _():
        for s in (seat, partner, beside, diagonal):
            lend(s).wait_recv()

            def borrow(w, _):
                row = near_out * PLANE + s
                out_ref[w, row] = rows_done(lent[w, s], orb_ref[w], orb_ref[w, row])
                return 0

            lax.fori_loop(0, owned, borrow, 0)

    gathered(part_in, part_sem).wait_send()
    gathered(fields_ref, field_sem).wait_send()
    every = send.at[:, pl.ds(0, (PLANE - 1) * line)]
    remote(every, every, pot_send.at[0], pot_recv.at[z, seat], at(ahead)).wait_send()

    def sent(ref, sem):
        remote(ref, ref, sem, lend_recv.at[0], at(ahead)).wait_send()

    @pl.when(outer)
    def _():
        sum_copy(0, at(ahead)).wait_send()

    @pl.when(inner)
    def _():
        sum_copy(1, at(ahead)).wait_send()
        total_copy().wait_send()

    sent(orb_ref, orb_send.at[0])

    @pl.when(inner)
    def _():
        for k in range(1, 4):
            sent(guest.at[0], orb_send.at[k])
        sent(done.at[pl.ds(0, owned)], done_send.at[near_out])

    @pl.when(outer)
    def _():
        sent(lent, lend_send.at[0])

    def settle(plane):
        block = out_ref.at[:, pl.ds(plane * PLANE, PLANE)]
        remote(block, block, done_send.at[plane], done_recv.at[plane], at(plane)).wait_recv()

    for plane in (far_in, far_out):
        sent(done.at[pl.ds(0, owned)], done_send.at[plane])
        settle(plane)

    @pl.when(outer)
    def _():
        settle(near_in)


def on_device(n, chol_full, chol_half, green, gauss, orbitals):
    walkers, local_rows, nocc = green.shape
    owned, width, _ = orbitals.shape
    vectors = chol_half.shape[0]
    tiles = local_rows // TILE
    vmem = pl.BlockSpec(memory_space=pltpu.VMEM)
    hbm = pl.BlockSpec(memory_space=pl.ANY)
    dma = pltpu.SemaphoreType.DMA
    split = (owned, n, tiles, TILE, nocc)
    params = pltpu.CompilerParams(collective_id=0, has_side_effects=True, vmem_limit_bytes=60 << 20)
    shared = [
        pltpu.VMEM((tiles, vectors, TILE, width), jnp.bfloat16),
        pltpu.VMEM((vectors, local_rows, nocc), jnp.bfloat16),
        pltpu.VMEM((walkers, local_rows, nocc), jnp.bfloat16),
    ]
    arrays = (chol_full, chol_half, green, gauss.reshape(n, owned, vectors), orbitals.reshape(split))
    if n == 4 * PLANE and orbitals.size * orbitals.dtype.itemsize <= OWN_LIMIT:
        line = walkers // PLANE
        planes = n // PLANE
        moved, logs = pl.pallas_call(
            functools.partial(line_kernel, n),
            out_shape=(pltpu.VMEM(split, jnp.bfloat16), pltpu.VMEM((owned, LANES), jnp.float32)),
            in_specs=[hbm] * 5,
            out_specs=(vmem, vmem),
            scratch_shapes=[
                *shared,
                pltpu.VMEM((n, owned, vectors), jnp.float32),
                pltpu.VMEM(split, jnp.bfloat16),
                pltpu.VMEM((PLANE, line, vectors), jnp.float32),
                pltpu.VMEM((PLANE, line, vectors), jnp.float32),
                pltpu.VMEM((2, line, vectors), jnp.float32),
                pltpu.VMEM((2, line, vectors), jnp.float32),
                pltpu.VMEM((line, vectors), jnp.float32),
                pltpu.VMEM((planes, owned, LANES), jnp.float32),
                pltpu.VMEM((PLANE, line, vectors), jnp.bfloat16),
                pltpu.VMEM((tiles, walkers, TILE, width), jnp.bfloat16),
                pltpu.VMEM((line, PLANE, tiles, TILE, width), jnp.bfloat16),
                pltpu.VMEM((planes,) + split, jnp.bfloat16),
                pltpu.VMEM((line, PLANE, tiles, TILE, nocc), jnp.bfloat16),
                pltpu.VMEM((owned, PLANE, tiles, TILE, width), jnp.bfloat16),
                dma((tiles,)), dma((4,)), dma((2,)), dma((2, 3)), dma((2,)), dma((1,)), dma((planes, PLANE)),
                dma((4,)), dma((planes, CHUNKS * owned)), dma((1,)), dma((PLANE,)), dma((planes,)), dma((planes,)),
            ],
            compiler_params=params,
        )(*arrays)
    else:
        moved, logs = pl.pallas_call(
            functools.partial(direct_kernel, n),
            out_shape=(
                jax.ShapeDtypeStruct(split, jnp.bfloat16),
                jax.ShapeDtypeStruct((owned, LANES), jnp.float32),
            ),
            in_specs=[hbm, hbm, hbm, vmem, vmem],
            out_specs=(vmem, vmem),
            scratch_shapes=[
                *shared,
                pltpu.VMEM((n, owned, vectors), jnp.float32),
                pltpu.VMEM((n, owned, vectors), jnp.float32),
                pltpu.VMEM((owned, vectors), jnp.float32),
                pltpu.VMEM((n, owned, vectors), jnp.float32),
                pltpu.VMEM((tiles, walkers, TILE, width), jnp.bfloat16),
                pltpu.VMEM((tiles, owned, n * TILE, width), jnp.bfloat16),
                dma((tiles,)), dma((2,)), dma((n,)), dma((n,)), dma((n,)), dma((n,)),
                dma((tiles, n)), dma((tiles, n)),
            ],
            compiler_params=params,
        )(*arrays)
    return moved.reshape(orbitals.shape), logs[:, 0]


def solution(mesh):
    placed = (
        P(None, "chol", None),
        P(None, "chol", None),
        P("grp", "chol", None),
        P("grp", None),
        P(("grp", "chol"), None, None),
    )
    return jax.shard_map(
        functools.partial(on_device, mesh.shape["chol"]),
        mesh=mesh,
        in_specs=placed,
        out_specs=(P(("grp", "chol"), None, None), P(("grp", "chol"))),
        check_vma=False,
    )
```

```python
import functools

import jax
import jax.numpy as jnp
from jax import lax
from jax.experimental import pallas as pl
from jax.experimental.pallas import tpu as pltpu
from jax.sharding import PartitionSpec as P

TILE = 16
LANES = 128
PLANE = 4
OWN_LIMIT = 2 << 20
CHUNKS = 2
FIRST = 1
SECOND = 2
THIRD = 3


def remote(src, dst, send, recv, peer):
    return pltpu.make_async_remote_copy(
        src_ref=src,
        dst_ref=dst,
        send_sem=send,
        recv_sem=recv,
        device_id={"chol": peer},
        device_id_type=pl.DeviceIdType.MESH,
    )


def direct_kernel(
    n, chol_hbm, half_hbm, green_hbm, gauss_ref, orb_ref,
    out_ref, log_ref,
    chol, half, green, part, part_in, fields_own, fields_in, send, recv,
    load_sem, aux_sem, part_send, part_recv, field_send, field_recv, pot_send, pot_recv,
):
    me = lax.axis_index("chol")
    owned = part.shape[1]
    tiles = chol.shape[0]
    width = chol.shape[3]

    half_copy = pltpu.make_async_copy(half_hbm, half, aux_sem.at[0])
    green_copy = pltpu.make_async_copy(green_hbm, green, aux_sem.at[1])
    half_copy.start()
    green_copy.start()
    loads = [
        pltpu.make_async_copy(chol_hbm.at[:, pl.ds(t * TILE, TILE), :], chol.at[t], load_sem.at[t])
        for t in range(tiles)
    ]
    for load in loads:
        load.start()

    barrier = pltpu.get_barrier_semaphore()

    def greet(k, _):
        pl.semaphore_signal(
            barrier, inc=1, device_id={"chol": lax.rem(me + k, n)}, device_id_type=pl.DeviceIdType.MESH
        )
        return 0

    lax.fori_loop(1, n, greet, 0)

    half_copy.wait()
    green_copy.wait()

    def bias(t, acc):
        rows = pl.ds(pl.multiple_of(t * TILE, TILE), TILE)
        left = jnp.swapaxes(green[:, rows, :], 0, 1)
        right = jnp.swapaxes(half[:, rows, :], 0, 1)
        for r in range(TILE):
            acc += lax.dot_general(
                left[r], right[r], (((1,), (1,)), ((), ())), preferred_element_type=jnp.float32
            )
        return acc

    total = lax.fori_loop(0, tiles, bias, jnp.zeros((n * owned, half.shape[0]), jnp.float32))
    for d in range(n):
        part[d] = total[d * owned:(d + 1) * owned]
    pl.semaphore_wait(barrier, n - 1)

    def peer_of(k):
        return lax.rem(me + k, n)

    def push_part(k, _):
        to = peer_of(k)
        remote(part.at[to], part_in.at[me], part_send.at[to], part_recv.at[me], to).start()
        return 0

    lax.fori_loop(1, n, push_part, 0)
    part_in[me] = part[me]

    def wait_part(k, _):
        peer = peer_of(k)
        copy = remote(part.at[peer], part_in.at[peer], part_send.at[peer], part_recv.at[peer], peer)
        copy.wait_recv()
        return 0

    lax.fori_loop(1, n, wait_part, 0)
    vbias = jnp.sum(part_in[...], axis=0)
    gauss = gauss_ref[me]
    xbar = jnp.clip(-0.3 * vbias, -1.0, 1.0)
    log_ref[...] = jnp.broadcast_to(
        jnp.sum(gauss * xbar - 0.5 * xbar * xbar, axis=1, keepdims=True), log_ref.shape
    )
    mine = gauss - xbar
    fields_own[...] = mine
    fields_in[me] = mine

    def push_field(k, _):
        to = peer_of(k)
        remote(fields_own, fields_in.at[me], field_send.at[to], field_recv.at[me], to).start()
        return 0

    lax.fori_loop(1, n, push_field, 0)

    def wait_field(k, _):
        peer = peer_of(k)
        remote(fields_own, fields_in.at[peer], field_send.at[peer], field_recv.at[peer], peer).wait_recv()
        return 0

    lax.fori_loop(1, n, wait_field, 0)
    fields = jnp.concatenate([fields_in[d] for d in range(n)], axis=0).astype(jnp.bfloat16)

    def walkers_of(d):
        return pl.ds(d * owned, owned)

    def rows_of(d):
        return pl.ds(pl.multiple_of(d * TILE, TILE), TILE)

    for t in range(tiles):
        loads[t].wait()

        def strip(c, _):
            cols = pl.ds(pl.multiple_of(c * LANES, LANES), LANES)
            block = jnp.swapaxes(chol[t, :, :, cols], 0, 1)
            pots = [
                (jnp.dot(fields, block[r], preferred_element_type=jnp.float32) * 0.3).astype(jnp.bfloat16)
                for r in range(TILE)
            ]
            send[t, :, :, cols] = jnp.swapaxes(jnp.stack(pots, axis=0), 0, 1)
            return 0

        lax.fori_loop(0, width // LANES, strip, 0)

        def push_pot(k, _):
            to = peer_of(k)
            remote(
                send.at[t, walkers_of(to)], recv.at[t, :, rows_of(me), :],
                pot_send.at[t, to], pot_recv.at[t, me], to,
            ).start()
            return 0

        lax.fori_loop(1, n, push_pot, 0)
        recv[t, :, rows_of(me), :] = send[t, walkers_of(me)]

    for t in range(tiles):

        def wait_pot(k, _):
            peer = peer_of(k)
            remote(
                send.at[t, walkers_of(peer)], recv.at[t, :, rows_of(peer), :],
                pot_send.at[t, peer], pot_recv.at[t, peer], peer,
            ).wait_recv()
            return 0

        lax.fori_loop(1, n, wait_pot, 0)

        def advance(w, _):
            orbit = orb_ref[w].reshape(width, orb_ref.shape[-1])
            for first in range(0, n, 16):
                span = min(16, n - first)
                moved = jnp.dot(
                    recv[t, w, first * TILE:(first + span) * TILE, :], orbit,
                    preferred_element_type=jnp.float32,
                ).reshape(span, TILE, orbit.shape[-1])
                old = orb_ref[w, first:first + span, t].astype(jnp.float32)
                out_ref[w, first:first + span, t] = (old + moved).astype(jnp.bfloat16)
            return 0

        lax.fori_loop(0, owned, advance, 0)

    def drain(k, _):
        peer = peer_of(k)
        remote(part.at[peer], part_in.at[peer], part_send.at[peer], part_recv.at[peer], peer).wait_send()
        remote(fields_own, fields_in.at[peer], field_send.at[peer], field_recv.at[peer], peer).wait_send()
        for t in range(tiles):
            remote(
                send.at[t, walkers_of(peer)], recv.at[t, :, rows_of(peer), :],
                pot_send.at[t, peer], pot_recv.at[t, peer], peer,
            ).wait_send()
        return 0

    lax.fori_loop(1, n, drain, 0)


def line_kernel(
    n, chol_hbm, half_hbm, green_hbm, gauss_hbm, orb_hbm,
    out_ref, log_ref,
    chol, half, green, gauss_ref, orb_ref, part, part_in, partial, partial_in, bias_ref, log_all, fields_ref,
    send, recv, guest, done, lent,
    load_sem, aux_sem, part_sem, sum_sem, field_sem, pot_send, pot_recv, orb_send, orb_recv,
    lend_sem, done_sem,
):
    me = lax.axis_index("chol")
    owned = orb_ref.shape[0]
    tiles = chol.shape[0]
    width = chol.shape[3]
    nocc = orb_ref.shape[-1]
    planes = n // PLANE
    line = planes * owned
    chunks = CHUNKS * owned
    span = n // CHUNKS

    z = me // PLANE
    seat = lax.rem(me, PLANE)
    side = z // 2
    far = 1 - side
    near_in, near_out = 1 + side, 3 * side
    far_in, far_out = 1 + far, 3 * far
    ahead = z + 1 - 2 * side
    buddy = near_in + near_out - z
    inner = z == near_in
    outer = z == near_out

    half_copy = pltpu.make_async_copy(half_hbm, half, aux_sem.at[0])
    green_copy = pltpu.make_async_copy(green_hbm, green, aux_sem.at[1])
    gauss_copy = pltpu.make_async_copy(gauss_hbm, gauss_ref, aux_sem.at[2])
    orb_copy = pltpu.make_async_copy(orb_hbm, orb_ref, aux_sem.at[3])
    for copy in (green_copy, half_copy, gauss_copy):
        copy.start()
    loads = [
        pltpu.make_async_copy(chol_hbm.at[:, pl.ds(t * TILE, TILE), :], chol.at[t], load_sem.at[0])
        for t in range(tiles)
    ]
    barrier = pltpu.get_barrier_semaphore()

    partner = seat + 1 - 2 * lax.rem(seat, 2)
    beside = lax.rem(seat + 2, PLANE)
    diagonal = lax.rem(partner + 2, PLANE)
    others = (beside, diagonal, partner)

    def greet(peer):
        pl.semaphore_signal(barrier, inc=1, device_id={"chol": peer}, device_id_type=pl.DeviceIdType.MESH)

    greet(ahead * PLANE + seat)
    for s in others:
        greet(z * PLANE + s)

    @pl.when(inner)
    def _():
        greet(buddy * PLANE + seat)
        pl.semaphore_wait(barrier, PLANE + 1)

    @pl.when(outer)
    def _():
        pl.semaphore_wait(barrier, PLANE)

    def at(plane):
        return plane * PLANE + seat

    def piece(ref, c):
        return ref.at[c // CHUNKS, pl.ds(lax.rem(c, CHUNKS) * span, span)]

    def landed(plane, to, c):
        return orb_recv.at[lax.rem(plane - to + planes, planes) - 1, c]

    def own_orbit(c):
        return remote(piece(orb_hbm, c), piece(guest.at[z], c), orb_send.at[0], landed(z, ahead, c), at(ahead))

    def orbit_copy(plane, to, c):
        there = piece(guest.at[plane], c)
        return remote(there, there, orb_send.at[0], landed(plane, to, c), at(to))

    def orbit_on(c):
        return orbit_copy(near_out, ahead, c)

    def orbit_back(plane, c):
        return orbit_copy(plane, buddy, c)

    def await_orbit(plane, c):
        there = piece(guest.at[plane], c)
        remote(there, there, orb_send.at[0], landed(plane, z, c), at(ahead)).wait_recv()

    def start_own(first, last):
        def step(c, _):
            own_orbit(c).start()
            return 0

        lax.fori_loop(first, last, step, 0)

    def pass_on(first, last):
        @pl.when(inner)
        def _():
            def step(c, _):
                await_orbit(near_out, c)
                orbit_on(c).start()
                return 0

            lax.fori_loop(first, last, step, 0)

    def pass_back(first, last):
        @pl.when(inner)
        def _():
            def step(c, _):
                await_orbit(far_in, c)
                orbit_back(far_in, c).start()
                return 0

            lax.fori_loop(first, last, step, 0)

    start_own(0, FIRST)

    half_copy.wait()
    green_copy.wait()
    for copy in (*loads, orb_copy):
        copy.start()
    gauss_copy.wait()

    def bias(t, acc):
        rows = pl.ds(pl.multiple_of(t * TILE, TILE), TILE)
        left = jnp.swapaxes(green[:, rows, :], 0, 1)
        right = jnp.swapaxes(half[:, rows, :], 0, 1)
        for r in range(TILE):
            acc += lax.dot_general(
                left[r], right[r], (((1,), (1,)), ((), ())), preferred_element_type=jnp.float32
            )
        return acc

    total = lax.fori_loop(0, tiles, bias, jnp.zeros((n * owned, half.shape[0]), jnp.float32))
    for d in range(n):
        plane, s = divmod(d, PLANE)
        part[s, plane * owned:(plane + 1) * owned] = total[d * owned:(d + 1) * owned]

    def part_copy(there, source):
        return remote(part.at[there], part_in.at[source], part_sem.at[0], part_sem.at[1], z * PLANE + there)

    def field_copy(there):
        mine = fields_ref.at[seat]
        return remote(mine, mine, field_sem.at[0], field_sem.at[1], z * PLANE + there)

    def gathered(ref, sem):
        every = ref.at[pl.ds(0, PLANE - 1)]
        return remote(every, every, sem.at[0], sem.at[1], at(ahead))

    def sum_copy(k, to):
        return remote(partial.at[k], partial_in.at[k], sum_sem.at[0, 0], sum_sem.at[1, k], to)

    def total_copy():
        return remote(bias_ref, bias_ref, sum_sem.at[0, 1], sum_sem.at[1, 0], at(buddy))

    for s in others:
        part_copy(s, seat).start()
    part_in[seat] = part[seat]

    @pl.when(inner)
    def _():
        start_own(FIRST, SECOND)

    pass_back(0, FIRST)
    gathered(part_in, part_sem).wait_recv()
    partial[0] = jnp.sum(part_in[...], axis=0)

    @pl.when(outer)
    def _():
        sum_copy(0, at(ahead)).start()
        start_own(FIRST, chunks)
        total_copy().wait_recv()

    @pl.when(inner)
    def _():
        sum_copy(0, at(ahead)).wait_recv()
        partial[1] = partial[0] + partial_in[0]
        sum_copy(1, at(ahead)).start()
        start_own(SECOND, THIRD)
        sum_copy(1, at(ahead)).wait_recv()
        bias_ref[...] = partial[1] + partial_in[1]
        total_copy().start()
        start_own(THIRD, chunks)

    pass_back(FIRST, SECOND)
    vbias = bias_ref[...]
    gauss = jnp.concatenate([gauss_ref[plane * PLANE + seat] for plane in range(planes)], axis=0)
    xbar = jnp.clip(-0.3 * vbias, -1.0, 1.0)
    logs = jnp.sum(gauss * xbar - 0.5 * xbar * xbar, axis=1, keepdims=True)
    log_all[...] = jnp.broadcast_to(logs, (line, LANES)).reshape(log_all.shape)
    log_ref[...] = log_all[z]
    fields_ref[seat] = (gauss - xbar).astype(jnp.bfloat16)

    for s in others:
        field_copy(s).start()
    gathered(fields_ref, field_sem).wait_recv()
    pltpu.make_async_copy(chol, chol, load_sem.at[0]).wait()
    fields = fields_ref[...].reshape(n * owned, fields_ref.shape[-1])

    order = (
        jnp.where(inner, far_in, near_in), jnp.where(inner, far_out, far_in),
        jnp.where(inner, near_out, far_out), z,
    )

    def pot_copy(t, plane, there, source):
        return remote(
            send.at[t, pl.ds(there * line + plane * owned, owned)],
            recv.at[pl.ds(plane * owned, owned), source, t],
            pot_send.at[0], pot_recv.at[plane], z * PLANE + there,
        )

    def push(t, plane):
        for s in others:
            pot_copy(t, plane, s, seat).start()

    def await_pots(plane):
        every = recv.at[pl.ds(plane * owned, owned), pl.ds(0, PLANE - 1)]
        remote(every, every, pot_send.at[0], pot_recv.at[plane], z * PLANE + partner).wait_recv()

    def fill(t):
        def strip(c, _):
            cols = pl.ds(pl.multiple_of(c * LANES, LANES), LANES)
            block = jnp.swapaxes(chol[t, :, :, cols], 0, 1)
            pots = [
                (jnp.dot(fields, block[r], preferred_element_type=jnp.float32) * 0.3).astype(jnp.bfloat16)
                for r in range(TILE)
            ]
            send[t, :, :, cols] = jnp.swapaxes(jnp.stack(pots, axis=0), 0, 1)
            return 0

        lax.fori_loop(0, width // LANES, strip, 0)
        recv[:, seat, t] = send[t, pl.ds(seat * line, line)]

    def forward_far(first, last):
        def step(c, _):
            await_orbit(far_out, c)

            @pl.when(inner)
            def _():
                orbit_back(far_out, c).start()

            return 0

        lax.fori_loop(first, last, step, 0)

    for t in range(tiles):
        fill(t)
        push(t, order[0])
        if t < tiles - 2:
            pass_back(SECOND + t, SECOND + t + 1)
    held = SECOND + tiles - 2
    for plane in order[1:]:
        for t in range(tiles):
            push(t, plane)

    def lend():
        return remote(recv.at[pl.ds(buddy * owned, owned)], lent, lend_sem.at[0], lend_sem.at[1], at(buddy))

    pass_on(0, held + 1)
    pass_back(held, held + 2)
    pass_on(held + 1, held + 2)
    pass_back(held + 2, chunks)
    pass_on(held + 2, chunks)
    @pl.when(outer)
    def _():
        await_pots(near_in)
        lend().start()

        def arrived(c, _):
            await_orbit(far_in, c)
            return 0

        lax.fori_loop(0, chunks, arrived, 0)

    def hand_back(plane, w):
        return remote(
            done.at[plane * owned + w], out_ref.at[w, pl.ds(z * PLANE, PLANE)],
            done_sem.at[0], done_sem.at[1], at(plane),
        )

    def rows_done(left, orbit, old):
        moved = jnp.dot(
            left.reshape(-1, width), orbit.reshape(width, nocc), preferred_element_type=jnp.float32
        )
        return (old.astype(jnp.float32) + moved.reshape(old.shape)).astype(jnp.bfloat16)

    here = pl.ds(z * PLANE, PLANE)

    def serve(plane, first, last):
        def step(w, _):
            done[plane * owned + w] = rows_done(
                recv[plane * owned + w], guest[plane, w], guest[plane, w, here]
            )
            hand_back(plane, w).start()
            return 0

        lax.fori_loop(first, last, step, 0)

    forward_far(0, CHUNKS)
    await_pots(far_in)
    @pl.when(outer)
    def _():
        serve(far_in, 0, owned)

    forward_far(CHUNKS, 2 * CHUNKS)
    await_pots(far_out)
    serve(far_out, 0, 2)
    for w in range(2, owned):
        forward_far(CHUNKS * w, CHUNKS * (w + 1))
        serve(far_out, w, w + 1)

    @pl.when(inner)
    def _():
        serve(far_in, 0, owned)

    @pl.when(inner)
    def _():
        await_pots(near_out)
        serve(near_out, 0, owned)

    await_pots(z)
    orb_copy.wait()

    def advance(w, _):
        out_ref[w, here] = rows_done(recv[z * owned + w], orb_ref[w], orb_ref[w, here])
        return 0

    lax.fori_loop(0, owned, advance, 0)

    @pl.when(inner)
    def _():
        lend().wait_recv()
        there = pl.ds(near_out * PLANE, PLANE)

        def borrow(w, _):
            out_ref[w, there] = rows_done(lent[w], orb_ref[w], orb_ref[w, there])
            return 0

        lax.fori_loop(0, owned, borrow, 0)

    gathered(part_in, part_sem).wait_send()
    gathered(fields_ref, field_sem).wait_send()
    every = send.at[:, pl.ds(0, (PLANE - 1) * line)]
    remote(every, every, pot_send.at[0], pot_recv.at[z], at(ahead)).wait_send()

    def through(ref, sem):
        return remote(ref, ref, sem.at[0], sem.at[1], at(ahead))

    @pl.when(outer)
    def _():
        sum_copy(0, at(ahead)).wait_send()
        lend().wait_send()
        remote(guest.at[0], guest.at[0], orb_send.at[0], orb_recv.at[0, 0], at(ahead)).wait_send()
        through(done.at[pl.ds(0, 2 * owned)], done_sem).wait_send()

    @pl.when(inner)
    def _():
        sum_copy(1, at(ahead)).wait_send()
        total_copy().wait_send()
        remote(guest, guest, orb_send.at[0], orb_recv.at[0, 0], at(ahead)).wait_send()
        through(done.at[pl.ds(0, 3 * owned)], done_sem).wait_send()

    @pl.when(outer)
    def _():
        through(out_ref.at[:, pl.ds(0, 3 * PLANE)], done_sem).wait_recv()

    @pl.when(inner)
    def _():
        through(out_ref.at[:, pl.ds(0, 2 * PLANE)], done_sem).wait_recv()


def close_kernel(moved_ref, logs_ref, out_hbm, log_hbm, log_ref, sem):
    copies = [
        pltpu.make_async_copy(moved_ref.at[w], out_hbm.at[w], sem.at[w]) for w in range(moved_ref.shape[0])
    ]
    for copy in copies:
        copy.start()
    log_ref[...] = logs_ref[:, 0]
    copies.append(pltpu.make_async_copy(log_ref, log_hbm, sem.at[len(copies)]))
    copies[-1].start()
    for copy in copies:
        copy.wait()


def on_device(n, chol_full, chol_half, green, gauss, orbitals):
    walkers, local_rows, nocc = green.shape
    owned, width, _ = orbitals.shape
    vectors = chol_half.shape[0]
    tiles = local_rows // TILE
    vmem = pl.BlockSpec(memory_space=pltpu.VMEM)
    hbm = pl.BlockSpec(memory_space=pl.ANY)
    dma = pltpu.SemaphoreType.DMA
    split = (owned, n, tiles, TILE, nocc)
    params = pltpu.CompilerParams(collective_id=0, has_side_effects=True, vmem_limit_bytes=60 << 20)
    shared = [
        pltpu.VMEM((tiles, vectors, TILE, width), jnp.bfloat16),
        pltpu.VMEM((vectors, local_rows, nocc), jnp.bfloat16),
        pltpu.VMEM((walkers, local_rows, nocc), jnp.bfloat16),
    ]
    arrays = (chol_full, chol_half, green, gauss.reshape(n, owned, vectors), orbitals.reshape(split))
    if n == 4 * PLANE and orbitals.size * orbitals.dtype.itemsize <= OWN_LIMIT:
        line = walkers // PLANE
        planes = n // PLANE
        moved, logs = pl.pallas_call(
            functools.partial(line_kernel, n),
            out_shape=(pltpu.VMEM(split, jnp.bfloat16), pltpu.VMEM((owned, LANES), jnp.float32)),
            in_specs=[hbm] * 5,
            out_specs=(vmem, vmem),
            scratch_shapes=[
                *shared,
                pltpu.VMEM((n, owned, vectors), jnp.float32),
                pltpu.VMEM(split, jnp.bfloat16),
                pltpu.VMEM((PLANE, line, vectors), jnp.float32),
                pltpu.VMEM((PLANE, line, vectors), jnp.float32),
                pltpu.VMEM((2, line, vectors), jnp.float32),
                pltpu.VMEM((2, line, vectors), jnp.float32),
                pltpu.VMEM((line, vectors), jnp.float32),
                pltpu.VMEM((planes, owned, LANES), jnp.float32),
                pltpu.VMEM((PLANE, line, vectors), jnp.bfloat16),
                pltpu.VMEM((tiles, walkers, TILE, width), jnp.bfloat16),
                pltpu.VMEM((line, PLANE, tiles, TILE, width), jnp.bfloat16),
                pltpu.VMEM((planes,) + split, jnp.bfloat16),
                pltpu.VMEM((line, PLANE, tiles, TILE, nocc), jnp.bfloat16),
                pltpu.VMEM((owned, PLANE, tiles, TILE, width), jnp.bfloat16),
                dma((1,)), dma((4,)), dma((2,)), dma((2, 2)), dma((2,)), dma((1,)), dma((planes,)),
                dma((1,)), dma((planes - 1, CHUNKS * owned)), dma((2,)), dma((2,)),
            ],
            compiler_params=params,
        )(*arrays)
        moved, logs = pl.pallas_call(
            close_kernel,
            out_shape=(
                jax.ShapeDtypeStruct(split, jnp.bfloat16),
                jax.ShapeDtypeStruct((owned,), jnp.float32),
            ),
            in_specs=[pl.BlockSpec(memory_space=pltpu.VMEM)] * 2,
            out_specs=(hbm, hbm),
            scratch_shapes=[pltpu.VMEM((owned,), jnp.float32), dma((owned + 1,))],
            compiler_params=pltpu.CompilerParams(vmem_limit_bytes=1 << 20),
        )(moved, logs)
        return moved.reshape(orbitals.shape), logs
    else:
        moved, logs = pl.pallas_call(
            functools.partial(direct_kernel, n),
            out_shape=(
                jax.ShapeDtypeStruct(split, jnp.bfloat16),
                jax.ShapeDtypeStruct((owned, LANES), jnp.float32),
            ),
            in_specs=[hbm, hbm, hbm, vmem, vmem],
            out_specs=(vmem, vmem),
            scratch_shapes=[
                *shared,
                pltpu.VMEM((n, owned, vectors), jnp.float32),
                pltpu.VMEM((n, owned, vectors), jnp.float32),
                pltpu.VMEM((owned, vectors), jnp.float32),
                pltpu.VMEM((n, owned, vectors), jnp.float32),
                pltpu.VMEM((tiles, walkers, TILE, width), jnp.bfloat16),
                pltpu.VMEM((tiles, owned, n * TILE, width), jnp.bfloat16),
                dma((tiles,)), dma((2,)), dma((n,)), dma((n,)), dma((n,)), dma((n,)),
                dma((tiles, n)), dma((tiles, n)),
            ],
            compiler_params=params,
        )(*arrays)
    return moved.reshape(orbitals.shape), logs[:, 0]


def solution(mesh):
    placed = (
        P(None, "chol", None),
        P(None, "chol", None),
        P("grp", "chol", None),
        P("grp", None),
        P(("grp", "chol"), None, None),
    )
    return jax.shard_map(
        functools.partial(on_device, mesh.shape["chol"]),
        mesh=mesh,
        in_specs=placed,
        out_specs=(P(("grp", "chol"), None, None), P(("grp", "chol"))),
        check_vma=False,
    )
```

```python
import functools

import jax
import jax.numpy as jnp
from jax import lax
from jax.experimental import pallas as pl
from jax.experimental.pallas import tpu as pltpu
from jax.sharding import PartitionSpec as P

TILE = 16
LANES = 128
PLANE = 4
OWN_LIMIT = 2 << 20
CHUNKS = 2
FIRST = 1
SECOND = 2
THIRD = 3


def remote(src, dst, send, recv, peer):
    return pltpu.make_async_remote_copy(
        src_ref=src,
        dst_ref=dst,
        send_sem=send,
        recv_sem=recv,
        device_id={"chol": peer},
        device_id_type=pl.DeviceIdType.MESH,
    )


def direct_kernel(
    n, chol_hbm, half_hbm, green_hbm, gauss_ref, orb_ref,
    out_ref, log_ref,
    chol, half, green, part, part_in, fields_own, fields_in, send, recv,
    load_sem, aux_sem, part_send, part_recv, field_send, field_recv, pot_send, pot_recv,
):
    me = lax.axis_index("chol")
    owned = part.shape[1]
    tiles = chol.shape[0]
    width = chol.shape[3]

    half_copy = pltpu.make_async_copy(half_hbm, half, aux_sem.at[0])
    green_copy = pltpu.make_async_copy(green_hbm, green, aux_sem.at[1])
    half_copy.start()
    green_copy.start()
    loads = [
        pltpu.make_async_copy(chol_hbm.at[:, pl.ds(t * TILE, TILE), :], chol.at[t], load_sem.at[t])
        for t in range(tiles)
    ]
    for load in loads:
        load.start()

    barrier = pltpu.get_barrier_semaphore()

    def greet(k, _):
        pl.semaphore_signal(
            barrier, inc=1, device_id={"chol": lax.rem(me + k, n)}, device_id_type=pl.DeviceIdType.MESH
        )
        return 0

    lax.fori_loop(1, n, greet, 0)

    half_copy.wait()
    green_copy.wait()

    def bias(t, acc):
        rows = pl.ds(pl.multiple_of(t * TILE, TILE), TILE)
        left = jnp.swapaxes(green[:, rows, :], 0, 1)
        right = jnp.swapaxes(half[:, rows, :], 0, 1)
        for r in range(TILE):
            acc += lax.dot_general(
                left[r], right[r], (((1,), (1,)), ((), ())), preferred_element_type=jnp.float32
            )
        return acc

    total = lax.fori_loop(0, tiles, bias, jnp.zeros((n * owned, half.shape[0]), jnp.float32))
    for d in range(n):
        part[d] = total[d * owned:(d + 1) * owned]
    pl.semaphore_wait(barrier, n - 1)

    def peer_of(k):
        return lax.rem(me + k, n)

    def push_part(k, _):
        to = peer_of(k)
        remote(part.at[to], part_in.at[me], part_send.at[to], part_recv.at[me], to).start()
        return 0

    lax.fori_loop(1, n, push_part, 0)
    part_in[me] = part[me]

    def wait_part(k, _):
        peer = peer_of(k)
        copy = remote(part.at[peer], part_in.at[peer], part_send.at[peer], part_recv.at[peer], peer)
        copy.wait_recv()
        return 0

    lax.fori_loop(1, n, wait_part, 0)
    vbias = jnp.sum(part_in[...], axis=0)
    gauss = gauss_ref[me]
    xbar = jnp.clip(-0.3 * vbias, -1.0, 1.0)
    log_ref[...] = jnp.broadcast_to(
        jnp.sum(gauss * xbar - 0.5 * xbar * xbar, axis=1, keepdims=True), log_ref.shape
    )
    mine = gauss - xbar
    fields_own[...] = mine
    fields_in[me] = mine

    def push_field(k, _):
        to = peer_of(k)
        remote(fields_own, fields_in.at[me], field_send.at[to], field_recv.at[me], to).start()
        return 0

    lax.fori_loop(1, n, push_field, 0)

    def wait_field(k, _):
        peer = peer_of(k)
        remote(fields_own, fields_in.at[peer], field_send.at[peer], field_recv.at[peer], peer).wait_recv()
        return 0

    lax.fori_loop(1, n, wait_field, 0)
    fields = jnp.concatenate([fields_in[d] for d in range(n)], axis=0).astype(jnp.bfloat16)

    def walkers_of(d):
        return pl.ds(d * owned, owned)

    def rows_of(d):
        return pl.ds(pl.multiple_of(d * TILE, TILE), TILE)

    for t in range(tiles):
        loads[t].wait()

        def strip(c, _):
            cols = pl.ds(pl.multiple_of(c * LANES, LANES), LANES)
            block = jnp.swapaxes(chol[t, :, :, cols], 0, 1)
            pots = [
                (jnp.dot(fields, block[r], preferred_element_type=jnp.float32) * 0.3).astype(jnp.bfloat16)
                for r in range(TILE)
            ]
            send[t, :, :, cols] = jnp.swapaxes(jnp.stack(pots, axis=0), 0, 1)
            return 0

        lax.fori_loop(0, width // LANES, strip, 0)

        def push_pot(k, _):
            to = peer_of(k)
            remote(
                send.at[t, walkers_of(to)], recv.at[t, :, rows_of(me), :],
                pot_send.at[t, to], pot_recv.at[t, me], to,
            ).start()
            return 0

        lax.fori_loop(1, n, push_pot, 0)
        recv[t, :, rows_of(me), :] = send[t, walkers_of(me)]

    for t in range(tiles):

        def wait_pot(k, _):
            peer = peer_of(k)
            remote(
                send.at[t, walkers_of(peer)], recv.at[t, :, rows_of(peer), :],
                pot_send.at[t, peer], pot_recv.at[t, peer], peer,
            ).wait_recv()
            return 0

        lax.fori_loop(1, n, wait_pot, 0)

        def advance(w, _):
            orbit = orb_ref[w].reshape(width, orb_ref.shape[-1])
            for first in range(0, n, 16):
                span = min(16, n - first)
                moved = jnp.dot(
                    recv[t, w, first * TILE:(first + span) * TILE, :], orbit,
                    preferred_element_type=jnp.float32,
                ).reshape(span, TILE, orbit.shape[-1])
                old = orb_ref[w, first:first + span, t].astype(jnp.float32)
                out_ref[w, first:first + span, t] = (old + moved).astype(jnp.bfloat16)
            return 0

        lax.fori_loop(0, owned, advance, 0)

    def drain(k, _):
        peer = peer_of(k)
        remote(part.at[peer], part_in.at[peer], part_send.at[peer], part_recv.at[peer], peer).wait_send()
        remote(fields_own, fields_in.at[peer], field_send.at[peer], field_recv.at[peer], peer).wait_send()
        for t in range(tiles):
            remote(
                send.at[t, walkers_of(peer)], recv.at[t, :, rows_of(peer), :],
                pot_send.at[t, peer], pot_recv.at[t, peer], peer,
            ).wait_send()
        return 0

    lax.fori_loop(1, n, drain, 0)


def line_kernel(
    n, chol_hbm, half_hbm, green_hbm, gauss_hbm, orb_hbm,
    out_ref, log_ref,
    chol, half, green, gauss_ref, orb_ref, part, part_in, partial, partial_in, bias_ref, log_all, fields_ref,
    send, recv, guest, done, lent,
    load_sem, aux_sem, part_sem, sum_sem, field_sem, pot_send, pot_recv, orb_send, orb_recv,
    lend_sem, done_sem, news, ready,
):
    me = lax.axis_index("chol")
    owned = orb_ref.shape[0]
    tiles = chol.shape[0]
    width = chol.shape[3]
    nocc = orb_ref.shape[-1]
    planes = n // PLANE
    line = planes * owned
    chunks = CHUNKS * owned
    span = n // CHUNKS

    z = me // PLANE
    seat = lax.rem(me, PLANE)
    side = z // 2
    far = 1 - side
    near_in, near_out = 1 + side, 3 * side
    far_in, far_out = 1 + far, 3 * far
    ahead = z + 1 - 2 * side
    buddy = near_in + near_out - z
    inner = z == near_in
    outer = z == near_out

    barrier = pltpu.get_barrier_semaphore()

    partner = seat + 1 - 2 * lax.rem(seat, 2)
    beside = lax.rem(seat + 2, PLANE)
    diagonal = lax.rem(partner + 2, PLANE)
    others = (beside, diagonal, partner)

    def greet(peer):
        pl.semaphore_signal(barrier, inc=1, device_id={"chol": peer}, device_id_type=pl.DeviceIdType.MESH)

    def tell(sem, peer):
        pl.semaphore_signal(sem, inc=1, device_id={"chol": peer}, device_id_type=pl.DeviceIdType.MESH)

    @pl.when(inner)
    def _():
        greet(ahead * PLANE + seat)
        greet(buddy * PLANE + seat)

    @pl.when(outer)
    def _():
        for s in others:
            greet(z * PLANE + s)

    half_copy = pltpu.make_async_copy(half_hbm, half, aux_sem.at[0])
    green_copy = pltpu.make_async_copy(green_hbm, green, aux_sem.at[1])
    gauss_copy = pltpu.make_async_copy(gauss_hbm, gauss_ref, aux_sem.at[2])
    orb_copy = pltpu.make_async_copy(orb_hbm, orb_ref, aux_sem.at[3])
    for copy in (green_copy, half_copy, gauss_copy):
        copy.start()
    loads = [
        pltpu.make_async_copy(chol_hbm.at[:, pl.ds(t * TILE, TILE), :], chol.at[t], load_sem.at[0])
        for t in range(tiles)
    ]
    @pl.when(inner)
    def _():
        pl.semaphore_wait(barrier, 1)

    @pl.when(outer)
    def _():
        pl.semaphore_wait(barrier, PLANE)
        for s in others:
            tell(news, z * PLANE + s)

    def at(plane):
        return plane * PLANE + seat

    def piece(ref, c):
        return ref.at[c // CHUNKS, pl.ds(lax.rem(c, CHUNKS) * span, span)]

    def landed(plane, to, c):
        return orb_recv.at[lax.rem(plane - to + planes, planes) - 1, c]

    def own_orbit(c):
        return remote(piece(orb_hbm, c), piece(guest.at[z], c), orb_send.at[0], landed(z, ahead, c), at(ahead))

    def orbit_copy(plane, to, c):
        there = piece(guest.at[plane], c)
        return remote(there, there, orb_send.at[0], landed(plane, to, c), at(to))

    def orbit_on(c):
        return orbit_copy(near_out, ahead, c)

    def orbit_back(plane, c):
        return orbit_copy(plane, buddy, c)

    def await_orbit(plane, c):
        there = piece(guest.at[plane], c)
        remote(there, there, orb_send.at[0], landed(plane, z, c), at(ahead)).wait_recv()

    def start_own(first, last):
        def step(c, _):
            own_orbit(c).start()
            return 0

        lax.fori_loop(first, last, step, 0)

    def pass_on(first, last):
        @pl.when(inner)
        def _():
            def step(c, _):
                await_orbit(near_out, c)
                orbit_on(c).start()
                return 0

            lax.fori_loop(first, last, step, 0)

    def pass_back(first, last):
        @pl.when(inner)
        def _():
            def step(c, _):
                await_orbit(far_in, c)
                orbit_back(far_in, c).start()
                return 0

            lax.fori_loop(first, last, step, 0)

    start_own(0, FIRST)

    @pl.when(outer)
    def _():
        pl.semaphore_wait(news, PLANE - 1)
        tell(ready, at(ahead))


    half_copy.wait()
    green_copy.wait()
    for copy in (*loads, orb_copy):
        copy.start()
    gauss_copy.wait()

    def bias(t, acc):
        rows = pl.ds(pl.multiple_of(t * TILE, TILE), TILE)
        left = jnp.swapaxes(green[:, rows, :], 0, 1)
        right = jnp.swapaxes(half[:, rows, :], 0, 1)
        for r in range(TILE):
            acc += lax.dot_general(
                left[r], right[r], (((1,), (1,)), ((), ())), preferred_element_type=jnp.float32
            )
        return acc

    total = lax.fori_loop(0, tiles, bias, jnp.zeros((n * owned, half.shape[0]), jnp.float32))
    for d in range(n):
        plane, s = divmod(d, PLANE)
        part[s, plane * owned:(plane + 1) * owned] = total[d * owned:(d + 1) * owned]

    @pl.when(inner)
    def _():
        pl.semaphore_wait(ready, 1)

    def part_copy(there, source):
        return remote(part.at[there], part_in.at[source], part_sem.at[0], part_sem.at[1], z * PLANE + there)

    def field_copy(there):
        mine = fields_ref.at[seat]
        return remote(mine, mine, field_sem.at[0], field_sem.at[1], z * PLANE + there)

    def gathered(ref, sem):
        every = ref.at[pl.ds(0, PLANE - 1)]
        return remote(every, every, sem.at[0], sem.at[1], at(ahead))

    def sum_copy(k, to):
        return remote(partial.at[k], partial_in.at[k], sum_sem.at[0, 0], sum_sem.at[1, k], to)

    def total_copy():
        return remote(bias_ref, bias_ref, sum_sem.at[0, 1], sum_sem.at[1, 0], at(buddy))

    for s in others:
        part_copy(s, seat).start()
    part_in[seat] = part[seat]

    @pl.when(inner)
    def _():
        start_own(FIRST, SECOND)

    pass_back(0, FIRST)
    gathered(part_in, part_sem).wait_recv()
    partial[0] = jnp.sum(part_in[...], axis=0)

    @pl.when(outer)
    def _():
        sum_copy(0, at(ahead)).start()
        start_own(FIRST, chunks)
        total_copy().wait_recv()

    @pl.when(inner)
    def _():
        sum_copy(0, at(ahead)).wait_recv()
        partial[1] = partial[0] + partial_in[0]
        sum_copy(1, at(ahead)).start()
        start_own(SECOND, THIRD)
        sum_copy(1, at(ahead)).wait_recv()
        bias_ref[...] = partial[1] + partial_in[1]
        total_copy().start()
        start_own(THIRD, chunks)

    pass_back(FIRST, SECOND)
    vbias = bias_ref[...]
    gauss = jnp.concatenate([gauss_ref[plane * PLANE + seat] for plane in range(planes)], axis=0)
    xbar = jnp.clip(-0.3 * vbias, -1.0, 1.0)
    logs = jnp.sum(gauss * xbar - 0.5 * xbar * xbar, axis=1, keepdims=True)
    log_all[...] = jnp.broadcast_to(logs, (line, LANES)).reshape(log_all.shape)
    log_ref[...] = log_all[z]
    fields_ref[seat] = (gauss - xbar).astype(jnp.bfloat16)

    for s in others:
        field_copy(s).start()
    gathered(fields_ref, field_sem).wait_recv()
    pltpu.make_async_copy(chol, chol, load_sem.at[0]).wait()
    fields = fields_ref[...].reshape(n * owned, fields_ref.shape[-1])

    order = (
        jnp.where(inner, far_in, near_in), jnp.where(inner, far_out, far_in),
        jnp.where(inner, near_out, far_out), z,
    )

    def pot_copy(t, plane, there, source):
        return remote(
            send.at[t, pl.ds(there * line + plane * owned, owned)],
            recv.at[pl.ds(plane * owned, owned), source, t],
            pot_send.at[0], pot_recv.at[plane], z * PLANE + there,
        )

    def push(t, plane):
        for s in others:
            pot_copy(t, plane, s, seat).start()

    def await_pots(plane):
        every = recv.at[pl.ds(plane * owned, owned), pl.ds(0, PLANE - 1)]
        remote(every, every, pot_send.at[0], pot_recv.at[plane], z * PLANE + partner).wait_recv()

    def fill(t):
        def strip(c, _):
            cols = pl.ds(pl.multiple_of(c * LANES, LANES), LANES)
            block = jnp.swapaxes(chol[t, :, :, cols], 0, 1)
            pots = [
                (jnp.dot(fields, block[r], preferred_element_type=jnp.float32) * 0.3).astype(jnp.bfloat16)
                for r in range(TILE)
            ]
            send[t, :, :, cols] = jnp.swapaxes(jnp.stack(pots, axis=0), 0, 1)
            return 0

        lax.fori_loop(0, width // LANES, strip, 0)
        recv[:, seat, t] = send[t, pl.ds(seat * line, line)]

    def forward_far(first, last):
        def step(c, _):
            await_orbit(far_out, c)

            @pl.when(inner)
            def _():
                orbit_back(far_out, c).start()

            return 0

        lax.fori_loop(first, last, step, 0)

    for t in range(tiles):
        fill(t)
        push(t, order[0])
        if t < tiles - 2:
            pass_back(SECOND + t, SECOND + t + 1)
    held = SECOND + tiles - 2
    for plane in order[1:]:
        for t in range(tiles):
            push(t, plane)

    def lend():
        return remote(recv.at[pl.ds(buddy * owned, owned)], lent, lend_sem.at[0], lend_sem.at[1], at(buddy))

    pass_on(0, held + 1)
    pass_back(held, held + 2)
    pass_on(held + 1, held + 2)
    pass_back(held + 2, chunks)
    pass_on(held + 2, chunks)
    @pl.when(outer)
    def _():
        await_pots(near_in)
        lend().start()

        def arrived(c, _):
            await_orbit(far_in, c)
            return 0

        lax.fori_loop(0, chunks, arrived, 0)

    def hand_back(plane, w):
        return remote(
            done.at[plane * owned + w], out_ref.at[w, pl.ds(z * PLANE, PLANE)],
            done_sem.at[0], done_sem.at[1], at(plane),
        )

    def rows_done(left, orbit, old):
        moved = jnp.dot(
            left.reshape(-1, width), orbit.reshape(width, nocc), preferred_element_type=jnp.float32
        )
        return (old.astype(jnp.float32) + moved.reshape(old.shape)).astype(jnp.bfloat16)

    here = pl.ds(z * PLANE, PLANE)

    def serve(plane, first, last):
        def step(w, _):
            done[plane * owned + w] = rows_done(
                recv[plane * owned + w], guest[plane, w], guest[plane, w, here]
            )
            hand_back(plane, w).start()
            return 0

        lax.fori_loop(first, last, step, 0)

    forward_far(0, CHUNKS)
    await_pots(far_in)
    @pl.when(outer)
    def _():
        serve(far_in, 0, owned)

    forward_far(CHUNKS, 2 * CHUNKS)
    await_pots(far_out)
    serve(far_out, 0, 2)
    for w in range(2, owned):
        forward_far(CHUNKS * w, CHUNKS * (w + 1))
        serve(far_out, w, w + 1)

    @pl.when(inner)
    def _():
        serve(far_in, 0, owned)

    @pl.when(inner)
    def _():
        await_pots(near_out)
        serve(near_out, 0, owned)

    await_pots(z)
    orb_copy.wait()

    def advance(w, _):
        out_ref[w, here] = rows_done(recv[z * owned + w], orb_ref[w], orb_ref[w, here])
        return 0

    lax.fori_loop(0, owned, advance, 0)

    @pl.when(inner)
    def _():
        lend().wait_recv()
        there = pl.ds(near_out * PLANE, PLANE)

        def borrow(w, _):
            out_ref[w, there] = rows_done(lent[w], orb_ref[w], orb_ref[w, there])
            return 0

        lax.fori_loop(0, owned, borrow, 0)

    gathered(part_in, part_sem).wait_send()
    gathered(fields_ref, field_sem).wait_send()
    every = send.at[:, pl.ds(0, (PLANE - 1) * line)]
    remote(every, every, pot_send.at[0], pot_recv.at[z], at(ahead)).wait_send()

    def through(ref, sem):
        return remote(ref, ref, sem.at[0], sem.at[1], at(ahead))

    @pl.when(outer)
    def _():
        sum_copy(0, at(ahead)).wait_send()
        lend().wait_send()
        remote(guest.at[0], guest.at[0], orb_send.at[0], orb_recv.at[0, 0], at(ahead)).wait_send()
        through(done.at[pl.ds(0, 2 * owned)], done_sem).wait_send()

    @pl.when(inner)
    def _():
        sum_copy(1, at(ahead)).wait_send()
        total_copy().wait_send()
        remote(guest, guest, orb_send.at[0], orb_recv.at[0, 0], at(ahead)).wait_send()
        through(done.at[pl.ds(0, 3 * owned)], done_sem).wait_send()

    @pl.when(outer)
    def _():
        through(out_ref.at[:, pl.ds(0, 3 * PLANE)], done_sem).wait_recv()

    @pl.when(inner)
    def _():
        through(out_ref.at[:, pl.ds(0, 2 * PLANE)], done_sem).wait_recv()


def close_kernel(moved_ref, logs_ref, out_hbm, log_hbm, log_ref, sem):
    copies = [
        pltpu.make_async_copy(moved_ref.at[w], out_hbm.at[w], sem.at[w]) for w in range(moved_ref.shape[0])
    ]
    for copy in copies:
        copy.start()
    log_ref[...] = logs_ref[:, 0]
    copies.append(pltpu.make_async_copy(log_ref, log_hbm, sem.at[len(copies)]))
    copies[-1].start()
    for copy in copies:
        copy.wait()


def on_device(n, chol_full, chol_half, green, gauss, orbitals):
    walkers, local_rows, nocc = green.shape
    owned, width, _ = orbitals.shape
    vectors = chol_half.shape[0]
    tiles = local_rows // TILE
    vmem = pl.BlockSpec(memory_space=pltpu.VMEM)
    hbm = pl.BlockSpec(memory_space=pl.ANY)
    dma = pltpu.SemaphoreType.DMA
    split = (owned, n, tiles, TILE, nocc)
    params = pltpu.CompilerParams(collective_id=0, has_side_effects=True, vmem_limit_bytes=60 << 20)
    shared = [
        pltpu.VMEM((tiles, vectors, TILE, width), jnp.bfloat16),
        pltpu.VMEM((vectors, local_rows, nocc), jnp.bfloat16),
        pltpu.VMEM((walkers, local_rows, nocc), jnp.bfloat16),
    ]
    arrays = (chol_full, chol_half, green, gauss.reshape(n, owned, vectors), orbitals.reshape(split))
    if n == 4 * PLANE and orbitals.size * orbitals.dtype.itemsize <= OWN_LIMIT:
        line = walkers // PLANE
        planes = n // PLANE
        moved, logs = pl.pallas_call(
            functools.partial(line_kernel, n),
            out_shape=(pltpu.VMEM(split, jnp.bfloat16), pltpu.VMEM((owned, LANES), jnp.float32)),
            in_specs=[hbm] * 5,
            out_specs=(vmem, vmem),
            scratch_shapes=[
                *shared,
                pltpu.VMEM((n, owned, vectors), jnp.float32),
                pltpu.VMEM(split, jnp.bfloat16),
                pltpu.VMEM((PLANE, line, vectors), jnp.float32),
                pltpu.VMEM((PLANE, line, vectors), jnp.float32),
                pltpu.VMEM((2, line, vectors), jnp.float32),
                pltpu.VMEM((2, line, vectors), jnp.float32),
                pltpu.VMEM((line, vectors), jnp.float32),
                pltpu.VMEM((planes, owned, LANES), jnp.float32),
                pltpu.VMEM((PLANE, line, vectors), jnp.bfloat16),
                pltpu.VMEM((tiles, walkers, TILE, width), jnp.bfloat16),
                pltpu.VMEM((line, PLANE, tiles, TILE, width), jnp.bfloat16),
                pltpu.VMEM((planes,) + split, jnp.bfloat16),
                pltpu.VMEM((line, PLANE, tiles, TILE, nocc), jnp.bfloat16),
                pltpu.VMEM((owned, PLANE, tiles, TILE, width), jnp.bfloat16),
                dma((1,)), dma((4,)), dma((2,)), dma((2, 2)), dma((2,)), dma((1,)), dma((planes,)),
                dma((1,)), dma((planes - 1, CHUNKS * owned)), dma((2,)), dma((2,)),
                pltpu.SemaphoreType.REGULAR, pltpu.SemaphoreType.REGULAR,
            ],
            compiler_params=params,
        )(*arrays)
        moved, logs = pl.pallas_call(
            close_kernel,
            out_shape=(
                jax.ShapeDtypeStruct(split, jnp.bfloat16),
                jax.ShapeDtypeStruct((owned,), jnp.float32),
            ),
            in_specs=[pl.BlockSpec(memory_space=pltpu.VMEM)] * 2,
            out_specs=(hbm, hbm),
            scratch_shapes=[pltpu.VMEM((owned,), jnp.float32), dma((owned + 1,))],
            compiler_params=pltpu.CompilerParams(vmem_limit_bytes=1 << 20),
        )(moved, logs)
        return moved.reshape(orbitals.shape), logs
    else:
        moved, logs = pl.pallas_call(
            functools.partial(direct_kernel, n),
            out_shape=(
                jax.ShapeDtypeStruct(split, jnp.bfloat16),
                jax.ShapeDtypeStruct((owned, LANES), jnp.float32),
            ),
            in_specs=[hbm, hbm, hbm, vmem, vmem],
            out_specs=(vmem, vmem),
            scratch_shapes=[
                *shared,
                pltpu.VMEM((n, owned, vectors), jnp.float32),
                pltpu.VMEM((n, owned, vectors), jnp.float32),
                pltpu.VMEM((owned, vectors), jnp.float32),
                pltpu.VMEM((n, owned, vectors), jnp.float32),
                pltpu.VMEM((tiles, walkers, TILE, width), jnp.bfloat16),
                pltpu.VMEM((tiles, owned, n * TILE, width), jnp.bfloat16),
                dma((tiles,)), dma((2,)), dma((n,)), dma((n,)), dma((n,)), dma((n,)),
                dma((tiles, n)), dma((tiles, n)),
            ],
            compiler_params=params,
        )(*arrays)
    return moved.reshape(orbitals.shape), logs[:, 0]


def solution(mesh):
    placed = (
        P(None, "chol", None),
        P(None, "chol", None),
        P("grp", "chol", None),
        P("grp", None),
        P(("grp", "chol"), None, None),
    )
    return jax.shard_map(
        functools.partial(on_device, mesh.shape["chol"]),
        mesh=mesh,
        in_specs=placed,
        out_specs=(P(("grp", "chol"), None, None), P(("grp", "chol"))),
        check_vma=False,
    )
```

```python
import functools

import jax
import jax.numpy as jnp
from jax import lax
from jax.experimental import pallas as pl
from jax.experimental.pallas import tpu as pltpu
from jax.sharding import PartitionSpec as P

TILE = 16
LANES = 128
PLANE = 4
OWN_LIMIT = 2 << 20
CHUNKS = 2
FIRST = 1
SECOND = 2
THIRD = 3


def remote(src, dst, send, recv, peer):
    return pltpu.make_async_remote_copy(
        src_ref=src,
        dst_ref=dst,
        send_sem=send,
        recv_sem=recv,
        device_id={"chol": peer},
        device_id_type=pl.DeviceIdType.MESH,
    )


def direct_kernel(
    n, chol_hbm, half_hbm, green_hbm, gauss_ref, orb_ref,
    out_ref, log_ref,
    chol, half, green, part, part_in, fields_own, fields_in, send, recv,
    load_sem, aux_sem, part_send, part_recv, field_send, field_recv, pot_send, pot_recv,
):
    me = lax.axis_index("chol")
    owned = part.shape[1]
    tiles = chol.shape[0]
    width = chol.shape[3]

    half_copy = pltpu.make_async_copy(half_hbm, half, aux_sem.at[0])
    green_copy = pltpu.make_async_copy(green_hbm, green, aux_sem.at[1])
    half_copy.start()
    green_copy.start()
    loads = [
        pltpu.make_async_copy(chol_hbm.at[:, pl.ds(t * TILE, TILE), :], chol.at[t], load_sem.at[t])
        for t in range(tiles)
    ]
    for load in loads:
        load.start()

    barrier = pltpu.get_barrier_semaphore()

    def greet(k, _):
        pl.semaphore_signal(
            barrier, inc=1, device_id={"chol": lax.rem(me + k, n)}, device_id_type=pl.DeviceIdType.MESH
        )
        return 0

    lax.fori_loop(1, n, greet, 0)

    half_copy.wait()
    green_copy.wait()

    def bias(t, acc):
        rows = pl.ds(pl.multiple_of(t * TILE, TILE), TILE)
        left = jnp.swapaxes(green[:, rows, :], 0, 1)
        right = jnp.swapaxes(half[:, rows, :], 0, 1)
        for r in range(TILE):
            acc += lax.dot_general(
                left[r], right[r], (((1,), (1,)), ((), ())), preferred_element_type=jnp.float32
            )
        return acc

    total = lax.fori_loop(0, tiles, bias, jnp.zeros((n * owned, half.shape[0]), jnp.float32))
    for d in range(n):
        part[d] = total[d * owned:(d + 1) * owned]
    pl.semaphore_wait(barrier, n - 1)

    def peer_of(k):
        return lax.rem(me + k, n)

    def push_part(k, _):
        to = peer_of(k)
        remote(part.at[to], part_in.at[me], part_send.at[to], part_recv.at[me], to).start()
        return 0

    lax.fori_loop(1, n, push_part, 0)
    part_in[me] = part[me]

    def wait_part(k, _):
        peer = peer_of(k)
        copy = remote(part.at[peer], part_in.at[peer], part_send.at[peer], part_recv.at[peer], peer)
        copy.wait_recv()
        return 0

    lax.fori_loop(1, n, wait_part, 0)
    vbias = jnp.sum(part_in[...], axis=0)
    gauss = gauss_ref[me]
    xbar = jnp.clip(-0.3 * vbias, -1.0, 1.0)
    log_ref[...] = jnp.broadcast_to(
        jnp.sum(gauss * xbar - 0.5 * xbar * xbar, axis=1, keepdims=True), log_ref.shape
    )
    mine = gauss - xbar
    fields_own[...] = mine
    fields_in[me] = mine

    def push_field(k, _):
        to = peer_of(k)
        remote(fields_own, fields_in.at[me], field_send.at[to], field_recv.at[me], to).start()
        return 0

    lax.fori_loop(1, n, push_field, 0)

    def wait_field(k, _):
        peer = peer_of(k)
        remote(fields_own, fields_in.at[peer], field_send.at[peer], field_recv.at[peer], peer).wait_recv()
        return 0

    lax.fori_loop(1, n, wait_field, 0)
    fields = jnp.concatenate([fields_in[d] for d in range(n)], axis=0).astype(jnp.bfloat16)

    def walkers_of(d):
        return pl.ds(d * owned, owned)

    def rows_of(d):
        return pl.ds(pl.multiple_of(d * TILE, TILE), TILE)

    for t in range(tiles):
        loads[t].wait()

        def strip(c, _):
            cols = pl.ds(pl.multiple_of(c * LANES, LANES), LANES)
            block = jnp.swapaxes(chol[t, :, :, cols], 0, 1)
            pots = [
                (jnp.dot(fields, block[r], preferred_element_type=jnp.float32) * 0.3).astype(jnp.bfloat16)
                for r in range(TILE)
            ]
            send[t, :, :, cols] = jnp.swapaxes(jnp.stack(pots, axis=0), 0, 1)
            return 0

        lax.fori_loop(0, width // LANES, strip, 0)

        def push_pot(k, _):
            to = peer_of(k)
            remote(
                send.at[t, walkers_of(to)], recv.at[t, :, rows_of(me), :],
                pot_send.at[t, to], pot_recv.at[t, me], to,
            ).start()
            return 0

        lax.fori_loop(1, n, push_pot, 0)
        recv[t, :, rows_of(me), :] = send[t, walkers_of(me)]

    for t in range(tiles):

        def wait_pot(k, _):
            peer = peer_of(k)
            remote(
                send.at[t, walkers_of(peer)], recv.at[t, :, rows_of(peer), :],
                pot_send.at[t, peer], pot_recv.at[t, peer], peer,
            ).wait_recv()
            return 0

        lax.fori_loop(1, n, wait_pot, 0)

        def advance(w, _):
            orbit = orb_ref[w].reshape(width, orb_ref.shape[-1])
            for first in range(0, n, 16):
                span = min(16, n - first)
                moved = jnp.dot(
                    recv[t, w, first * TILE:(first + span) * TILE, :], orbit,
                    preferred_element_type=jnp.float32,
                ).reshape(span, TILE, orbit.shape[-1])
                old = orb_ref[w, first:first + span, t].astype(jnp.float32)
                out_ref[w, first:first + span, t] = (old + moved).astype(jnp.bfloat16)
            return 0

        lax.fori_loop(0, owned, advance, 0)

    def drain(k, _):
        peer = peer_of(k)
        remote(part.at[peer], part_in.at[peer], part_send.at[peer], part_recv.at[peer], peer).wait_send()
        remote(fields_own, fields_in.at[peer], field_send.at[peer], field_recv.at[peer], peer).wait_send()
        for t in range(tiles):
            remote(
                send.at[t, walkers_of(peer)], recv.at[t, :, rows_of(peer), :],
                pot_send.at[t, peer], pot_recv.at[t, peer], peer,
            ).wait_send()
        return 0

    lax.fori_loop(1, n, drain, 0)


def line_kernel(
    n, chol_hbm, half_hbm, green_hbm, gauss_hbm, orb_hbm,
    out_ref, log_ref,
    chol, half, green, gauss_ref, orb_ref, part, part_in, partial, partial_in, bias_ref, log_all, fields_ref,
    send, recv, guest, done, lent,
    load_sem, aux_sem, part_sem, sum_sem, field_sem, pot_send, pot_recv, orb_send, orb_recv,
    lend_sem, done_sem, news, ready,
):
    me = lax.axis_index("chol")
    owned = orb_ref.shape[0]
    tiles = chol.shape[0]
    width = chol.shape[3]
    nocc = orb_ref.shape[-1]
    planes = n // PLANE
    line = planes * owned
    chunks = CHUNKS * owned
    span = n // CHUNKS

    z = me // PLANE
    seat = lax.rem(me, PLANE)
    side = z // 2
    far = 1 - side
    near_in, near_out = 1 + side, 3 * side
    far_in, far_out = 1 + far, 3 * far
    ahead = z + 1 - 2 * side
    buddy = near_in + near_out - z
    inner = z == near_in
    outer = z == near_out

    barrier = pltpu.get_barrier_semaphore()

    partner = seat + 1 - 2 * lax.rem(seat, 2)
    beside = lax.rem(seat + 2, PLANE)
    diagonal = lax.rem(partner + 2, PLANE)
    others = (beside, diagonal, partner)

    def greet(peer):
        pl.semaphore_signal(barrier, inc=1, device_id={"chol": peer}, device_id_type=pl.DeviceIdType.MESH)

    def tell(sem, peer):
        pl.semaphore_signal(sem, inc=1, device_id={"chol": peer}, device_id_type=pl.DeviceIdType.MESH)

    @pl.when(inner)
    def _():
        greet(ahead * PLANE + seat)
        greet(buddy * PLANE + seat)

    @pl.when(outer)
    def _():
        for s in others:
            greet(z * PLANE + s)

    half_copy = pltpu.make_async_copy(half_hbm, half, aux_sem.at[0])
    green_copy = pltpu.make_async_copy(green_hbm, green, aux_sem.at[1])
    gauss_copy = pltpu.make_async_copy(gauss_hbm, gauss_ref, aux_sem.at[2])
    orb_copy = pltpu.make_async_copy(orb_hbm, orb_ref, aux_sem.at[3])
    for copy in (green_copy, half_copy, gauss_copy):
        copy.start()
    loads = [
        pltpu.make_async_copy(chol_hbm.at[:, pl.ds(t * TILE, TILE), :], chol.at[t], load_sem.at[0])
        for t in range(tiles)
    ]
    @pl.when(inner)
    def _():
        pl.semaphore_wait(barrier, 1)

    @pl.when(outer)
    def _():
        pl.semaphore_wait(barrier, PLANE)
        for s in others:
            tell(news, z * PLANE + s)

    def at(plane):
        return plane * PLANE + seat

    def piece(ref, c):
        return ref.at[c // CHUNKS, pl.ds(lax.rem(c, CHUNKS) * span, span)]

    def landed(plane, to, c):
        return orb_recv.at[lax.rem(plane - to + planes, planes) - 1, c]

    def own_orbit(c):
        return remote(piece(orb_hbm, c), piece(guest.at[z], c), orb_send.at[0], landed(z, ahead, c), at(ahead))

    def orbit_copy(plane, to, c):
        there = piece(guest.at[plane], c)
        return remote(there, there, orb_send.at[0], landed(plane, to, c), at(to))

    def orbit_on(c):
        return orbit_copy(near_out, ahead, c)

    def orbit_back(plane, c):
        return orbit_copy(plane, buddy, c)

    def await_orbit(plane, c):
        there = piece(guest.at[plane], c)
        remote(there, there, orb_send.at[0], landed(plane, z, c), at(ahead)).wait_recv()

    def start_own(first, last):
        def step(c, _):
            own_orbit(c).start()
            return 0

        lax.fori_loop(first, last, step, 0)

    def pass_on(first, last):
        @pl.when(inner)
        def _():
            def step(c, _):
                await_orbit(near_out, c)
                orbit_on(c).start()
                return 0

            lax.fori_loop(first, last, step, 0)

    def pass_back(first, last):
        @pl.when(inner)
        def _():
            def step(c, _):
                await_orbit(far_in, c)
                orbit_back(far_in, c).start()
                return 0

            lax.fori_loop(first, last, step, 0)

    start_own(0, FIRST)

    @pl.when(outer)
    def _():
        pl.semaphore_wait(news, PLANE - 1)
        tell(ready, at(ahead))


    half_copy.wait()
    green_copy.wait()
    for copy in (*loads, orb_copy):
        copy.start()
    gauss_copy.wait()

    def bias(t, acc):
        rows = pl.ds(pl.multiple_of(t * TILE, TILE), TILE)
        left = jnp.swapaxes(green[:, rows, :], 0, 1)
        right = jnp.swapaxes(half[:, rows, :], 0, 1)
        for r in range(TILE):
            acc += lax.dot_general(
                left[r], right[r], (((1,), (1,)), ((), ())), preferred_element_type=jnp.float32
            )
        return acc

    total = lax.fori_loop(0, tiles, bias, jnp.zeros((n * owned, half.shape[0]), jnp.float32))
    for d in range(n):
        plane, s = divmod(d, PLANE)
        part[s, plane * owned:(plane + 1) * owned] = total[d * owned:(d + 1) * owned]

    @pl.when(inner)
    def _():
        pl.semaphore_wait(ready, 1)

    def part_copy(there, source):
        return remote(part.at[there], part_in.at[source], part_sem.at[0], part_sem.at[1], z * PLANE + there)

    def field_copy(there):
        mine = fields_ref.at[seat]
        return remote(mine, mine, field_sem.at[0], field_sem.at[1], z * PLANE + there)

    def gathered(ref, sem):
        every = ref.at[pl.ds(0, PLANE - 1)]
        return remote(every, every, sem.at[0], sem.at[1], at(ahead))

    def sum_copy(k, to):
        return remote(partial.at[k], partial_in.at[k], sum_sem.at[0, 0], sum_sem.at[1, k], to)

    def total_copy():
        return remote(bias_ref, bias_ref, sum_sem.at[0, 1], sum_sem.at[1, 0], at(buddy))

    for s in others:
        part_copy(s, seat).start()
    part_in[seat] = part[seat]

    @pl.when(inner)
    def _():
        start_own(FIRST, SECOND)

    pass_back(0, FIRST)
    gathered(part_in, part_sem).wait_recv()
    partial[0] = jnp.sum(part_in[...], axis=0)

    @pl.when(outer)
    def _():
        sum_copy(0, at(ahead)).start()
        start_own(FIRST, chunks)
        total_copy().wait_recv()

    @pl.when(inner)
    def _():
        sum_copy(0, at(ahead)).wait_recv()
        partial[1] = partial[0] + partial_in[0]
        sum_copy(1, at(ahead)).start()
        start_own(SECOND, THIRD)
        sum_copy(1, at(ahead)).wait_recv()
        bias_ref[...] = partial[1] + partial_in[1]
        total_copy().start()
        start_own(THIRD, chunks)

    pass_back(FIRST, SECOND)
    vbias = bias_ref[...]
    gauss = jnp.concatenate([gauss_ref[plane * PLANE + seat] for plane in range(planes)], axis=0)
    xbar = jnp.clip(-0.3 * vbias, -1.0, 1.0)
    logs = jnp.sum(gauss * xbar - 0.5 * xbar * xbar, axis=1, keepdims=True)
    log_all[...] = jnp.broadcast_to(logs, (line, LANES)).reshape(log_all.shape)
    log_ref[...] = log_all[z]
    fields_ref[seat] = (gauss - xbar).astype(jnp.bfloat16)

    for s in others:
        field_copy(s).start()
    gathered(fields_ref, field_sem).wait_recv()
    pltpu.make_async_copy(chol, chol, load_sem.at[0]).wait()
    fields = fields_ref[...].reshape(n * owned, fields_ref.shape[-1])

    order = (
        jnp.where(inner, far_in, near_in), jnp.where(inner, far_out, far_in),
        jnp.where(inner, near_out, far_out), z,
    )

    def pot_copy(t, plane, there, source):
        return remote(
            send.at[t, pl.ds(there * line + plane * owned, owned)],
            recv.at[pl.ds(plane * owned, owned), source, t],
            pot_send.at[0], pot_recv.at[plane], z * PLANE + there,
        )

    def push(t, plane):
        for s in others:
            pot_copy(t, plane, s, seat).start()

    def await_pots(plane):
        every = recv.at[pl.ds(plane * owned, owned), pl.ds(0, PLANE - 1)]
        remote(every, every, pot_send.at[0], pot_recv.at[plane], z * PLANE + partner).wait_recv()

    def fill(t):
        def strip(c, _):
            cols = pl.ds(pl.multiple_of(c * LANES, LANES), LANES)
            block = jnp.swapaxes(chol[t, :, :, cols], 0, 1)
            pots = [
                (jnp.dot(fields, block[r], preferred_element_type=jnp.float32) * 0.3).astype(jnp.bfloat16)
                for r in range(TILE)
            ]
            send[t, :, :, cols] = jnp.swapaxes(jnp.stack(pots, axis=0), 0, 1)
            return 0

        lax.fori_loop(0, width // LANES, strip, 0)
        recv[:, seat, t] = send[t, pl.ds(seat * line, line)]

    def forward_far(first, last):
        def step(c, _):
            await_orbit(far_out, c)

            @pl.when(inner)
            def _():
                orbit_back(far_out, c).start()

            return 0

        lax.fori_loop(first, last, step, 0)

    for t in range(tiles):
        fill(t)
        push(t, order[0])
        if t < tiles - 1:
            pass_back(SECOND + t, SECOND + t + 1)
    held = SECOND + tiles - 1
    for plane in order[1:]:
        for t in range(tiles):
            push(t, plane)

    def lend():
        return remote(recv.at[pl.ds(buddy * owned, owned)], lent, lend_sem.at[0], lend_sem.at[1], at(buddy))

    pass_back(held, held + 1)
    pass_on(0, held + 1)
    pass_back(held + 1, held + 2)
    pass_on(held + 1, held + 2)
    pass_back(held + 2, chunks)
    pass_on(held + 2, chunks)
    @pl.when(outer)
    def _():
        await_pots(near_in)
        lend().start()

        def arrived(c, _):
            await_orbit(far_in, c)
            return 0

        lax.fori_loop(0, chunks, arrived, 0)

    def hand_back(plane, w):
        return remote(
            done.at[plane * owned + w], out_ref.at[w, pl.ds(z * PLANE, PLANE)],
            done_sem.at[0], done_sem.at[1], at(plane),
        )

    def rows_done(left, orbit, old):
        moved = jnp.dot(
            left.reshape(-1, width), orbit.reshape(width, nocc), preferred_element_type=jnp.float32
        )
        return (old.astype(jnp.float32) + moved.reshape(old.shape)).astype(jnp.bfloat16)

    here = pl.ds(z * PLANE, PLANE)

    def serve(plane, first, last):
        def step(w, _):
            done[plane * owned + w] = rows_done(
                recv[plane * owned + w], guest[plane, w], guest[plane, w, here]
            )
            hand_back(plane, w).start()
            return 0

        lax.fori_loop(first, last, step, 0)

    forward_far(0, CHUNKS)
    await_pots(far_in)
    @pl.when(outer)
    def _():
        serve(far_in, 0, owned)

    forward_far(CHUNKS, 2 * CHUNKS)
    await_pots(far_out)
    serve(far_out, 0, 2)
    for w in range(2, owned):
        forward_far(CHUNKS * w, CHUNKS * (w + 1))
        serve(far_out, w, w + 1)

    @pl.when(inner)
    def _():
        serve(far_in, 0, owned)

    @pl.when(inner)
    def _():
        await_pots(near_out)
        serve(near_out, 0, owned)

    await_pots(z)
    orb_copy.wait()

    def advance(w, _):
        out_ref[w, here] = rows_done(recv[z * owned + w], orb_ref[w], orb_ref[w, here])
        return 0

    lax.fori_loop(0, owned, advance, 0)

    @pl.when(inner)
    def _():
        lend().wait_recv()
        there = pl.ds(near_out * PLANE, PLANE)

        def borrow(w, _):
            out_ref[w, there] = rows_done(lent[w], orb_ref[w], orb_ref[w, there])
            return 0

        lax.fori_loop(0, owned, borrow, 0)

    gathered(part_in, part_sem).wait_send()
    gathered(fields_ref, field_sem).wait_send()
    every = send.at[:, pl.ds(0, (PLANE - 1) * line)]
    remote(every, every, pot_send.at[0], pot_recv.at[z], at(ahead)).wait_send()

    def through(ref, sem):
        return remote(ref, ref, sem.at[0], sem.at[1], at(ahead))

    @pl.when(outer)
    def _():
        sum_copy(0, at(ahead)).wait_send()
        lend().wait_send()
        remote(guest.at[0], guest.at[0], orb_send.at[0], orb_recv.at[0, 0], at(ahead)).wait_send()
        through(done.at[pl.ds(0, 2 * owned)], done_sem).wait_send()

    @pl.when(inner)
    def _():
        sum_copy(1, at(ahead)).wait_send()
        total_copy().wait_send()
        remote(guest, guest, orb_send.at[0], orb_recv.at[0, 0], at(ahead)).wait_send()
        through(done.at[pl.ds(0, 3 * owned)], done_sem).wait_send()

    @pl.when(outer)
    def _():
        through(out_ref.at[:, pl.ds(0, 3 * PLANE)], done_sem).wait_recv()

    @pl.when(inner)
    def _():
        through(out_ref.at[:, pl.ds(0, 2 * PLANE)], done_sem).wait_recv()


def close_kernel(moved_ref, logs_ref, out_hbm, log_hbm, log_ref, sem):
    copies = [
        pltpu.make_async_copy(moved_ref.at[w], out_hbm.at[w], sem.at[w]) for w in range(moved_ref.shape[0])
    ]
    for copy in copies:
        copy.start()
    log_ref[...] = logs_ref[:, 0]
    copies.append(pltpu.make_async_copy(log_ref, log_hbm, sem.at[len(copies)]))
    copies[-1].start()
    for copy in copies:
        copy.wait()


def on_device(n, chol_full, chol_half, green, gauss, orbitals):
    walkers, local_rows, nocc = green.shape
    owned, width, _ = orbitals.shape
    vectors = chol_half.shape[0]
    tiles = local_rows // TILE
    vmem = pl.BlockSpec(memory_space=pltpu.VMEM)
    hbm = pl.BlockSpec(memory_space=pl.ANY)
    dma = pltpu.SemaphoreType.DMA
    split = (owned, n, tiles, TILE, nocc)
    params = pltpu.CompilerParams(collective_id=0, has_side_effects=True, vmem_limit_bytes=60 << 20)
    shared = [
        pltpu.VMEM((tiles, vectors, TILE, width), jnp.bfloat16),
        pltpu.VMEM((vectors, local_rows, nocc), jnp.bfloat16),
        pltpu.VMEM((walkers, local_rows, nocc), jnp.bfloat16),
    ]
    arrays = (chol_full, chol_half, green, gauss.reshape(n, owned, vectors), orbitals.reshape(split))
    if n == 4 * PLANE and orbitals.size * orbitals.dtype.itemsize <= OWN_LIMIT:
        line = walkers // PLANE
        planes = n // PLANE
        moved, logs = pl.pallas_call(
            functools.partial(line_kernel, n),
            out_shape=(pltpu.VMEM(split, jnp.bfloat16), pltpu.VMEM((owned, LANES), jnp.float32)),
            in_specs=[hbm] * 5,
            out_specs=(vmem, vmem),
            scratch_shapes=[
                *shared,
                pltpu.VMEM((n, owned, vectors), jnp.float32),
                pltpu.VMEM(split, jnp.bfloat16),
                pltpu.VMEM((PLANE, line, vectors), jnp.float32),
                pltpu.VMEM((PLANE, line, vectors), jnp.float32),
                pltpu.VMEM((2, line, vectors), jnp.float32),
                pltpu.VMEM((2, line, vectors), jnp.float32),
                pltpu.VMEM((line, vectors), jnp.float32),
                pltpu.VMEM((planes, owned, LANES), jnp.float32),
                pltpu.VMEM((PLANE, line, vectors), jnp.bfloat16),
                pltpu.VMEM((tiles, walkers, TILE, width), jnp.bfloat16),
                pltpu.VMEM((line, PLANE, tiles, TILE, width), jnp.bfloat16),
                pltpu.VMEM((planes,) + split, jnp.bfloat16),
                pltpu.VMEM((line, PLANE, tiles, TILE, nocc), jnp.bfloat16),
                pltpu.VMEM((owned, PLANE, tiles, TILE, width), jnp.bfloat16),
                dma((1,)), dma((4,)), dma((2,)), dma((2, 2)), dma((2,)), dma((1,)), dma((planes,)),
                dma((1,)), dma((planes - 1, CHUNKS * owned)), dma((2,)), dma((2,)),
                pltpu.SemaphoreType.REGULAR, pltpu.SemaphoreType.REGULAR,
            ],
            compiler_params=params,
        )(*arrays)
        moved, logs = pl.pallas_call(
            close_kernel,
            out_shape=(
                jax.ShapeDtypeStruct(split, jnp.bfloat16),
                jax.ShapeDtypeStruct((owned,), jnp.float32),
            ),
            in_specs=[pl.BlockSpec(memory_space=pltpu.VMEM)] * 2,
            out_specs=(hbm, hbm),
            scratch_shapes=[pltpu.VMEM((owned,), jnp.float32), dma((owned + 1,))],
            compiler_params=pltpu.CompilerParams(vmem_limit_bytes=1 << 20),
        )(moved, logs)
        return moved.reshape(orbitals.shape), logs
    else:
        moved, logs = pl.pallas_call(
            functools.partial(direct_kernel, n),
            out_shape=(
                jax.ShapeDtypeStruct(split, jnp.bfloat16),
                jax.ShapeDtypeStruct((owned, LANES), jnp.float32),
            ),
            in_specs=[hbm, hbm, hbm, vmem, vmem],
            out_specs=(vmem, vmem),
            scratch_shapes=[
                *shared,
                pltpu.VMEM((n, owned, vectors), jnp.float32),
                pltpu.VMEM((n, owned, vectors), jnp.float32),
                pltpu.VMEM((owned, vectors), jnp.float32),
                pltpu.VMEM((n, owned, vectors), jnp.float32),
                pltpu.VMEM((tiles, walkers, TILE, width), jnp.bfloat16),
                pltpu.VMEM((tiles, owned, n * TILE, width), jnp.bfloat16),
                dma((tiles,)), dma((2,)), dma((n,)), dma((n,)), dma((n,)), dma((n,)),
                dma((tiles, n)), dma((tiles, n)),
            ],
            compiler_params=params,
        )(*arrays)
    return moved.reshape(orbitals.shape), logs[:, 0]


def solution(mesh):
    placed = (
        P(None, "chol", None),
        P(None, "chol", None),
        P("grp", "chol", None),
        P("grp", None),
        P(("grp", "chol"), None, None),
    )
    return jax.shard_map(
        functools.partial(on_device, mesh.shape["chol"]),
        mesh=mesh,
        in_specs=placed,
        out_specs=(P(("grp", "chol"), None, None), P(("grp", "chol"))),
        check_vma=False,
    )
```

```python
import functools

import jax
import jax.numpy as jnp
from jax import lax
from jax.experimental import pallas as pl
from jax.experimental.pallas import tpu as pltpu
from jax.sharding import PartitionSpec as P

TILE = 16
LANES = 128
PLANE = 4
OWN_LIMIT = 2 << 20
CHUNKS = 4
FIRST = 2
SECOND = 4
THIRD = 6


def remote(src, dst, send, recv, peer):
    return pltpu.make_async_remote_copy(
        src_ref=src,
        dst_ref=dst,
        send_sem=send,
        recv_sem=recv,
        device_id={"chol": peer},
        device_id_type=pl.DeviceIdType.MESH,
    )


def direct_kernel(
    n, chol_hbm, half_hbm, green_hbm, gauss_ref, orb_ref,
    out_ref, log_ref,
    chol, half, green, part, part_in, fields_own, fields_in, send, recv,
    load_sem, aux_sem, part_send, part_recv, field_send, field_recv, pot_send, pot_recv,
):
    me = lax.axis_index("chol")
    owned = part.shape[1]
    tiles = chol.shape[0]
    width = chol.shape[3]

    half_copy = pltpu.make_async_copy(half_hbm, half, aux_sem.at[0])
    green_copy = pltpu.make_async_copy(green_hbm, green, aux_sem.at[1])
    half_copy.start()
    green_copy.start()
    loads = [
        pltpu.make_async_copy(chol_hbm.at[:, pl.ds(t * TILE, TILE), :], chol.at[t], load_sem.at[t])
        for t in range(tiles)
    ]
    for load in loads:
        load.start()

    barrier = pltpu.get_barrier_semaphore()

    def greet(k, _):
        pl.semaphore_signal(
            barrier, inc=1, device_id={"chol": lax.rem(me + k, n)}, device_id_type=pl.DeviceIdType.MESH
        )
        return 0

    lax.fori_loop(1, n, greet, 0)

    half_copy.wait()
    green_copy.wait()

    def bias(t, acc):
        rows = pl.ds(pl.multiple_of(t * TILE, TILE), TILE)
        left = jnp.swapaxes(green[:, rows, :], 0, 1)
        right = jnp.swapaxes(half[:, rows, :], 0, 1)
        for r in range(TILE):
            acc += lax.dot_general(
                left[r], right[r], (((1,), (1,)), ((), ())), preferred_element_type=jnp.float32
            )
        return acc

    total = lax.fori_loop(0, tiles, bias, jnp.zeros((n * owned, half.shape[0]), jnp.float32))
    for d in range(n):
        part[d] = total[d * owned:(d + 1) * owned]
    pl.semaphore_wait(barrier, n - 1)

    def peer_of(k):
        return lax.rem(me + k, n)

    def push_part(k, _):
        to = peer_of(k)
        remote(part.at[to], part_in.at[me], part_send.at[to], part_recv.at[me], to).start()
        return 0

    lax.fori_loop(1, n, push_part, 0)
    part_in[me] = part[me]

    def wait_part(k, _):
        peer = peer_of(k)
        copy = remote(part.at[peer], part_in.at[peer], part_send.at[peer], part_recv.at[peer], peer)
        copy.wait_recv()
        return 0

    lax.fori_loop(1, n, wait_part, 0)
    vbias = jnp.sum(part_in[...], axis=0)
    gauss = gauss_ref[me]
    xbar = jnp.clip(-0.3 * vbias, -1.0, 1.0)
    log_ref[...] = jnp.broadcast_to(
        jnp.sum(gauss * xbar - 0.5 * xbar * xbar, axis=1, keepdims=True), log_ref.shape
    )
    mine = gauss - xbar
    fields_own[...] = mine
    fields_in[me] = mine

    def push_field(k, _):
        to = peer_of(k)
        remote(fields_own, fields_in.at[me], field_send.at[to], field_recv.at[me], to).start()
        return 0

    lax.fori_loop(1, n, push_field, 0)

    def wait_field(k, _):
        peer = peer_of(k)
        remote(fields_own, fields_in.at[peer], field_send.at[peer], field_recv.at[peer], peer).wait_recv()
        return 0

    lax.fori_loop(1, n, wait_field, 0)
    fields = jnp.concatenate([fields_in[d] for d in range(n)], axis=0).astype(jnp.bfloat16)

    def walkers_of(d):
        return pl.ds(d * owned, owned)

    def rows_of(d):
        return pl.ds(pl.multiple_of(d * TILE, TILE), TILE)

    for t in range(tiles):
        loads[t].wait()

        def strip(c, _):
            cols = pl.ds(pl.multiple_of(c * LANES, LANES), LANES)
            block = jnp.swapaxes(chol[t, :, :, cols], 0, 1)
            pots = [
                (jnp.dot(fields, block[r], preferred_element_type=jnp.float32) * 0.3).astype(jnp.bfloat16)
                for r in range(TILE)
            ]
            send[t, :, :, cols] = jnp.swapaxes(jnp.stack(pots, axis=0), 0, 1)
            return 0

        lax.fori_loop(0, width // LANES, strip, 0)

        def push_pot(k, _):
            to = peer_of(k)
            remote(
                send.at[t, walkers_of(to)], recv.at[t, :, rows_of(me), :],
                pot_send.at[t, to], pot_recv.at[t, me], to,
            ).start()
            return 0

        lax.fori_loop(1, n, push_pot, 0)
        recv[t, :, rows_of(me), :] = send[t, walkers_of(me)]

    for t in range(tiles):

        def wait_pot(k, _):
            peer = peer_of(k)
            remote(
                send.at[t, walkers_of(peer)], recv.at[t, :, rows_of(peer), :],
                pot_send.at[t, peer], pot_recv.at[t, peer], peer,
            ).wait_recv()
            return 0

        lax.fori_loop(1, n, wait_pot, 0)

        def advance(w, _):
            orbit = orb_ref[w].reshape(width, orb_ref.shape[-1])
            for first in range(0, n, 16):
                span = min(16, n - first)
                moved = jnp.dot(
                    recv[t, w, first * TILE:(first + span) * TILE, :], orbit,
                    preferred_element_type=jnp.float32,
                ).reshape(span, TILE, orbit.shape[-1])
                old = orb_ref[w, first:first + span, t].astype(jnp.float32)
                out_ref[w, first:first + span, t] = (old + moved).astype(jnp.bfloat16)
            return 0

        lax.fori_loop(0, owned, advance, 0)

    def drain(k, _):
        peer = peer_of(k)
        remote(part.at[peer], part_in.at[peer], part_send.at[peer], part_recv.at[peer], peer).wait_send()
        remote(fields_own, fields_in.at[peer], field_send.at[peer], field_recv.at[peer], peer).wait_send()
        for t in range(tiles):
            remote(
                send.at[t, walkers_of(peer)], recv.at[t, :, rows_of(peer), :],
                pot_send.at[t, peer], pot_recv.at[t, peer], peer,
            ).wait_send()
        return 0

    lax.fori_loop(1, n, drain, 0)


def line_kernel(
    n, chol_hbm, half_hbm, green_hbm, gauss_hbm, orb_hbm,
    out_ref, log_ref,
    chol, half, green, gauss_ref, orb_ref, part, part_in, partial, partial_in, bias_ref, log_all, fields_ref,
    send, recv, guest, done, lent,
    load_sem, aux_sem, part_sem, sum_sem, field_sem, pot_send, pot_recv, orb_send, orb_recv,
    lend_sem, done_sem, news, ready,
):
    me = lax.axis_index("chol")
    owned = orb_ref.shape[0]
    tiles = chol.shape[0]
    width = chol.shape[3]
    nocc = orb_ref.shape[-1]
    planes = n // PLANE
    line = planes * owned
    chunks = CHUNKS * owned
    span = n // CHUNKS

    z = me // PLANE
    seat = lax.rem(me, PLANE)
    side = z // 2
    far = 1 - side
    near_in, near_out = 1 + side, 3 * side
    far_in, far_out = 1 + far, 3 * far
    ahead = z + 1 - 2 * side
    buddy = near_in + near_out - z
    inner = z == near_in
    outer = z == near_out

    barrier = pltpu.get_barrier_semaphore()

    partner = seat + 1 - 2 * lax.rem(seat, 2)
    beside = lax.rem(seat + 2, PLANE)
    diagonal = lax.rem(partner + 2, PLANE)
    others = (beside, diagonal, partner)

    def greet(peer):
        pl.semaphore_signal(barrier, inc=1, device_id={"chol": peer}, device_id_type=pl.DeviceIdType.MESH)

    def tell(sem, peer):
        pl.semaphore_signal(sem, inc=1, device_id={"chol": peer}, device_id_type=pl.DeviceIdType.MESH)

    @pl.when(inner)
    def _():
        greet(ahead * PLANE + seat)
        greet(buddy * PLANE + seat)

    @pl.when(outer)
    def _():
        for s in others:
            greet(z * PLANE + s)

    half_copy = pltpu.make_async_copy(half_hbm, half, aux_sem.at[0])
    green_copy = pltpu.make_async_copy(green_hbm, green, aux_sem.at[1])
    gauss_copy = pltpu.make_async_copy(gauss_hbm, gauss_ref, aux_sem.at[2])
    orb_copy = pltpu.make_async_copy(orb_hbm, orb_ref, aux_sem.at[3])
    for copy in (green_copy, half_copy, gauss_copy):
        copy.start()
    loads = [
        pltpu.make_async_copy(chol_hbm.at[:, pl.ds(t * TILE, TILE), :], chol.at[t], load_sem.at[0])
        for t in range(tiles)
    ]
    @pl.when(inner)
    def _():
        pl.semaphore_wait(barrier, 1)

    @pl.when(outer)
    def _():
        pl.semaphore_wait(barrier, PLANE)
        for s in others:
            tell(news, z * PLANE + s)

    def at(plane):
        return plane * PLANE + seat

    def piece(ref, c):
        return ref.at[c // CHUNKS, pl.ds(lax.rem(c, CHUNKS) * span, span)]

    def landed(plane, to, c):
        return orb_recv.at[lax.rem(plane - to + planes, planes) - 1, c]

    def own_orbit(c):
        return remote(piece(orb_hbm, c), piece(guest.at[z], c), orb_send.at[0], landed(z, ahead, c), at(ahead))

    def orbit_copy(plane, to, c):
        there = piece(guest.at[plane], c)
        return remote(there, there, orb_send.at[0], landed(plane, to, c), at(to))

    def orbit_on(c):
        return orbit_copy(near_out, ahead, c)

    def orbit_back(plane, c):
        return orbit_copy(plane, buddy, c)

    def await_orbit(plane, c):
        there = piece(guest.at[plane], c)
        remote(there, there, orb_send.at[0], landed(plane, z, c), at(ahead)).wait_recv()

    def start_own(first, last):
        def step(c, _):
            own_orbit(c).start()
            return 0

        lax.fori_loop(first, last, step, 0)

    def pass_on(first, last):
        @pl.when(inner)
        def _():
            def step(c, _):
                await_orbit(near_out, c)
                orbit_on(c).start()
                return 0

            lax.fori_loop(first, last, step, 0)

    def pass_back(first, last):
        @pl.when(inner)
        def _():
            def step(c, _):
                await_orbit(far_in, c)
                orbit_back(far_in, c).start()
                return 0

            lax.fori_loop(first, last, step, 0)

    start_own(0, FIRST)

    @pl.when(outer)
    def _():
        pl.semaphore_wait(news, PLANE - 1)
        tell(ready, at(ahead))


    half_copy.wait()
    green_copy.wait()
    for copy in (*loads, orb_copy):
        copy.start()
    gauss_copy.wait()

    def bias(t, acc):
        rows = pl.ds(pl.multiple_of(t * TILE, TILE), TILE)
        left = jnp.swapaxes(green[:, rows, :], 0, 1)
        right = jnp.swapaxes(half[:, rows, :], 0, 1)
        for r in range(TILE):
            acc += lax.dot_general(
                left[r], right[r], (((1,), (1,)), ((), ())), preferred_element_type=jnp.float32
            )
        return acc

    total = lax.fori_loop(0, tiles, bias, jnp.zeros((n * owned, half.shape[0]), jnp.float32))
    for d in range(n):
        plane, s = divmod(d, PLANE)
        part[s, plane * owned:(plane + 1) * owned] = total[d * owned:(d + 1) * owned]

    @pl.when(inner)
    def _():
        pl.semaphore_wait(ready, 1)

    def part_copy(there, source):
        return remote(part.at[there], part_in.at[source], part_sem.at[0], part_sem.at[1], z * PLANE + there)

    def field_copy(there):
        mine = fields_ref.at[seat]
        return remote(mine, mine, field_sem.at[0], field_sem.at[1], z * PLANE + there)

    def gathered(ref, sem):
        every = ref.at[pl.ds(0, PLANE - 1)]
        return remote(every, every, sem.at[0], sem.at[1], at(ahead))

    def sum_copy(k, to):
        return remote(partial.at[k], partial_in.at[k], sum_sem.at[0, 0], sum_sem.at[1, k], to)

    def total_copy():
        return remote(bias_ref, bias_ref, sum_sem.at[0, 1], sum_sem.at[1, 0], at(buddy))

    for s in others:
        part_copy(s, seat).start()
    part_in[seat] = part[seat]

    @pl.when(inner)
    def _():
        start_own(FIRST, SECOND)

    pass_back(0, FIRST)
    gathered(part_in, part_sem).wait_recv()
    partial[0] = jnp.sum(part_in[...], axis=0)

    @pl.when(outer)
    def _():
        sum_copy(0, at(ahead)).start()
        start_own(FIRST, chunks)
        total_copy().wait_recv()

    @pl.when(inner)
    def _():
        sum_copy(0, at(ahead)).wait_recv()
        partial[1] = partial[0] + partial_in[0]
        sum_copy(1, at(ahead)).start()
        start_own(SECOND, THIRD)
        pass_back(FIRST, FIRST + 1)
        sum_copy(1, at(ahead)).wait_recv()
        bias_ref[...] = partial[1] + partial_in[1]
        total_copy().start()
        start_own(THIRD, chunks)

    pass_back(FIRST + 1, SECOND)
    vbias = bias_ref[...]
    gauss = jnp.concatenate([gauss_ref[plane * PLANE + seat] for plane in range(planes)], axis=0)
    xbar = jnp.clip(-0.3 * vbias, -1.0, 1.0)
    logs = jnp.sum(gauss * xbar - 0.5 * xbar * xbar, axis=1, keepdims=True)
    log_all[...] = jnp.broadcast_to(logs, (line, LANES)).reshape(log_all.shape)
    log_ref[...] = log_all[z]
    fields_ref[seat] = (gauss - xbar).astype(jnp.bfloat16)

    for s in others:
        field_copy(s).start()
    gathered(fields_ref, field_sem).wait_recv()
    pltpu.make_async_copy(chol, chol, load_sem.at[0]).wait()
    fields = fields_ref[...].reshape(n * owned, fields_ref.shape[-1])

    order = (
        jnp.where(inner, far_in, near_in), jnp.where(inner, far_out, far_in),
        jnp.where(inner, near_out, far_out), z,
    )

    def pot_copy(t, plane, there, source):
        return remote(
            send.at[t, pl.ds(there * line + plane * owned, owned)],
            recv.at[pl.ds(plane * owned, owned), source, t],
            pot_send.at[0], pot_recv.at[plane], z * PLANE + there,
        )

    def push(t, plane):
        for s in others:
            pot_copy(t, plane, s, seat).start()

    def await_pots(plane):
        every = recv.at[pl.ds(plane * owned, owned), pl.ds(0, PLANE - 1)]
        remote(every, every, pot_send.at[0], pot_recv.at[plane], z * PLANE + partner).wait_recv()

    def fill(t):
        def strip(c, _):
            cols = pl.ds(pl.multiple_of(c * LANES, LANES), LANES)
            block = jnp.swapaxes(chol[t, :, :, cols], 0, 1)
            pots = [
                (jnp.dot(fields, block[r], preferred_element_type=jnp.float32) * 0.3).astype(jnp.bfloat16)
                for r in range(TILE)
            ]
            send[t, :, :, cols] = jnp.swapaxes(jnp.stack(pots, axis=0), 0, 1)
            return 0

        half_way = width // LANES // 2
        lax.fori_loop(0, half_way, strip, 0)
        pass_back(SECOND + 2 * t, SECOND + 2 * t + 1)
        lax.fori_loop(half_way, width // LANES, strip, 0)
        recv[:, seat, t] = send[t, pl.ds(seat * line, line)]

    def forward_far(first, last):
        def step(c, _):
            await_orbit(far_out, c)

            @pl.when(inner)
            def _():
                orbit_back(far_out, c).start()

            return 0

        lax.fori_loop(first, last, step, 0)

    for t in range(tiles):
        fill(t)
        push(t, order[0])
        pass_back(SECOND + 2 * t + 1, SECOND + 2 * t + 2)
    held = SECOND + 2 * tiles

    for plane in order[1:]:
        for t in range(tiles):
            push(t, plane)

    def lend():
        return remote(recv.at[pl.ds(buddy * owned, owned)], lent, lend_sem.at[0], lend_sem.at[1], at(buddy))

    pass_on(0, held)
    for c in range(held, chunks):
        pass_back(c, c + 1)
        pass_on(c, c + 1)
    @pl.when(outer)
    def _():
        await_pots(near_in)
        lend().start()

        def arrived(c, _):
            await_orbit(far_in, c)
            return 0

        lax.fori_loop(0, chunks, arrived, 0)

    def hand_back(plane, w):
        return remote(
            done.at[plane * owned + w], out_ref.at[w, pl.ds(z * PLANE, PLANE)],
            done_sem.at[0], done_sem.at[1], at(plane),
        )

    def rows_done(left, orbit, old):
        moved = jnp.dot(
            left.reshape(-1, width), orbit.reshape(width, nocc), preferred_element_type=jnp.float32
        )
        return (old.astype(jnp.float32) + moved.reshape(old.shape)).astype(jnp.bfloat16)

    here = pl.ds(z * PLANE, PLANE)

    def serve(plane, first, last):
        def step(w, _):
            done[plane * owned + w] = rows_done(
                recv[plane * owned + w], guest[plane, w], guest[plane, w, here]
            )
            hand_back(plane, w).start()
            return 0

        lax.fori_loop(first, last, step, 0)

    forward_far(0, CHUNKS)
    await_pots(far_in)
    @pl.when(outer)
    def _():
        serve(far_in, 0, owned)

    forward_far(CHUNKS, 2 * CHUNKS)
    await_pots(far_out)
    serve(far_out, 0, 2)
    for w in range(2, owned):
        forward_far(CHUNKS * w, CHUNKS * (w + 1))
        serve(far_out, w, w + 1)

    @pl.when(inner)
    def _():
        serve(far_in, 0, owned)

    @pl.when(inner)
    def _():
        await_pots(near_out)
        serve(near_out, 0, owned)

    await_pots(z)
    orb_copy.wait()

    def advance(w, _):
        out_ref[w, here] = rows_done(recv[z * owned + w], orb_ref[w], orb_ref[w, here])
        return 0

    lax.fori_loop(0, owned, advance, 0)

    @pl.when(inner)
    def _():
        lend().wait_recv()
        there = pl.ds(near_out * PLANE, PLANE)

        def borrow(w, _):
            out_ref[w, there] = rows_done(lent[w], orb_ref[w], orb_ref[w, there])
            return 0

        lax.fori_loop(0, owned, borrow, 0)

    gathered(part_in, part_sem).wait_send()
    gathered(fields_ref, field_sem).wait_send()
    every = send.at[:, pl.ds(0, (PLANE - 1) * line)]
    remote(every, every, pot_send.at[0], pot_recv.at[z], at(ahead)).wait_send()

    def through(ref, sem):
        return remote(ref, ref, sem.at[0], sem.at[1], at(ahead))

    @pl.when(outer)
    def _():
        sum_copy(0, at(ahead)).wait_send()
        lend().wait_send()
        remote(guest.at[0], guest.at[0], orb_send.at[0], orb_recv.at[0, 0], at(ahead)).wait_send()
        through(done.at[pl.ds(0, 2 * owned)], done_sem).wait_send()

    @pl.when(inner)
    def _():
        sum_copy(1, at(ahead)).wait_send()
        total_copy().wait_send()
        remote(guest, guest, orb_send.at[0], orb_recv.at[0, 0], at(ahead)).wait_send()
        through(done.at[pl.ds(0, 3 * owned)], done_sem).wait_send()

    @pl.when(outer)
    def _():
        through(out_ref.at[:, pl.ds(0, 3 * PLANE)], done_sem).wait_recv()

    @pl.when(inner)
    def _():
        through(out_ref.at[:, pl.ds(0, 2 * PLANE)], done_sem).wait_recv()


def close_kernel(moved_ref, logs_ref, out_hbm, log_hbm, log_ref, sem):
    copies = [
        pltpu.make_async_copy(moved_ref.at[w], out_hbm.at[w], sem.at[w]) for w in range(moved_ref.shape[0])
    ]
    for copy in copies:
        copy.start()
    log_ref[...] = logs_ref[:, 0]
    copies.append(pltpu.make_async_copy(log_ref, log_hbm, sem.at[len(copies)]))
    copies[-1].start()
    for copy in copies:
        copy.wait()


def on_device(n, chol_full, chol_half, green, gauss, orbitals):
    walkers, local_rows, nocc = green.shape
    owned, width, _ = orbitals.shape
    vectors = chol_half.shape[0]
    tiles = local_rows // TILE
    vmem = pl.BlockSpec(memory_space=pltpu.VMEM)
    hbm = pl.BlockSpec(memory_space=pl.ANY)
    dma = pltpu.SemaphoreType.DMA
    split = (owned, n, tiles, TILE, nocc)
    params = pltpu.CompilerParams(collective_id=0, has_side_effects=True, vmem_limit_bytes=60 << 20)
    shared = [
        pltpu.VMEM((tiles, vectors, TILE, width), jnp.bfloat16),
        pltpu.VMEM((vectors, local_rows, nocc), jnp.bfloat16),
        pltpu.VMEM((walkers, local_rows, nocc), jnp.bfloat16),
    ]
    arrays = (chol_full, chol_half, green, gauss.reshape(n, owned, vectors), orbitals.reshape(split))
    if n == 4 * PLANE and orbitals.size * orbitals.dtype.itemsize <= OWN_LIMIT:
        line = walkers // PLANE
        planes = n // PLANE
        moved, logs = pl.pallas_call(
            functools.partial(line_kernel, n),
            out_shape=(pltpu.VMEM(split, jnp.bfloat16), pltpu.VMEM((owned, LANES), jnp.float32)),
            in_specs=[hbm] * 5,
            out_specs=(vmem, vmem),
            scratch_shapes=[
                *shared,
                pltpu.VMEM((n, owned, vectors), jnp.float32),
                pltpu.VMEM(split, jnp.bfloat16),
                pltpu.VMEM((PLANE, line, vectors), jnp.float32),
                pltpu.VMEM((PLANE, line, vectors), jnp.float32),
                pltpu.VMEM((2, line, vectors), jnp.float32),
                pltpu.VMEM((2, line, vectors), jnp.float32),
                pltpu.VMEM((line, vectors), jnp.float32),
                pltpu.VMEM((planes, owned, LANES), jnp.float32),
                pltpu.VMEM((PLANE, line, vectors), jnp.bfloat16),
                pltpu.VMEM((tiles, walkers, TILE, width), jnp.bfloat16),
                pltpu.VMEM((line, PLANE, tiles, TILE, width), jnp.bfloat16),
                pltpu.VMEM((planes,) + split, jnp.bfloat16),
                pltpu.VMEM((line, PLANE, tiles, TILE, nocc), jnp.bfloat16),
                pltpu.VMEM((owned, PLANE, tiles, TILE, width), jnp.bfloat16),
                dma((1,)), dma((4,)), dma((2,)), dma((2, 2)), dma((2,)), dma((1,)), dma((planes,)),
                dma((1,)), dma((planes - 1, CHUNKS * owned)), dma((2,)), dma((2,)),
                pltpu.SemaphoreType.REGULAR, pltpu.SemaphoreType.REGULAR,
            ],
            compiler_params=params,
        )(*arrays)
        moved, logs = pl.pallas_call(
            close_kernel,
            out_shape=(
                jax.ShapeDtypeStruct(split, jnp.bfloat16),
                jax.ShapeDtypeStruct((owned,), jnp.float32),
            ),
            in_specs=[pl.BlockSpec(memory_space=pltpu.VMEM)] * 2,
            out_specs=(hbm, hbm),
            scratch_shapes=[pltpu.VMEM((owned,), jnp.float32), dma((owned + 1,))],
            compiler_params=pltpu.CompilerParams(vmem_limit_bytes=1 << 20),
        )(moved, logs)
        return moved.reshape(orbitals.shape), logs
    else:
        moved, logs = pl.pallas_call(
            functools.partial(direct_kernel, n),
            out_shape=(
                jax.ShapeDtypeStruct(split, jnp.bfloat16),
                jax.ShapeDtypeStruct((owned, LANES), jnp.float32),
            ),
            in_specs=[hbm, hbm, hbm, vmem, vmem],
            out_specs=(vmem, vmem),
            scratch_shapes=[
                *shared,
                pltpu.VMEM((n, owned, vectors), jnp.float32),
                pltpu.VMEM((n, owned, vectors), jnp.float32),
                pltpu.VMEM((owned, vectors), jnp.float32),
                pltpu.VMEM((n, owned, vectors), jnp.float32),
                pltpu.VMEM((tiles, walkers, TILE, width), jnp.bfloat16),
                pltpu.VMEM((tiles, owned, n * TILE, width), jnp.bfloat16),
                dma((tiles,)), dma((2,)), dma((n,)), dma((n,)), dma((n,)), dma((n,)),
                dma((tiles, n)), dma((tiles, n)),
            ],
            compiler_params=params,
        )(*arrays)
    return moved.reshape(orbitals.shape), logs[:, 0]


def solution(mesh):
    placed = (
        P(None, "chol", None),
        P(None, "chol", None),
        P("grp", "chol", None),
        P("grp", None),
        P(("grp", "chol"), None, None),
    )
    return jax.shard_map(
        functools.partial(on_device, mesh.shape["chol"]),
        mesh=mesh,
        in_specs=placed,
        out_specs=(P(("grp", "chol"), None, None), P(("grp", "chol"))),
        check_vma=False,
    )
```

```python
import functools

import jax
import jax.numpy as jnp
from jax import lax
from jax.experimental import pallas as pl
from jax.experimental.pallas import tpu as pltpu
from jax.sharding import PartitionSpec as P

TILE = 16
LANES = 128
PLANE = 4
OWN_LIMIT = 2 << 20
CHUNKS = 4
HALVES = 2
FIRST = 2
SECOND = 4
THIRD = 6


def remote(src, dst, send, recv, peer):
    return pltpu.make_async_remote_copy(
        src_ref=src,
        dst_ref=dst,
        send_sem=send,
        recv_sem=recv,
        device_id={"chol": peer},
        device_id_type=pl.DeviceIdType.MESH,
    )


def direct_kernel(
    n, chol_hbm, half_hbm, green_hbm, gauss_ref, orb_ref,
    out_ref, log_ref,
    chol, half, green, part, part_in, fields_own, fields_in, send, recv,
    load_sem, aux_sem, part_send, part_recv, field_send, field_recv, pot_send, pot_recv,
):
    me = lax.axis_index("chol")
    owned = part.shape[1]
    tiles = chol.shape[0]
    width = chol.shape[3]

    half_copy = pltpu.make_async_copy(half_hbm, half, aux_sem.at[0])
    green_copy = pltpu.make_async_copy(green_hbm, green, aux_sem.at[1])
    half_copy.start()
    green_copy.start()
    loads = [
        pltpu.make_async_copy(chol_hbm.at[:, pl.ds(t * TILE, TILE), :], chol.at[t], load_sem.at[t])
        for t in range(tiles)
    ]
    for load in loads:
        load.start()

    barrier = pltpu.get_barrier_semaphore()

    def greet(k, _):
        pl.semaphore_signal(
            barrier, inc=1, device_id={"chol": lax.rem(me + k, n)}, device_id_type=pl.DeviceIdType.MESH
        )
        return 0

    lax.fori_loop(1, n, greet, 0)

    half_copy.wait()
    green_copy.wait()

    def bias(t, acc):
        rows = pl.ds(pl.multiple_of(t * TILE, TILE), TILE)
        left = jnp.swapaxes(green[:, rows, :], 0, 1)
        right = jnp.swapaxes(half[:, rows, :], 0, 1)
        for r in range(TILE):
            acc += lax.dot_general(
                left[r], right[r], (((1,), (1,)), ((), ())), preferred_element_type=jnp.float32
            )
        return acc

    total = lax.fori_loop(0, tiles, bias, jnp.zeros((n * owned, half.shape[0]), jnp.float32))
    for d in range(n):
        part[d] = total[d * owned:(d + 1) * owned]
    pl.semaphore_wait(barrier, n - 1)

    def peer_of(k):
        return lax.rem(me + k, n)

    def push_part(k, _):
        to = peer_of(k)
        remote(part.at[to], part_in.at[me], part_send.at[to], part_recv.at[me], to).start()
        return 0

    lax.fori_loop(1, n, push_part, 0)
    part_in[me] = part[me]

    def wait_part(k, _):
        peer = peer_of(k)
        copy = remote(part.at[peer], part_in.at[peer], part_send.at[peer], part_recv.at[peer], peer)
        copy.wait_recv()
        return 0

    lax.fori_loop(1, n, wait_part, 0)
    vbias = jnp.sum(part_in[...], axis=0)
    gauss = gauss_ref[me]
    xbar = jnp.clip(-0.3 * vbias, -1.0, 1.0)
    log_ref[...] = jnp.broadcast_to(
        jnp.sum(gauss * xbar - 0.5 * xbar * xbar, axis=1, keepdims=True), log_ref.shape
    )
    mine = gauss - xbar
    fields_own[...] = mine
    fields_in[me] = mine

    def push_field(k, _):
        to = peer_of(k)
        remote(fields_own, fields_in.at[me], field_send.at[to], field_recv.at[me], to).start()
        return 0

    lax.fori_loop(1, n, push_field, 0)

    def wait_field(k, _):
        peer = peer_of(k)
        remote(fields_own, fields_in.at[peer], field_send.at[peer], field_recv.at[peer], peer).wait_recv()
        return 0

    lax.fori_loop(1, n, wait_field, 0)
    fields = jnp.concatenate([fields_in[d] for d in range(n)], axis=0).astype(jnp.bfloat16)

    def walkers_of(d):
        return pl.ds(d * owned, owned)

    def rows_of(d):
        return pl.ds(pl.multiple_of(d * TILE, TILE), TILE)

    for t in range(tiles):
        loads[t].wait()

        def strip(c, _):
            cols = pl.ds(pl.multiple_of(c * LANES, LANES), LANES)
            block = jnp.swapaxes(chol[t, :, :, cols], 0, 1)
            pots = [
                (jnp.dot(fields, block[r], preferred_element_type=jnp.float32) * 0.3).astype(jnp.bfloat16)
                for r in range(TILE)
            ]
            send[t, :, :, cols] = jnp.swapaxes(jnp.stack(pots, axis=0), 0, 1)
            return 0

        lax.fori_loop(0, width // LANES, strip, 0)

        def push_pot(k, _):
            to = peer_of(k)
            remote(
                send.at[t, walkers_of(to)], recv.at[t, :, rows_of(me), :],
                pot_send.at[t, to], pot_recv.at[t, me], to,
            ).start()
            return 0

        lax.fori_loop(1, n, push_pot, 0)
        recv[t, :, rows_of(me), :] = send[t, walkers_of(me)]

    for t in range(tiles):

        def wait_pot(k, _):
            peer = peer_of(k)
            remote(
                send.at[t, walkers_of(peer)], recv.at[t, :, rows_of(peer), :],
                pot_send.at[t, peer], pot_recv.at[t, peer], peer,
            ).wait_recv()
            return 0

        lax.fori_loop(1, n, wait_pot, 0)

        def advance(w, _):
            orbit = orb_ref[w].reshape(width, orb_ref.shape[-1])
            for first in range(0, n, 16):
                span = min(16, n - first)
                moved = jnp.dot(
                    recv[t, w, first * TILE:(first + span) * TILE, :], orbit,
                    preferred_element_type=jnp.float32,
                ).reshape(span, TILE, orbit.shape[-1])
                old = orb_ref[w, first:first + span, t].astype(jnp.float32)
                out_ref[w, first:first + span, t] = (old + moved).astype(jnp.bfloat16)
            return 0

        lax.fori_loop(0, owned, advance, 0)

    def drain(k, _):
        peer = peer_of(k)
        remote(part.at[peer], part_in.at[peer], part_send.at[peer], part_recv.at[peer], peer).wait_send()
        remote(fields_own, fields_in.at[peer], field_send.at[peer], field_recv.at[peer], peer).wait_send()
        for t in range(tiles):
            remote(
                send.at[t, walkers_of(peer)], recv.at[t, :, rows_of(peer), :],
                pot_send.at[t, peer], pot_recv.at[t, peer], peer,
            ).wait_send()
        return 0

    lax.fori_loop(1, n, drain, 0)


def line_kernel(
    n, chol_hbm, half_hbm, green_hbm, gauss_hbm, orb_hbm,
    out_ref, log_ref,
    chol, half, green, gauss_ref, orb_ref, part, part_in, partial, partial_in, bias_ref, log_all, fields_ref,
    send, recv, guest, done, lent,
    load_sem, aux_sem, part_sem, sum_sem, field_sem, pot_send, pot_recv, orb_send, orb_recv, half_recv,
    lend_sem, done_sem, news, ready,
):
    me = lax.axis_index("chol")
    owned = orb_ref.shape[0]
    tiles = chol.shape[0]
    width = chol.shape[3]
    nocc = orb_ref.shape[-1]
    planes = n // PLANE
    line = planes * owned
    chunks = CHUNKS * owned

    z = me // PLANE
    seat = lax.rem(me, PLANE)
    side = z // 2
    far = 1 - side
    near_in, near_out = 1 + side, 3 * side
    far_in, far_out = 1 + far, 3 * far
    ahead = z + 1 - 2 * side
    buddy = near_in + near_out - z
    inner = z == near_in
    outer = z == near_out

    barrier = pltpu.get_barrier_semaphore()

    partner = seat + 1 - 2 * lax.rem(seat, 2)
    beside = lax.rem(seat + 2, PLANE)
    diagonal = lax.rem(partner + 2, PLANE)
    others = (beside, diagonal, partner)

    def greet(peer):
        pl.semaphore_signal(barrier, inc=1, device_id={"chol": peer}, device_id_type=pl.DeviceIdType.MESH)

    def tell(sem, peer):
        pl.semaphore_signal(sem, inc=1, device_id={"chol": peer}, device_id_type=pl.DeviceIdType.MESH)

    @pl.when(inner)
    def _():
        greet(ahead * PLANE + seat)
        greet(buddy * PLANE + seat)

    @pl.when(outer)
    def _():
        for s in others:
            greet(z * PLANE + s)

    half_copy = pltpu.make_async_copy(half_hbm, half, aux_sem.at[0])
    green_copy = pltpu.make_async_copy(green_hbm, green, aux_sem.at[1])
    gauss_copy = pltpu.make_async_copy(gauss_hbm, gauss_ref, aux_sem.at[2])
    orb_copy = pltpu.make_async_copy(orb_hbm, orb_ref, aux_sem.at[3])
    for copy in (green_copy, half_copy, gauss_copy):
        copy.start()
    loads = [
        pltpu.make_async_copy(chol_hbm.at[:, pl.ds(t * TILE, TILE), :], chol.at[t], load_sem.at[0])
        for t in range(tiles)
    ]
    @pl.when(inner)
    def _():
        pl.semaphore_wait(barrier, 1)

    @pl.when(outer)
    def _():
        pl.semaphore_wait(barrier, PLANE)
        for s in others:
            tell(news, z * PLANE + s)

    def at(plane):
        return plane * PLANE + seat

    def piece(ref, c, parts):
        span = n // parts
        return ref.at[c // parts, pl.ds(lax.rem(c, parts) * span, span)]

    def own_inner(c):
        there = piece(guest.at[z], c, CHUNKS)
        return remote(piece(orb_hbm, c, CHUNKS), there, orb_send.at[0], orb_recv.at[c], at(ahead))

    def own_outer(c):
        there = piece(guest.at[z], c, HALVES)
        return remote(piece(orb_hbm, c, HALVES), there, orb_send.at[0], half_recv.at[1, c], at(ahead))

    def inner_orbit(c):
        there = piece(guest.at[far_in], c, CHUNKS)
        return remote(there, there, orb_send.at[0], orb_recv.at[c], at(buddy))

    def outer_orbit(plane, k, to, c):
        there = piece(guest.at[plane], c, HALVES)
        return remote(there, there, orb_send.at[0], half_recv.at[k, c], at(to))

    def start_own(first, last, copy=own_inner):
        def step(c, _):
            copy(c).start()
            return 0

        lax.fori_loop(first, last, step, 0)

    def pass_on(first, last):
        @pl.when(inner)
        def _():
            def step(c, _):
                outer_orbit(near_out, 1, ahead, c).wait_recv()
                outer_orbit(near_out, 0, ahead, c).start()
                return 0

            lax.fori_loop(first, last, step, 0)

    def pass_back(first, last):
        @pl.when(inner)
        def _():
            def step(c, _):
                inner_orbit(c).wait_recv()
                inner_orbit(c).start()
                return 0

            lax.fori_loop(first, last, step, 0)

    @pl.when(inner)
    def _():
        start_own(0, FIRST)

    @pl.when(outer)
    def _():
        start_own(0, 1, own_outer)
        pl.semaphore_wait(news, PLANE - 1)
        tell(ready, at(ahead))


    half_copy.wait()
    green_copy.wait()
    for copy in (*loads, orb_copy):
        copy.start()
    gauss_copy.wait()

    def bias(t, acc):
        rows = pl.ds(pl.multiple_of(t * TILE, TILE), TILE)
        left = jnp.swapaxes(green[:, rows, :], 0, 1)
        right = jnp.swapaxes(half[:, rows, :], 0, 1)
        for r in range(TILE):
            acc += lax.dot_general(
                left[r], right[r], (((1,), (1,)), ((), ())), preferred_element_type=jnp.float32
            )
        return acc

    total = lax.fori_loop(0, tiles, bias, jnp.zeros((n * owned, half.shape[0]), jnp.float32))
    for d in range(n):
        plane, s = divmod(d, PLANE)
        part[s, plane * owned:(plane + 1) * owned] = total[d * owned:(d + 1) * owned]

    @pl.when(inner)
    def _():
        pl.semaphore_wait(ready, 1)

    def part_copy(there, source):
        return remote(part.at[there], part_in.at[source], part_sem.at[0], part_sem.at[1], z * PLANE + there)

    def field_copy(there):
        mine = fields_ref.at[seat]
        return remote(mine, mine, field_sem.at[0], field_sem.at[1], z * PLANE + there)

    def gathered(ref, sem):
        every = ref.at[pl.ds(0, PLANE - 1)]
        return remote(every, every, sem.at[0], sem.at[1], at(ahead))

    def sum_copy(k, to):
        return remote(partial.at[k], partial_in.at[k], sum_sem.at[0, 0], sum_sem.at[1, k], to)

    def total_copy():
        return remote(bias_ref, bias_ref, sum_sem.at[0, 1], sum_sem.at[1, 0], at(buddy))

    for s in others:
        part_copy(s, seat).start()
    part_in[seat] = part[seat]

    @pl.when(inner)
    def _():
        start_own(FIRST, SECOND)

    pass_back(0, FIRST)
    gathered(part_in, part_sem).wait_recv()
    partial[0] = jnp.sum(part_in[...], axis=0)

    @pl.when(outer)
    def _():
        sum_copy(0, at(ahead)).start()
        start_own(1, HALVES * owned, own_outer)
        total_copy().wait_recv()

    @pl.when(inner)
    def _():
        sum_copy(0, at(ahead)).wait_recv()
        partial[1] = partial[0] + partial_in[0]
        sum_copy(1, at(ahead)).start()
        start_own(SECOND, THIRD)
        pass_back(FIRST, FIRST + 1)
        sum_copy(1, at(ahead)).wait_recv()
        bias_ref[...] = partial[1] + partial_in[1]
        total_copy().start()
        start_own(THIRD, chunks)

    pass_back(FIRST + 1, SECOND)
    vbias = bias_ref[...]
    gauss = jnp.concatenate([gauss_ref[plane * PLANE + seat] for plane in range(planes)], axis=0)
    xbar = jnp.clip(-0.3 * vbias, -1.0, 1.0)
    logs = jnp.sum(gauss * xbar - 0.5 * xbar * xbar, axis=1, keepdims=True)
    log_all[...] = jnp.broadcast_to(logs, (line, LANES)).reshape(log_all.shape)
    log_ref[...] = log_all[z]
    fields_ref[seat] = (gauss - xbar).astype(jnp.bfloat16)

    for s in others:
        field_copy(s).start()
    gathered(fields_ref, field_sem).wait_recv()
    pltpu.make_async_copy(chol, chol, load_sem.at[0]).wait()
    fields = fields_ref[...].reshape(n * owned, fields_ref.shape[-1])

    order = (
        jnp.where(inner, far_in, near_in), jnp.where(inner, far_out, far_in),
        jnp.where(inner, near_out, far_out), z,
    )

    def pot_copy(t, plane, there, source):
        return remote(
            send.at[t, pl.ds(there * line + plane * owned, owned)],
            recv.at[pl.ds(plane * owned, owned), source, t],
            pot_send.at[0], pot_recv.at[plane], z * PLANE + there,
        )

    def push(t, plane):
        for s in others:
            pot_copy(t, plane, s, seat).start()

    def await_pots(plane):
        every = recv.at[pl.ds(plane * owned, owned), pl.ds(0, PLANE - 1)]
        remote(every, every, pot_send.at[0], pot_recv.at[plane], z * PLANE + partner).wait_recv()

    def fill(t):
        def strip(c, _):
            cols = pl.ds(pl.multiple_of(c * LANES, LANES), LANES)
            block = jnp.swapaxes(chol[t, :, :, cols], 0, 1)
            pots = [
                (jnp.dot(fields, block[r], preferred_element_type=jnp.float32) * 0.3).astype(jnp.bfloat16)
                for r in range(TILE)
            ]
            send[t, :, :, cols] = jnp.swapaxes(jnp.stack(pots, axis=0), 0, 1)
            return 0

        half_way = width // LANES // 2
        lax.fori_loop(0, half_way, strip, 0)
        pass_back(SECOND + 2 * t, SECOND + 2 * t + 1)
        lax.fori_loop(half_way, width // LANES, strip, 0)
        recv[:, seat, t] = send[t, pl.ds(seat * line, line)]

    def forward_far(first, last):
        def step(c, _):
            outer_orbit(far_out, 0, buddy, c).wait_recv()

            @pl.when(inner)
            def _():
                outer_orbit(far_out, 0, buddy, c).start()

            return 0

        lax.fori_loop(first, last, step, 0)

    for t in range(tiles):
        fill(t)
        push(t, order[0])
        pass_back(SECOND + 2 * t + 1, SECOND + 2 * t + 2)
    held = SECOND + 2 * tiles

    for plane in order[1:]:
        for t in range(tiles):
            push(t, plane)

    def lend():
        return remote(recv.at[pl.ds(buddy * owned, owned)], lent, lend_sem.at[0], lend_sem.at[1], at(buddy))

    passed = held * HALVES // CHUNKS
    pass_on(0, passed)
    for w in range(passed, HALVES * owned):
        pass_back(w * CHUNKS // HALVES, (w + 1) * CHUNKS // HALVES)
        pass_on(w, w + 1)
    @pl.when(outer)
    def _():
        await_pots(near_in)
        lend().start()

        def arrived(c, _):
            inner_orbit(c).wait_recv()
            return 0

        lax.fori_loop(0, chunks, arrived, 0)

    def hand_back(plane, w):
        return remote(
            done.at[plane * owned + w], out_ref.at[w, pl.ds(z * PLANE, PLANE)],
            done_sem.at[0], done_sem.at[1], at(plane),
        )

    def rows_done(left, orbit, old):
        moved = jnp.dot(
            left.reshape(-1, width), orbit.reshape(width, nocc), preferred_element_type=jnp.float32
        )
        return (old.astype(jnp.float32) + moved.reshape(old.shape)).astype(jnp.bfloat16)

    here = pl.ds(z * PLANE, PLANE)

    def serve(plane, first, last):
        def step(w, _):
            done[plane * owned + w] = rows_done(
                recv[plane * owned + w], guest[plane, w], guest[plane, w, here]
            )
            hand_back(plane, w).start()
            return 0

        lax.fori_loop(first, last, step, 0)

    forward_far(0, HALVES)
    await_pots(far_in)
    @pl.when(outer)
    def _():
        serve(far_in, 0, owned)

    forward_far(HALVES, 2 * HALVES)
    await_pots(far_out)
    serve(far_out, 0, 2)
    for w in range(2, owned):
        forward_far(HALVES * w, HALVES * (w + 1))
        serve(far_out, w, w + 1)

    @pl.when(inner)
    def _():
        serve(far_in, 0, owned)

    @pl.when(inner)
    def _():
        await_pots(near_out)
        serve(near_out, 0, owned)

    await_pots(z)
    orb_copy.wait()

    def advance(w, _):
        out_ref[w, here] = rows_done(recv[z * owned + w], orb_ref[w], orb_ref[w, here])
        return 0

    lax.fori_loop(0, owned, advance, 0)

    @pl.when(inner)
    def _():
        lend().wait_recv()
        there = pl.ds(near_out * PLANE, PLANE)

        def borrow(w, _):
            out_ref[w, there] = rows_done(lent[w], orb_ref[w], orb_ref[w, there])
            return 0

        lax.fori_loop(0, owned, borrow, 0)

    gathered(part_in, part_sem).wait_send()
    gathered(fields_ref, field_sem).wait_send()
    every = send.at[:, pl.ds(0, (PLANE - 1) * line)]
    remote(every, every, pot_send.at[0], pot_recv.at[z], at(ahead)).wait_send()

    def through(ref, sem):
        return remote(ref, ref, sem.at[0], sem.at[1], at(ahead))

    @pl.when(outer)
    def _():
        sum_copy(0, at(ahead)).wait_send()
        lend().wait_send()
        remote(guest.at[0], guest.at[0], orb_send.at[0], orb_recv.at[0], at(ahead)).wait_send()
        through(done.at[pl.ds(0, 2 * owned)], done_sem).wait_send()

    @pl.when(inner)
    def _():
        sum_copy(1, at(ahead)).wait_send()
        total_copy().wait_send()
        remote(guest, guest, orb_send.at[0], orb_recv.at[0], at(ahead)).wait_send()
        through(done.at[pl.ds(0, 3 * owned)], done_sem).wait_send()

    @pl.when(outer)
    def _():
        through(out_ref.at[:, pl.ds(0, 3 * PLANE)], done_sem).wait_recv()

    @pl.when(inner)
    def _():
        through(out_ref.at[:, pl.ds(0, 2 * PLANE)], done_sem).wait_recv()


def close_kernel(moved_ref, logs_ref, out_hbm, log_hbm, log_ref, sem):
    copies = [
        pltpu.make_async_copy(moved_ref.at[w], out_hbm.at[w], sem.at[w]) for w in range(moved_ref.shape[0])
    ]
    for copy in copies:
        copy.start()
    log_ref[...] = logs_ref[:, 0]
    copies.append(pltpu.make_async_copy(log_ref, log_hbm, sem.at[len(copies)]))
    copies[-1].start()
    for copy in copies:
        copy.wait()


def on_device(n, chol_full, chol_half, green, gauss, orbitals):
    walkers, local_rows, nocc = green.shape
    owned, width, _ = orbitals.shape
    vectors = chol_half.shape[0]
    tiles = local_rows // TILE
    vmem = pl.BlockSpec(memory_space=pltpu.VMEM)
    hbm = pl.BlockSpec(memory_space=pl.ANY)
    dma = pltpu.SemaphoreType.DMA
    split = (owned, n, tiles, TILE, nocc)
    params = pltpu.CompilerParams(collective_id=0, has_side_effects=True, vmem_limit_bytes=60 << 20)
    shared = [
        pltpu.VMEM((tiles, vectors, TILE, width), jnp.bfloat16),
        pltpu.VMEM((vectors, local_rows, nocc), jnp.bfloat16),
        pltpu.VMEM((walkers, local_rows, nocc), jnp.bfloat16),
    ]
    arrays = (chol_full, chol_half, green, gauss.reshape(n, owned, vectors), orbitals.reshape(split))
    if n == 4 * PLANE and orbitals.size * orbitals.dtype.itemsize <= OWN_LIMIT:
        line = walkers // PLANE
        planes = n // PLANE
        moved, logs = pl.pallas_call(
            functools.partial(line_kernel, n),
            out_shape=(pltpu.VMEM(split, jnp.bfloat16), pltpu.VMEM((owned, LANES), jnp.float32)),
            in_specs=[hbm] * 5,
            out_specs=(vmem, vmem),
            scratch_shapes=[
                *shared,
                pltpu.VMEM((n, owned, vectors), jnp.float32),
                pltpu.VMEM(split, jnp.bfloat16),
                pltpu.VMEM((PLANE, line, vectors), jnp.float32),
                pltpu.VMEM((PLANE, line, vectors), jnp.float32),
                pltpu.VMEM((2, line, vectors), jnp.float32),
                pltpu.VMEM((2, line, vectors), jnp.float32),
                pltpu.VMEM((line, vectors), jnp.float32),
                pltpu.VMEM((planes, owned, LANES), jnp.float32),
                pltpu.VMEM((PLANE, line, vectors), jnp.bfloat16),
                pltpu.VMEM((tiles, walkers, TILE, width), jnp.bfloat16),
                pltpu.VMEM((line, PLANE, tiles, TILE, width), jnp.bfloat16),
                pltpu.VMEM((planes,) + split, jnp.bfloat16),
                pltpu.VMEM((line, PLANE, tiles, TILE, nocc), jnp.bfloat16),
                pltpu.VMEM((owned, PLANE, tiles, TILE, width), jnp.bfloat16),
                dma((1,)), dma((4,)), dma((2,)), dma((2, 2)), dma((2,)), dma((1,)), dma((planes,)),
                dma((1,)), dma((CHUNKS * owned,)), dma((2, HALVES * owned)), dma((2,)), dma((2,)),
                pltpu.SemaphoreType.REGULAR, pltpu.SemaphoreType.REGULAR,
            ],
            compiler_params=params,
        )(*arrays)
        moved, logs = pl.pallas_call(
            close_kernel,
            out_shape=(
                jax.ShapeDtypeStruct(split, jnp.bfloat16),
                jax.ShapeDtypeStruct((owned,), jnp.float32),
            ),
            in_specs=[pl.BlockSpec(memory_space=pltpu.VMEM)] * 2,
            out_specs=(hbm, hbm),
            scratch_shapes=[pltpu.VMEM((owned,), jnp.float32), dma((owned + 1,))],
            compiler_params=pltpu.CompilerParams(vmem_limit_bytes=1 << 20),
        )(moved, logs)
        return moved.reshape(orbitals.shape), logs
    else:
        moved, logs = pl.pallas_call(
            functools.partial(direct_kernel, n),
            out_shape=(
                jax.ShapeDtypeStruct(split, jnp.bfloat16),
                jax.ShapeDtypeStruct((owned, LANES), jnp.float32),
            ),
            in_specs=[hbm, hbm, hbm, vmem, vmem],
            out_specs=(vmem, vmem),
            scratch_shapes=[
                *shared,
                pltpu.VMEM((n, owned, vectors), jnp.float32),
                pltpu.VMEM((n, owned, vectors), jnp.float32),
                pltpu.VMEM((owned, vectors), jnp.float32),
                pltpu.VMEM((n, owned, vectors), jnp.float32),
                pltpu.VMEM((tiles, walkers, TILE, width), jnp.bfloat16),
                pltpu.VMEM((tiles, owned, n * TILE, width), jnp.bfloat16),
                dma((tiles,)), dma((2,)), dma((n,)), dma((n,)), dma((n,)), dma((n,)),
                dma((tiles, n)), dma((tiles, n)),
            ],
            compiler_params=params,
        )(*arrays)
    return moved.reshape(orbitals.shape), logs[:, 0]


def solution(mesh):
    placed = (
        P(None, "chol", None),
        P(None, "chol", None),
        P("grp", "chol", None),
        P("grp", None),
        P(("grp", "chol"), None, None),
    )
    return jax.shard_map(
        functools.partial(on_device, mesh.shape["chol"]),
        mesh=mesh,
        in_specs=placed,
        out_specs=(P(("grp", "chol"), None, None), P(("grp", "chol"))),
        check_vma=False,
    )
```

```python
import functools

import jax
import jax.numpy as jnp
from jax import lax
from jax.experimental import pallas as pl
from jax.experimental.pallas import tpu as pltpu
from jax.sharding import PartitionSpec as P

TILE = 16
LANES = 128
PLANE = 4
OWN_LIMIT = 2 << 20
CHUNKS = 2
FIRST = 1
SECOND = 2
THIRD = 3


def remote(src, dst, send, recv, peer):
    return pltpu.make_async_remote_copy(
        src_ref=src,
        dst_ref=dst,
        send_sem=send,
        recv_sem=recv,
        device_id={"chol": peer},
        device_id_type=pl.DeviceIdType.MESH,
    )


def direct_kernel(
    n, chol_hbm, half_hbm, green_hbm, gauss_ref, orb_ref,
    out_ref, log_ref,
    chol, half, green, part, part_in, fields_own, fields_in, send, recv,
    load_sem, aux_sem, part_send, part_recv, field_send, field_recv, pot_send, pot_recv,
):
    me = lax.axis_index("chol")
    owned = part.shape[1]
    tiles = chol.shape[0]
    width = chol.shape[3]

    half_copy = pltpu.make_async_copy(half_hbm, half, aux_sem.at[0])
    green_copy = pltpu.make_async_copy(green_hbm, green, aux_sem.at[1])
    half_copy.start()
    green_copy.start()
    loads = [
        pltpu.make_async_copy(chol_hbm.at[:, pl.ds(t * TILE, TILE), :], chol.at[t], load_sem.at[t])
        for t in range(tiles)
    ]
    for load in loads:
        load.start()

    barrier = pltpu.get_barrier_semaphore()

    def greet(k, _):
        pl.semaphore_signal(
            barrier, inc=1, device_id={"chol": lax.rem(me + k, n)}, device_id_type=pl.DeviceIdType.MESH
        )
        return 0

    lax.fori_loop(1, n, greet, 0)

    half_copy.wait()
    green_copy.wait()

    def bias(t, acc):
        rows = pl.ds(pl.multiple_of(t * TILE, TILE), TILE)
        left = jnp.swapaxes(green[:, rows, :], 0, 1)
        right = jnp.swapaxes(half[:, rows, :], 0, 1)
        for r in range(TILE):
            acc += lax.dot_general(
                left[r], right[r], (((1,), (1,)), ((), ())), preferred_element_type=jnp.float32
            )
        return acc

    total = lax.fori_loop(0, tiles, bias, jnp.zeros((n * owned, half.shape[0]), jnp.float32))
    for d in range(n):
        part[d] = total[d * owned:(d + 1) * owned]
    pl.semaphore_wait(barrier, n - 1)

    def peer_of(k):
        return lax.rem(me + k, n)

    def push_part(k, _):
        to = peer_of(k)
        remote(part.at[to], part_in.at[me], part_send.at[to], part_recv.at[me], to).start()
        return 0

    lax.fori_loop(1, n, push_part, 0)
    part_in[me] = part[me]

    def wait_part(k, _):
        peer = peer_of(k)
        copy = remote(part.at[peer], part_in.at[peer], part_send.at[peer], part_recv.at[peer], peer)
        copy.wait_recv()
        return 0

    lax.fori_loop(1, n, wait_part, 0)
    vbias = jnp.sum(part_in[...], axis=0)
    gauss = gauss_ref[me]
    xbar = jnp.clip(-0.3 * vbias, -1.0, 1.0)
    log_ref[...] = jnp.broadcast_to(
        jnp.sum(gauss * xbar - 0.5 * xbar * xbar, axis=1, keepdims=True), log_ref.shape
    )
    mine = gauss - xbar
    fields_own[...] = mine
    fields_in[me] = mine

    def push_field(k, _):
        to = peer_of(k)
        remote(fields_own, fields_in.at[me], field_send.at[to], field_recv.at[me], to).start()
        return 0

    lax.fori_loop(1, n, push_field, 0)

    def wait_field(k, _):
        peer = peer_of(k)
        remote(fields_own, fields_in.at[peer], field_send.at[peer], field_recv.at[peer], peer).wait_recv()
        return 0

    lax.fori_loop(1, n, wait_field, 0)
    fields = jnp.concatenate([fields_in[d] for d in range(n)], axis=0).astype(jnp.bfloat16)

    def walkers_of(d):
        return pl.ds(d * owned, owned)

    def rows_of(d):
        return pl.ds(pl.multiple_of(d * TILE, TILE), TILE)

    for t in range(tiles):
        loads[t].wait()

        def strip(c, _):
            cols = pl.ds(pl.multiple_of(c * LANES, LANES), LANES)
            block = jnp.swapaxes(chol[t, :, :, cols], 0, 1)
            pots = [
                (jnp.dot(fields, block[r], preferred_element_type=jnp.float32) * 0.3).astype(jnp.bfloat16)
                for r in range(TILE)
            ]
            send[t, :, :, cols] = jnp.swapaxes(jnp.stack(pots, axis=0), 0, 1)
            return 0

        lax.fori_loop(0, width // LANES, strip, 0)

        def push_pot(k, _):
            to = peer_of(k)
            remote(
                send.at[t, walkers_of(to)], recv.at[t, :, rows_of(me), :],
                pot_send.at[t, to], pot_recv.at[t, me], to,
            ).start()
            return 0

        lax.fori_loop(1, n, push_pot, 0)
        recv[t, :, rows_of(me), :] = send[t, walkers_of(me)]

    for t in range(tiles):

        def wait_pot(k, _):
            peer = peer_of(k)
            remote(
                send.at[t, walkers_of(peer)], recv.at[t, :, rows_of(peer), :],
                pot_send.at[t, peer], pot_recv.at[t, peer], peer,
            ).wait_recv()
            return 0

        lax.fori_loop(1, n, wait_pot, 0)

        def advance(w, _):
            orbit = orb_ref[w].reshape(width, orb_ref.shape[-1])
            for first in range(0, n, 16):
                span = min(16, n - first)
                moved = jnp.dot(
                    recv[t, w, first * TILE:(first + span) * TILE, :], orbit,
                    preferred_element_type=jnp.float32,
                ).reshape(span, TILE, orbit.shape[-1])
                old = orb_ref[w, first:first + span, t].astype(jnp.float32)
                out_ref[w, first:first + span, t] = (old + moved).astype(jnp.bfloat16)
            return 0

        lax.fori_loop(0, owned, advance, 0)

    def drain(k, _):
        peer = peer_of(k)
        remote(part.at[peer], part_in.at[peer], part_send.at[peer], part_recv.at[peer], peer).wait_send()
        remote(fields_own, fields_in.at[peer], field_send.at[peer], field_recv.at[peer], peer).wait_send()
        for t in range(tiles):
            remote(
                send.at[t, walkers_of(peer)], recv.at[t, :, rows_of(peer), :],
                pot_send.at[t, peer], pot_recv.at[t, peer], peer,
            ).wait_send()
        return 0

    lax.fori_loop(1, n, drain, 0)


def line_kernel(
    n, chol_hbm, half_hbm, green_hbm, gauss_hbm, orb_hbm,
    out_ref, log_ref,
    chol, half, green, gauss_ref, orb_ref, part, part_in, partial, partial_in, bias_ref, log_all, fields_ref,
    send, recv, guest, done, lent,
    load_sem, aux_sem, part_sem, sum_sem, field_sem, pot_send, pot_recv, orb_send, orb_recv,
    lend_sem, done_sem, told,
):
    me = lax.axis_index("chol")
    owned = orb_ref.shape[0]
    tiles = chol.shape[0]
    width = chol.shape[3]
    nocc = orb_ref.shape[-1]
    planes = n // PLANE
    line = planes * owned
    chunks = CHUNKS * owned
    span = n // CHUNKS

    z = me // PLANE
    seat = lax.rem(me, PLANE)
    side = z // 2
    far = 1 - side
    near_in, near_out = 1 + side, 3 * side
    far_in, far_out = 1 + far, 3 * far
    ahead = z + 1 - 2 * side
    buddy = near_in + near_out - z
    inner = z == near_in
    outer = z == near_out

    barrier = pltpu.get_barrier_semaphore()

    partner = seat + 1 - 2 * lax.rem(seat, 2)
    beside = lax.rem(seat + 2, PLANE)
    diagonal = lax.rem(partner + 2, PLANE)
    others = (beside, diagonal, partner)

    def greet(peer):
        pl.semaphore_signal(barrier, inc=1, device_id={"chol": peer}, device_id_type=pl.DeviceIdType.MESH)

    def tell(sem, peer):
        pl.semaphore_signal(sem, inc=1, device_id={"chol": peer}, device_id_type=pl.DeviceIdType.MESH)

    @pl.when(inner)
    def _():
        greet(ahead * PLANE + seat)
        greet(buddy * PLANE + seat)

    @pl.when(outer)
    def _():
        for s in others:
            greet(z * PLANE + s)

    half_copy = pltpu.make_async_copy(half_hbm, half, aux_sem.at[0])
    green_copy = pltpu.make_async_copy(green_hbm, green, aux_sem.at[1])
    gauss_copy = pltpu.make_async_copy(gauss_hbm, gauss_ref, aux_sem.at[2])
    orb_copy = pltpu.make_async_copy(orb_hbm, orb_ref, aux_sem.at[3])
    for copy in (green_copy, half_copy, gauss_copy):
        copy.start()
    loads = [
        pltpu.make_async_copy(chol_hbm.at[:, pl.ds(t * TILE, TILE), :], chol.at[t], load_sem.at[0])
        for t in range(tiles)
    ]
    @pl.when(inner)
    def _():
        pl.semaphore_wait(barrier, 1)

    @pl.when(outer)
    def _():
        pl.semaphore_wait(barrier, PLANE)
        for s in others:
            tell(told, z * PLANE + s)

    def at(plane):
        return plane * PLANE + seat

    def piece(ref, c):
        return ref.at[c // CHUNKS, pl.ds(lax.rem(c, CHUNKS) * span, span)]

    def landed(plane, to, c):
        return orb_recv.at[lax.rem(plane - to + planes, planes) - 1, c]

    def own_orbit(c):
        return remote(piece(orb_hbm, c), piece(guest.at[z], c), orb_send.at[0], landed(z, ahead, c), at(ahead))

    def orbit_copy(plane, to, c):
        there = piece(guest.at[plane], c)
        return remote(there, there, orb_send.at[0], landed(plane, to, c), at(to))

    def orbit_on(c):
        return orbit_copy(near_out, ahead, c)

    def orbit_back(plane, c):
        return orbit_copy(plane, buddy, c)

    def await_orbit(plane, c):
        there = piece(guest.at[plane], c)
        remote(there, there, orb_send.at[0], landed(plane, z, c), at(ahead)).wait_recv()

    def start_own(first, last):
        def step(c, _):
            own_orbit(c).start()
            return 0

        lax.fori_loop(first, last, step, 0)

    def pass_on(first, last):
        @pl.when(inner)
        def _():
            def step(c, _):
                await_orbit(near_out, c)
                orbit_on(c).start()
                return 0

            lax.fori_loop(first, last, step, 0)

    def pass_back(first, last):
        @pl.when(inner)
        def _():
            def step(c, _):
                await_orbit(far_in, c)
                orbit_back(far_in, c).start()
                return 0

            lax.fori_loop(first, last, step, 0)

    start_own(0, FIRST)

    @pl.when(outer)
    def _():
        pl.semaphore_wait(told, PLANE - 1)
        tell(told, at(ahead))


    half_copy.wait()
    green_copy.wait()
    for copy in (*loads, orb_copy):
        copy.start()
    gauss_copy.wait()

    def bias(t, acc):
        rows = pl.ds(pl.multiple_of(t * TILE, TILE), TILE)
        left = jnp.swapaxes(green[:, rows, :], 0, 1)
        right = jnp.swapaxes(half[:, rows, :], 0, 1)
        for r in range(TILE):
            acc += lax.dot_general(
                left[r], right[r], (((1,), (1,)), ((), ())), preferred_element_type=jnp.float32
            )
        return acc

    total = lax.fori_loop(0, tiles, bias, jnp.zeros((n * owned, half.shape[0]), jnp.float32))
    for d in range(n):
        plane, s = divmod(d, PLANE)
        part[s, plane * owned:(plane + 1) * owned] = total[d * owned:(d + 1) * owned]

    @pl.when(inner)
    def _():
        pl.semaphore_wait(told, 1)

    def part_copy(there, source):
        return remote(part.at[there], part_in.at[source], part_sem.at[0], part_sem.at[1], z * PLANE + there)

    def field_copy(there):
        mine = fields_ref.at[seat]
        return remote(mine, mine, field_sem.at[0], field_sem.at[1], z * PLANE + there)

    def gathered(ref, sem):
        every = ref.at[pl.ds(0, PLANE - 1)]
        return remote(every, every, sem.at[0], sem.at[1], at(ahead))

    def sum_copy(k, to):
        return remote(partial.at[k], partial_in.at[k], sum_sem.at[0, 0], sum_sem.at[1, k], to)

    def total_copy():
        return remote(bias_ref, bias_ref, sum_sem.at[0, 1], sum_sem.at[1, 0], at(buddy))

    for s in others:
        part_copy(s, seat).start()
    part_in[seat] = part[seat]

    @pl.when(inner)
    def _():
        start_own(FIRST, SECOND)

    pass_back(0, FIRST)
    gathered(part_in, part_sem).wait_recv()
    partial[0] = jnp.sum(part_in[...], axis=0)

    @pl.when(outer)
    def _():
        sum_copy(0, at(ahead)).start()
        start_own(FIRST, chunks)
        total_copy().wait_recv()

    @pl.when(inner)
    def _():
        sum_copy(0, at(ahead)).wait_recv()
        partial[1] = partial[0] + partial_in[0]
        sum_copy(1, at(ahead)).start()
        start_own(SECOND, THIRD)
        sum_copy(1, at(ahead)).wait_recv()
        bias_ref[...] = partial[1] + partial_in[1]
        total_copy().start()
        start_own(THIRD, chunks)

    pass_back(FIRST, SECOND)
    vbias = bias_ref[...]
    gauss = jnp.concatenate([gauss_ref[plane * PLANE + seat] for plane in range(planes)], axis=0)
    xbar = jnp.clip(-0.3 * vbias, -1.0, 1.0)
    logs = jnp.sum(gauss * xbar - 0.5 * xbar * xbar, axis=1, keepdims=True)
    log_all[...] = jnp.broadcast_to(logs, (line, LANES)).reshape(log_all.shape)
    log_ref[...] = log_all[z]
    fields_ref[seat] = (gauss - xbar).astype(jnp.bfloat16)

    for s in others:
        field_copy(s).start()
    gathered(fields_ref, field_sem).wait_recv()
    pltpu.make_async_copy(chol, chol, load_sem.at[0]).wait()
    fields = fields_ref[...].reshape(n * owned, fields_ref.shape[-1])

    order = (
        jnp.where(inner, far_in, near_in), jnp.where(inner, far_out, far_in),
        jnp.where(inner, near_out, far_out), z,
    )

    def pot_copy(t, plane, there, source):
        return remote(
            send.at[t, pl.ds(there * line + plane * owned, owned)],
            recv.at[pl.ds(plane * owned, owned), source, t],
            pot_send.at[0], pot_recv.at[plane], z * PLANE + there,
        )

    def push(t, plane):
        for s in others:
            pot_copy(t, plane, s, seat).start()

    def await_pots(plane):
        every = recv.at[pl.ds(plane * owned, owned), pl.ds(0, PLANE - 1)]
        remote(every, every, pot_send.at[0], pot_recv.at[plane], z * PLANE + partner).wait_recv()

    def fill(t):
        def strip(c, _):
            cols = pl.ds(pl.multiple_of(c * LANES, LANES), LANES)
            block = jnp.swapaxes(chol[t, :, :, cols], 0, 1)
            pots = [
                (jnp.dot(fields, block[r], preferred_element_type=jnp.float32) * 0.3).astype(jnp.bfloat16)
                for r in range(TILE)
            ]
            send[t, :, :, cols] = jnp.swapaxes(jnp.stack(pots, axis=0), 0, 1)
            return 0

        lax.fori_loop(0, width // LANES, strip, 0)
        recv[:, seat, t] = send[t, pl.ds(seat * line, line)]

    def forward_far(first, last):
        def step(c, _):
            await_orbit(far_out, c)

            @pl.when(inner)
            def _():
                orbit_back(far_out, c).start()

            return 0

        lax.fori_loop(first, last, step, 0)

    for t in range(tiles):
        fill(t)
        push(t, order[0])
        if t < tiles - 1:
            pass_back(SECOND + t, SECOND + t + 1)
    held = SECOND + tiles - 1
    for plane in order[1:]:
        for t in range(tiles):
            push(t, plane)

    def lend():
        return remote(recv.at[pl.ds(buddy * owned, owned)], lent, lend_sem.at[0], lend_sem.at[0], at(buddy))

    pass_back(held, held + 1)
    pass_on(0, held + 1)
    pass_back(held + 1, held + 2)
    pass_on(held + 1, held + 2)
    pass_back(held + 2, chunks)
    pass_on(held + 2, chunks)
    @pl.when(outer)
    def _():
        await_pots(near_in)
        lend().start()

        def arrived(c, _):
            await_orbit(far_in, c)
            return 0

        lax.fori_loop(0, chunks, arrived, 0)

    def hand_back(plane, w):
        return remote(
            done.at[plane * owned + w], out_ref.at[w, pl.ds(z * PLANE, PLANE)],
            done_sem.at[0], done_sem.at[1], at(plane),
        )

    def rows_done(left, orbit, old):
        moved = jnp.dot(
            left.reshape(-1, width), orbit.reshape(width, nocc), preferred_element_type=jnp.float32
        )
        return (old.astype(jnp.float32) + moved.reshape(old.shape)).astype(jnp.bfloat16)

    here = pl.ds(z * PLANE, PLANE)

    def serve(plane, first, last):
        def step(w, _):
            done[plane * owned + w] = rows_done(
                recv[plane * owned + w], guest[plane, w], guest[plane, w, here]
            )
            hand_back(plane, w).start()
            return 0

        lax.fori_loop(first, last, step, 0)

    forward_far(0, CHUNKS)
    await_pots(far_in)
    @pl.when(outer)
    def _():
        serve(far_in, 0, owned)

    forward_far(CHUNKS, 2 * CHUNKS)
    await_pots(far_out)
    serve(far_out, 0, 2)
    for w in range(2, owned):
        forward_far(CHUNKS * w, CHUNKS * (w + 1))
        serve(far_out, w, w + 1)

    @pl.when(inner)
    def _():
        serve(far_in, 0, owned)

    @pl.when(inner)
    def _():
        await_pots(near_out)
        serve(near_out, 0, owned)

    await_pots(z)
    orb_copy.wait()

    def advance(w, _):
        out_ref[w, here] = rows_done(recv[z * owned + w], orb_ref[w], orb_ref[w, here])
        return 0

    lax.fori_loop(0, owned, advance, 0)

    @pl.when(inner)
    def _():
        lend().wait_recv()
        there = pl.ds(near_out * PLANE, PLANE)

        def borrow(w, _):
            out_ref[w, there] = rows_done(lent[w], orb_ref[w], orb_ref[w, there])
            return 0

        lax.fori_loop(0, owned, borrow, 0)

    gathered(part_in, part_sem).wait_send()
    gathered(fields_ref, field_sem).wait_send()
    every = send.at[:, pl.ds(0, (PLANE - 1) * line)]
    remote(every, every, pot_send.at[0], pot_recv.at[z], at(ahead)).wait_send()

    def through(ref, sem):
        return remote(ref, ref, sem.at[0], sem.at[1], at(ahead))

    @pl.when(outer)
    def _():
        sum_copy(0, at(ahead)).wait_send()
        lend().wait_send()
        remote(guest.at[0], guest.at[0], orb_send.at[0], orb_recv.at[0, 0], at(ahead)).wait_send()
        through(done.at[pl.ds(0, 2 * owned)], done_sem).wait_send()

    @pl.when(inner)
    def _():
        sum_copy(1, at(ahead)).wait_send()
        total_copy().wait_send()
        remote(guest, guest, orb_send.at[0], orb_recv.at[0, 0], at(ahead)).wait_send()
        through(done.at[pl.ds(0, 3 * owned)], done_sem).wait_send()

    @pl.when(outer)
    def _():
        through(out_ref.at[:, pl.ds(0, 3 * PLANE)], done_sem).wait_recv()

    @pl.when(inner)
    def _():
        through(out_ref.at[:, pl.ds(0, 2 * PLANE)], done_sem).wait_recv()


def close_kernel(moved_ref, logs_ref, out_hbm, log_hbm, log_ref, sem):
    copies = [
        pltpu.make_async_copy(moved_ref.at[w], out_hbm.at[w], sem.at[w]) for w in range(moved_ref.shape[0])
    ]
    for copy in copies:
        copy.start()
    log_ref[...] = logs_ref[:, 0]
    copies.append(pltpu.make_async_copy(log_ref, log_hbm, sem.at[len(copies)]))
    copies[-1].start()
    for copy in copies:
        copy.wait()


def on_device(n, chol_full, chol_half, green, gauss, orbitals):
    walkers, local_rows, nocc = green.shape
    owned, width, _ = orbitals.shape
    vectors = chol_half.shape[0]
    tiles = local_rows // TILE
    vmem = pl.BlockSpec(memory_space=pltpu.VMEM)
    hbm = pl.BlockSpec(memory_space=pl.ANY)
    dma = pltpu.SemaphoreType.DMA
    split = (owned, n, tiles, TILE, nocc)
    params = pltpu.CompilerParams(collective_id=0, has_side_effects=True, vmem_limit_bytes=60 << 20)
    shared = [
        pltpu.VMEM((tiles, vectors, TILE, width), jnp.bfloat16),
        pltpu.VMEM((vectors, local_rows, nocc), jnp.bfloat16),
        pltpu.VMEM((walkers, local_rows, nocc), jnp.bfloat16),
    ]
    arrays = (chol_full, chol_half, green, gauss.reshape(n, owned, vectors), orbitals.reshape(split))
    if n == 4 * PLANE and orbitals.size * orbitals.dtype.itemsize <= OWN_LIMIT:
        line = walkers // PLANE
        planes = n // PLANE
        moved, logs = pl.pallas_call(
            functools.partial(line_kernel, n),
            out_shape=(pltpu.VMEM(split, jnp.bfloat16), pltpu.VMEM((owned, LANES), jnp.float32)),
            in_specs=[hbm] * 5,
            out_specs=(vmem, vmem),
            scratch_shapes=[
                *shared,
                pltpu.VMEM((n, owned, vectors), jnp.float32),
                pltpu.VMEM(split, jnp.bfloat16),
                pltpu.VMEM((PLANE, line, vectors), jnp.float32),
                pltpu.VMEM((PLANE, line, vectors), jnp.float32),
                pltpu.VMEM((2, line, vectors), jnp.float32),
                pltpu.VMEM((2, line, vectors), jnp.float32),
                pltpu.VMEM((line, vectors), jnp.float32),
                pltpu.VMEM((planes, owned, LANES), jnp.float32),
                pltpu.VMEM((PLANE, line, vectors), jnp.bfloat16),
                pltpu.VMEM((tiles, walkers, TILE, width), jnp.bfloat16),
                pltpu.VMEM((line, PLANE, tiles, TILE, width), jnp.bfloat16),
                pltpu.VMEM((planes,) + split, jnp.bfloat16),
                pltpu.VMEM((line, PLANE, tiles, TILE, nocc), jnp.bfloat16),
                pltpu.VMEM((owned, PLANE, tiles, TILE, width), jnp.bfloat16),
                dma((1,)), dma((4,)), dma((2,)), dma((2, 2)), dma((2,)), dma((1,)), dma((planes,)),
                dma((1,)), dma((planes - 1, CHUNKS * owned)), dma((1,)), dma((2,)),
                pltpu.SemaphoreType.REGULAR,
            ],
            compiler_params=params,
        )(*arrays)
        moved, logs = pl.pallas_call(
            close_kernel,
            out_shape=(
                jax.ShapeDtypeStruct(split, jnp.bfloat16),
                jax.ShapeDtypeStruct((owned,), jnp.float32),
            ),
            in_specs=[pl.BlockSpec(memory_space=pltpu.VMEM)] * 2,
            out_specs=(hbm, hbm),
            scratch_shapes=[pltpu.VMEM((owned,), jnp.float32), dma((owned + 1,))],
            compiler_params=pltpu.CompilerParams(vmem_limit_bytes=1 << 20),
        )(moved, logs)
        return moved.reshape(orbitals.shape), logs
    else:
        moved, logs = pl.pallas_call(
            functools.partial(direct_kernel, n),
            out_shape=(
                jax.ShapeDtypeStruct(split, jnp.bfloat16),
                jax.ShapeDtypeStruct((owned, LANES), jnp.float32),
            ),
            in_specs=[hbm, hbm, hbm, vmem, vmem],
            out_specs=(vmem, vmem),
            scratch_shapes=[
                *shared,
                pltpu.VMEM((n, owned, vectors), jnp.float32),
                pltpu.VMEM((n, owned, vectors), jnp.float32),
                pltpu.VMEM((owned, vectors), jnp.float32),
                pltpu.VMEM((n, owned, vectors), jnp.float32),
                pltpu.VMEM((tiles, walkers, TILE, width), jnp.bfloat16),
                pltpu.VMEM((tiles, owned, n * TILE, width), jnp.bfloat16),
                dma((tiles,)), dma((2,)), dma((n,)), dma((n,)), dma((n,)), dma((n,)),
                dma((tiles, n)), dma((tiles, n)),
            ],
            compiler_params=params,
        )(*arrays)
    return moved.reshape(orbitals.shape), logs[:, 0]


def solution(mesh):
    placed = (
        P(None, "chol", None),
        P(None, "chol", None),
        P("grp", "chol", None),
        P("grp", None),
        P(("grp", "chol"), None, None),
    )
    return jax.shard_map(
        functools.partial(on_device, mesh.shape["chol"]),
        mesh=mesh,
        in_specs=placed,
        out_specs=(P(("grp", "chol"), None, None), P(("grp", "chol"))),
        check_vma=False,
    )
```

```python
import functools

import jax
import jax.numpy as jnp
from jax import lax
from jax.experimental import pallas as pl
from jax.experimental.pallas import tpu as pltpu
from jax.sharding import PartitionSpec as P

TILE = 16
LANES = 128
PLANE = 4
OWN_LIMIT = 2 << 20
CHUNKS = 2
FIRST = 1
SECOND = 2
THIRD = 3


def remote(src, dst, send, recv, peer):
    return pltpu.make_async_remote_copy(
        src_ref=src,
        dst_ref=dst,
        send_sem=send,
        recv_sem=recv,
        device_id={"chol": peer},
        device_id_type=pl.DeviceIdType.MESH,
    )


def direct_kernel(
    n, chol_hbm, half_hbm, green_hbm, gauss_ref, orb_ref,
    out_ref, log_ref,
    chol, half, green, part, part_in, fields_own, fields_in, send, recv,
    load_sem, aux_sem, part_send, part_recv, field_send, field_recv, pot_send, pot_recv,
):
    me = lax.axis_index("chol")
    owned = part.shape[1]
    tiles = chol.shape[0]
    width = chol.shape[3]

    half_copy = pltpu.make_async_copy(half_hbm, half, aux_sem.at[0])
    green_copy = pltpu.make_async_copy(green_hbm, green, aux_sem.at[1])
    half_copy.start()
    green_copy.start()
    loads = [
        pltpu.make_async_copy(chol_hbm.at[:, pl.ds(t * TILE, TILE), :], chol.at[t], load_sem.at[t])
        for t in range(tiles)
    ]
    for load in loads:
        load.start()

    barrier = pltpu.get_barrier_semaphore()

    def greet(k, _):
        pl.semaphore_signal(
            barrier, inc=1, device_id={"chol": lax.rem(me + k, n)}, device_id_type=pl.DeviceIdType.MESH
        )
        return 0

    lax.fori_loop(1, n, greet, 0)

    half_copy.wait()
    green_copy.wait()

    def bias(t, acc):
        rows = pl.ds(pl.multiple_of(t * TILE, TILE), TILE)
        left = jnp.swapaxes(green[:, rows, :], 0, 1)
        right = jnp.swapaxes(half[:, rows, :], 0, 1)
        for r in range(TILE):
            acc += lax.dot_general(
                left[r], right[r], (((1,), (1,)), ((), ())), preferred_element_type=jnp.float32
            )
        return acc

    total = lax.fori_loop(0, tiles, bias, jnp.zeros((n * owned, half.shape[0]), jnp.float32))
    for d in range(n):
        part[d] = total[d * owned:(d + 1) * owned]
    pl.semaphore_wait(barrier, n - 1)

    def peer_of(k):
        return lax.rem(me + k, n)

    def push_part(k, _):
        to = peer_of(k)
        remote(part.at[to], part_in.at[me], part_send.at[to], part_recv.at[me], to).start()
        return 0

    lax.fori_loop(1, n, push_part, 0)
    part_in[me] = part[me]

    def wait_part(k, _):
        peer = peer_of(k)
        copy = remote(part.at[peer], part_in.at[peer], part_send.at[peer], part_recv.at[peer], peer)
        copy.wait_recv()
        return 0

    lax.fori_loop(1, n, wait_part, 0)
    vbias = jnp.sum(part_in[...], axis=0)
    gauss = gauss_ref[me]
    xbar = jnp.clip(-0.3 * vbias, -1.0, 1.0)
    log_ref[...] = jnp.broadcast_to(
        jnp.sum(gauss * xbar - 0.5 * xbar * xbar, axis=1, keepdims=True), log_ref.shape
    )
    mine = gauss - xbar
    fields_own[...] = mine
    fields_in[me] = mine

    def push_field(k, _):
        to = peer_of(k)
        remote(fields_own, fields_in.at[me], field_send.at[to], field_recv.at[me], to).start()
        return 0

    lax.fori_loop(1, n, push_field, 0)

    def wait_field(k, _):
        peer = peer_of(k)
        remote(fields_own, fields_in.at[peer], field_send.at[peer], field_recv.at[peer], peer).wait_recv()
        return 0

    lax.fori_loop(1, n, wait_field, 0)
    fields = jnp.concatenate([fields_in[d] for d in range(n)], axis=0).astype(jnp.bfloat16)

    def walkers_of(d):
        return pl.ds(d * owned, owned)

    def rows_of(d):
        return pl.ds(pl.multiple_of(d * TILE, TILE), TILE)

    for t in range(tiles):
        loads[t].wait()

        def strip(c, _):
            cols = pl.ds(pl.multiple_of(c * LANES, LANES), LANES)
            block = jnp.swapaxes(chol[t, :, :, cols], 0, 1)
            pots = [
                (jnp.dot(fields, block[r], preferred_element_type=jnp.float32) * 0.3).astype(jnp.bfloat16)
                for r in range(TILE)
            ]
            send[t, :, :, cols] = jnp.swapaxes(jnp.stack(pots, axis=0), 0, 1)
            return 0

        lax.fori_loop(0, width // LANES, strip, 0)

        def push_pot(k, _):
            to = peer_of(k)
            remote(
                send.at[t, walkers_of(to)], recv.at[t, :, rows_of(me), :],
                pot_send.at[t, to], pot_recv.at[t, me], to,
            ).start()
            return 0

        lax.fori_loop(1, n, push_pot, 0)
        recv[t, :, rows_of(me), :] = send[t, walkers_of(me)]

    for t in range(tiles):

        def wait_pot(k, _):
            peer = peer_of(k)
            remote(
                send.at[t, walkers_of(peer)], recv.at[t, :, rows_of(peer), :],
                pot_send.at[t, peer], pot_recv.at[t, peer], peer,
            ).wait_recv()
            return 0

        lax.fori_loop(1, n, wait_pot, 0)

        def advance(w, _):
            orbit = orb_ref[w].reshape(width, orb_ref.shape[-1])
            for first in range(0, n, 16):
                span = min(16, n - first)
                moved = jnp.dot(
                    recv[t, w, first * TILE:(first + span) * TILE, :], orbit,
                    preferred_element_type=jnp.float32,
                ).reshape(span, TILE, orbit.shape[-1])
                old = orb_ref[w, first:first + span, t].astype(jnp.float32)
                out_ref[w, first:first + span, t] = (old + moved).astype(jnp.bfloat16)
            return 0

        lax.fori_loop(0, owned, advance, 0)

    def drain(k, _):
        peer = peer_of(k)
        remote(part.at[peer], part_in.at[peer], part_send.at[peer], part_recv.at[peer], peer).wait_send()
        remote(fields_own, fields_in.at[peer], field_send.at[peer], field_recv.at[peer], peer).wait_send()
        for t in range(tiles):
            remote(
                send.at[t, walkers_of(peer)], recv.at[t, :, rows_of(peer), :],
                pot_send.at[t, peer], pot_recv.at[t, peer], peer,
            ).wait_send()
        return 0

    lax.fori_loop(1, n, drain, 0)


def line_kernel(
    n, chol_hbm, half_hbm, green_hbm, gauss_hbm, orb_hbm,
    out_ref, log_ref,
    chol, half, green, gauss_ref, orb_ref, part, part_in, partial, partial_in, bias_ref, log_all, fields_ref,
    send, recv, guest, done, lent,
    load_sem, aux_sem, part_sem, sum_sem, field_sem, pot_send, pot_recv, orb_send, orb_recv,
    lend_sem, done_sem, news, ready,
):
    me = lax.axis_index("chol")
    owned = orb_ref.shape[0]
    tiles = chol.shape[0]
    width = chol.shape[3]
    nocc = orb_ref.shape[-1]
    planes = n // PLANE
    line = planes * owned
    chunks = CHUNKS * owned
    span = n // CHUNKS

    z = me // PLANE
    seat = lax.rem(me, PLANE)
    side = z // 2
    far = 1 - side
    near_in, near_out = 1 + side, 3 * side
    far_in, far_out = 1 + far, 3 * far
    ahead = z + 1 - 2 * side
    buddy = near_in + near_out - z
    inner = z == near_in
    outer = z == near_out

    barrier = pltpu.get_barrier_semaphore()

    partner = seat + 1 - 2 * lax.rem(seat, 2)
    beside = lax.rem(seat + 2, PLANE)
    diagonal = lax.rem(partner + 2, PLANE)
    others = (beside, diagonal, partner)

    def greet(peer):
        pl.semaphore_signal(barrier, inc=1, device_id={"chol": peer}, device_id_type=pl.DeviceIdType.MESH)

    def tell(sem, peer):
        pl.semaphore_signal(sem, inc=1, device_id={"chol": peer}, device_id_type=pl.DeviceIdType.MESH)

    @pl.when(inner)
    def _():
        greet(ahead * PLANE + seat)
        greet(buddy * PLANE + seat)

    @pl.when(outer)
    def _():
        for s in others:
            greet(z * PLANE + s)

    half_copy = pltpu.make_async_copy(half_hbm, half, aux_sem.at[0])
    green_copy = pltpu.make_async_copy(green_hbm, green, aux_sem.at[1])
    gauss_copy = pltpu.make_async_copy(gauss_hbm, gauss_ref, aux_sem.at[2])
    orb_copy = pltpu.make_async_copy(orb_hbm, orb_ref, aux_sem.at[3])
    for copy in (green_copy, half_copy, gauss_copy):
        copy.start()
    loads = [
        pltpu.make_async_copy(chol_hbm.at[:, pl.ds(t * TILE, TILE), :], chol.at[t], load_sem.at[0])
        for t in range(tiles)
    ]
    @pl.when(inner)
    def _():
        pl.semaphore_wait(barrier, 1)

    @pl.when(outer)
    def _():
        pl.semaphore_wait(barrier, PLANE)
        for s in others:
            tell(news, z * PLANE + s)

    def at(plane):
        return plane * PLANE + seat

    def piece(ref, c):
        return ref.at[c // CHUNKS, pl.ds(lax.rem(c, CHUNKS) * span, span)]

    def landed(plane, to, c):
        return orb_recv.at[lax.rem(plane - to + planes, planes) - 1, c]

    def own_orbit(c):
        return remote(piece(orb_hbm, c), piece(guest.at[z], c), orb_send.at[0], landed(z, ahead, c), at(ahead))

    def orbit_copy(plane, to, c):
        there = piece(guest.at[plane], c)
        return remote(there, there, orb_send.at[0], landed(plane, to, c), at(to))

    def orbit_on(c):
        return orbit_copy(near_out, ahead, c)

    def orbit_back(plane, c):
        return orbit_copy(plane, buddy, c)

    def await_orbit(plane, c):
        there = piece(guest.at[plane], c)
        remote(there, there, orb_send.at[0], landed(plane, z, c), at(ahead)).wait_recv()

    def start_own(first, last):
        def step(c, _):
            own_orbit(c).start()
            return 0

        lax.fori_loop(first, last, step, 0)

    def pass_on(first, last):
        @pl.when(inner)
        def _():
            def step(c, _):
                await_orbit(near_out, c)
                orbit_on(c).start()
                return 0

            lax.fori_loop(first, last, step, 0)

    def pass_back(first, last):
        @pl.when(inner)
        def _():
            def step(c, _):
                await_orbit(far_in, c)
                orbit_back(far_in, c).start()
                return 0

            lax.fori_loop(first, last, step, 0)

    start_own(0, FIRST)

    @pl.when(outer)
    def _():
        pl.semaphore_wait(news, PLANE - 1)
        tell(ready, at(ahead))


    half_copy.wait()
    green_copy.wait()
    for copy in (*loads, orb_copy):
        copy.start()
    gauss_copy.wait()

    def bias(t, acc):
        rows = pl.ds(pl.multiple_of(t * TILE, TILE), TILE)
        left = jnp.swapaxes(green[:, rows, :], 0, 1)
        right = jnp.swapaxes(half[:, rows, :], 0, 1)
        for r in range(TILE):
            acc += lax.dot_general(
                left[r], right[r], (((1,), (1,)), ((), ())), preferred_element_type=jnp.float32
            )
        return acc

    total = lax.fori_loop(0, tiles, bias, jnp.zeros((n * owned, half.shape[0]), jnp.float32))
    for d in range(n):
        plane, s = divmod(d, PLANE)
        part[s, plane * owned:(plane + 1) * owned] = total[d * owned:(d + 1) * owned]

    @pl.when(inner)
    def _():
        pl.semaphore_wait(ready, 1)

    def part_copy(there, source):
        return remote(part.at[there], part_in.at[source], part_sem.at[0], part_sem.at[1], z * PLANE + there)

    def field_copy(there):
        mine = fields_ref.at[seat]
        return remote(mine, mine, field_sem.at[0], field_sem.at[1], z * PLANE + there)

    def gathered(ref, sem):
        every = ref.at[pl.ds(0, PLANE - 1)]
        return remote(every, every, sem.at[0], sem.at[1], at(ahead))

    def sum_copy(k, to):
        return remote(partial.at[k], partial_in.at[k], sum_sem.at[0, 0], sum_sem.at[1, k], to)

    def total_copy():
        return remote(bias_ref, bias_ref, sum_sem.at[0, 1], sum_sem.at[1, 0], at(buddy))

    for s in others:
        part_copy(s, seat).start()
    part_in[seat] = part[seat]

    @pl.when(inner)
    def _():
        start_own(FIRST, SECOND)

    pass_back(0, FIRST)
    gathered(part_in, part_sem).wait_recv()
    partial[0] = jnp.sum(part_in[...], axis=0)

    @pl.when(outer)
    def _():
        sum_copy(0, at(ahead)).start()
        start_own(FIRST, chunks)
        total_copy().wait_recv()

    @pl.when(inner)
    def _():
        sum_copy(0, at(ahead)).wait_recv()
        partial[1] = partial[0] + partial_in[0]
        sum_copy(1, at(ahead)).start()
        start_own(SECOND, THIRD)
        sum_copy(1, at(ahead)).wait_recv()
        bias_ref[...] = partial[1] + partial_in[1]
        total_copy().start()
        start_own(THIRD, chunks)

    pass_back(FIRST, SECOND)
    vbias = bias_ref[...]
    gauss = jnp.concatenate([gauss_ref[plane * PLANE + seat] for plane in range(planes)], axis=0)
    xbar = jnp.clip(-0.3 * vbias, -1.0, 1.0)
    logs = jnp.sum(gauss * xbar - 0.5 * xbar * xbar, axis=1, keepdims=True)
    log_all[...] = jnp.broadcast_to(logs, (line, LANES)).reshape(log_all.shape)
    log_ref[...] = log_all[z]
    fields_ref[seat] = (gauss - xbar).astype(jnp.bfloat16)

    for s in others:
        field_copy(s).start()
    gathered(fields_ref, field_sem).wait_recv()
    pltpu.make_async_copy(chol, chol, load_sem.at[0]).wait()
    fields = fields_ref[...].reshape(n * owned, fields_ref.shape[-1])

    order = (
        jnp.where(inner, far_in, near_in), far_out, jnp.where(inner, near_out, far_in), z,
    )

    def pot_copy(t, plane, there, source):
        return remote(
            send.at[t, pl.ds(there * line + plane * owned, owned)],
            recv.at[pl.ds(plane * owned, owned), source, t],
            pot_send.at[0], pot_recv.at[plane], z * PLANE + there,
        )

    def push(t, plane):
        for s in others:
            pot_copy(t, plane, s, seat).start()

    def await_pots(plane):
        every = recv.at[pl.ds(plane * owned, owned), pl.ds(0, PLANE - 1)]
        remote(every, every, pot_send.at[0], pot_recv.at[plane], z * PLANE + partner).wait_recv()

    def fill(t):
        def strip(c, _):
            cols = pl.ds(pl.multiple_of(c * LANES, LANES), LANES)
            block = jnp.swapaxes(chol[t, :, :, cols], 0, 1)
            pots = [
                (jnp.dot(fields, block[r], preferred_element_type=jnp.float32) * 0.3).astype(jnp.bfloat16)
                for r in range(TILE)
            ]
            send[t, :, :, cols] = jnp.swapaxes(jnp.stack(pots, axis=0), 0, 1)
            return 0

        lax.fori_loop(0, width // LANES, strip, 0)
        recv[:, seat, t] = send[t, pl.ds(seat * line, line)]

    def forward_far(first, last):
        def step(c, _):
            await_orbit(far_out, c)

            @pl.when(inner)
            def _():
                orbit_back(far_out, c).start()

            return 0

        lax.fori_loop(first, last, step, 0)

    for t in range(tiles):
        fill(t)
        push(t, order[0])
        if t < tiles - 1:
            pass_back(SECOND + t, SECOND + t + 1)
    held = SECOND + tiles - 1
    for plane in order[1:]:
        for t in range(tiles):
            push(t, plane)

    def lend():
        return remote(recv.at[pl.ds(buddy * owned, owned)], lent, lend_sem.at[0], lend_sem.at[1], at(buddy))

    pass_back(held, held + 1)
    pass_on(0, held + 1)
    pass_back(held + 1, held + 2)
    pass_on(held + 1, held + 2)
    pass_back(held + 2, chunks)
    pass_on(held + 2, chunks)
    @pl.when(outer)
    def _():
        await_pots(near_in)
        lend().start()

        def arrived(c, _):
            await_orbit(far_in, c)
            return 0

        lax.fori_loop(0, chunks, arrived, 0)

    def hand_back(plane, w):
        return remote(
            done.at[plane * owned + w], out_ref.at[w, pl.ds(z * PLANE, PLANE)],
            done_sem.at[0], done_sem.at[1], at(plane),
        )

    def rows_done(left, orbit, old):
        moved = jnp.dot(
            left.reshape(-1, width), orbit.reshape(width, nocc), preferred_element_type=jnp.float32
        )
        return (old.astype(jnp.float32) + moved.reshape(old.shape)).astype(jnp.bfloat16)

    here = pl.ds(z * PLANE, PLANE)

    def serve(plane, first, last):
        def step(w, _):
            done[plane * owned + w] = rows_done(
                recv[plane * owned + w], guest[plane, w], guest[plane, w, here]
            )
            hand_back(plane, w).start()
            return 0

        lax.fori_loop(first, last, step, 0)

    forward_far(0, 2 * CHUNKS)
    await_pots(far_out)
    serve(far_out, 0, 2)
    for w in range(2, owned):
        forward_far(CHUNKS * w, CHUNKS * (w + 1))
        serve(far_out, w, w + 1)

        if w == 2:
            @pl.when(outer)
            def _():
                await_pots(far_in)
                serve(far_in, 0, owned // 2)

    @pl.when(outer)
    def _():
        serve(far_in, owned // 2, owned)

    @pl.when(inner)
    def _():
        await_pots(far_in)
        serve(far_in, 0, owned)
        await_pots(near_out)
        serve(near_out, 0, owned)

    await_pots(z)
    orb_copy.wait()

    def advance(w, _):
        out_ref[w, here] = rows_done(recv[z * owned + w], orb_ref[w], orb_ref[w, here])
        return 0

    lax.fori_loop(0, owned, advance, 0)

    @pl.when(inner)
    def _():
        lend().wait_recv()
        there = pl.ds(near_out * PLANE, PLANE)

        def borrow(w, _):
            out_ref[w, there] = rows_done(lent[w], orb_ref[w], orb_ref[w, there])
            return 0

        lax.fori_loop(0, owned, borrow, 0)

    gathered(part_in, part_sem).wait_send()
    gathered(fields_ref, field_sem).wait_send()
    every = send.at[:, pl.ds(0, (PLANE - 1) * line)]
    remote(every, every, pot_send.at[0], pot_recv.at[z], at(ahead)).wait_send()

    def through(ref, sem):
        return remote(ref, ref, sem.at[0], sem.at[1], at(ahead))

    @pl.when(outer)
    def _():
        sum_copy(0, at(ahead)).wait_send()
        lend().wait_send()
        remote(guest.at[0], guest.at[0], orb_send.at[0], orb_recv.at[0, 0], at(ahead)).wait_send()
        through(done.at[pl.ds(0, 2 * owned)], done_sem).wait_send()

    @pl.when(inner)
    def _():
        sum_copy(1, at(ahead)).wait_send()
        total_copy().wait_send()
        remote(guest, guest, orb_send.at[0], orb_recv.at[0, 0], at(ahead)).wait_send()
        through(done.at[pl.ds(0, 3 * owned)], done_sem).wait_send()

    @pl.when(outer)
    def _():
        through(out_ref.at[:, pl.ds(0, 3 * PLANE)], done_sem).wait_recv()

    @pl.when(inner)
    def _():
        through(out_ref.at[:, pl.ds(0, 2 * PLANE)], done_sem).wait_recv()


def close_kernel(moved_ref, logs_ref, out_hbm, log_hbm, log_ref, sem):
    copies = [
        pltpu.make_async_copy(moved_ref.at[w], out_hbm.at[w], sem.at[w]) for w in range(moved_ref.shape[0])
    ]
    for copy in copies:
        copy.start()
    log_ref[...] = logs_ref[:, 0]
    copies.append(pltpu.make_async_copy(log_ref, log_hbm, sem.at[len(copies)]))
    copies[-1].start()
    for copy in copies:
        copy.wait()


def on_device(n, chol_full, chol_half, green, gauss, orbitals):
    walkers, local_rows, nocc = green.shape
    owned, width, _ = orbitals.shape
    vectors = chol_half.shape[0]
    tiles = local_rows // TILE
    vmem = pl.BlockSpec(memory_space=pltpu.VMEM)
    hbm = pl.BlockSpec(memory_space=pl.ANY)
    dma = pltpu.SemaphoreType.DMA
    split = (owned, n, tiles, TILE, nocc)
    params = pltpu.CompilerParams(collective_id=0, has_side_effects=True, vmem_limit_bytes=60 << 20)
    shared = [
        pltpu.VMEM((tiles, vectors, TILE, width), jnp.bfloat16),
        pltpu.VMEM((vectors, local_rows, nocc), jnp.bfloat16),
        pltpu.VMEM((walkers, local_rows, nocc), jnp.bfloat16),
    ]
    arrays = (chol_full, chol_half, green, gauss.reshape(n, owned, vectors), orbitals.reshape(split))
    if n == 4 * PLANE and orbitals.size * orbitals.dtype.itemsize <= OWN_LIMIT:
        line = walkers // PLANE
        planes = n // PLANE
        moved, logs = pl.pallas_call(
            functools.partial(line_kernel, n),
            out_shape=(pltpu.VMEM(split, jnp.bfloat16), pltpu.VMEM((owned, LANES), jnp.float32)),
            in_specs=[hbm] * 5,
            out_specs=(vmem, vmem),
            scratch_shapes=[
                *shared,
                pltpu.VMEM((n, owned, vectors), jnp.float32),
                pltpu.VMEM(split, jnp.bfloat16),
                pltpu.VMEM((PLANE, line, vectors), jnp.float32),
                pltpu.VMEM((PLANE, line, vectors), jnp.float32),
                pltpu.VMEM((2, line, vectors), jnp.float32),
                pltpu.VMEM((2, line, vectors), jnp.float32),
                pltpu.VMEM((line, vectors), jnp.float32),
                pltpu.VMEM((planes, owned, LANES), jnp.float32),
                pltpu.VMEM((PLANE, line, vectors), jnp.bfloat16),
                pltpu.VMEM((tiles, walkers, TILE, width), jnp.bfloat16),
                pltpu.VMEM((line, PLANE, tiles, TILE, width), jnp.bfloat16),
                pltpu.VMEM((planes,) + split, jnp.bfloat16),
                pltpu.VMEM((line, PLANE, tiles, TILE, nocc), jnp.bfloat16),
                pltpu.VMEM((owned, PLANE, tiles, TILE, width), jnp.bfloat16),
                dma((1,)), dma((4,)), dma((2,)), dma((2, 2)), dma((2,)), dma((1,)), dma((planes,)),
                dma((1,)), dma((planes - 1, CHUNKS * owned)), dma((2,)), dma((2,)),
                pltpu.SemaphoreType.REGULAR, pltpu.SemaphoreType.REGULAR,
            ],
            compiler_params=params,
        )(*arrays)
        moved, logs = pl.pallas_call(
            close_kernel,
            out_shape=(
                jax.ShapeDtypeStruct(split, jnp.bfloat16),
                jax.ShapeDtypeStruct((owned,), jnp.float32),
            ),
            in_specs=[pl.BlockSpec(memory_space=pltpu.VMEM)] * 2,
            out_specs=(hbm, hbm),
            scratch_shapes=[pltpu.VMEM((owned,), jnp.float32), dma((owned + 1,))],
            compiler_params=pltpu.CompilerParams(vmem_limit_bytes=1 << 20),
        )(moved, logs)
        return moved.reshape(orbitals.shape), logs
    else:
        moved, logs = pl.pallas_call(
            functools.partial(direct_kernel, n),
            out_shape=(
                jax.ShapeDtypeStruct(split, jnp.bfloat16),
                jax.ShapeDtypeStruct((owned, LANES), jnp.float32),
            ),
            in_specs=[hbm, hbm, hbm, vmem, vmem],
            out_specs=(vmem, vmem),
            scratch_shapes=[
                *shared,
                pltpu.VMEM((n, owned, vectors), jnp.float32),
                pltpu.VMEM((n, owned, vectors), jnp.float32),
                pltpu.VMEM((owned, vectors), jnp.float32),
                pltpu.VMEM((n, owned, vectors), jnp.float32),
                pltpu.VMEM((tiles, walkers, TILE, width), jnp.bfloat16),
                pltpu.VMEM((tiles, owned, n * TILE, width), jnp.bfloat16),
                dma((tiles,)), dma((2,)), dma((n,)), dma((n,)), dma((n,)), dma((n,)),
                dma((tiles, n)), dma((tiles, n)),
            ],
            compiler_params=params,
        )(*arrays)
    return moved.reshape(orbitals.shape), logs[:, 0]


def solution(mesh):
    placed = (
        P(None, "chol", None),
        P(None, "chol", None),
        P("grp", "chol", None),
        P("grp", None),
        P(("grp", "chol"), None, None),
    )
    return jax.shard_map(
        functools.partial(on_device, mesh.shape["chol"]),
        mesh=mesh,
        in_specs=placed,
        out_specs=(P(("grp", "chol"), None, None), P(("grp", "chol"))),
        check_vma=False,
    )
```
